32 devices in a mesh: comp: 2 (over x), gy: 4 (over y, core), gx: 4 (over z).
Axes of the slice: x: 2, y: 2, z: 4, core: 2. Of those that a mesh axis runs over, the one named last changes fastest.
Arguments:
- state: float32 [2, 8, 512, 512], P('comp', None, 'gy', 'gx'), may hold values from -6 to 6
- target: float32 [2, 8, 512, 512], P('comp', None, 'gy', 'gx'), may hold values from -2.5 to 0.5
- land_mask: int32 [2, 512, 512], P('comp', 'gy', 'gx'), may hold values 0 or 1
- diffusivity: float32 [2, 8], replicated, may hold values from 0.03 to 0.24
- coupling: float32 [2, 8, 4], replicated, may hold values from -3 to 3
- w_in: bfloat16 [16, 256], replicated, may hold values from -1.5 to 1.5
- b_in: float32 [256], replicated, may hold values from -3 to 3
- w_mid: bfloat16 [256, 256], replicated, may hold values from -0.375 to 0.375
- b_mid: float32 [256], replicated, may hold values from -3 to 3
- w_out: bfloat16 [256, 4], replicated, may hold values from -0.375 to 0.375
- b_out: float32 [4], replicated, may hold values from -3 to 3
- remap_weight: bfloat16 [2, 4, 4, 16, 4, 128, 128], P('comp', 'gy', 'gx'), may hold values from -0.5 to 0.5
- remap_source: int32 [2, 4, 4, 16, 4], P('comp', 'gy', 'gx'), may hold values from 0 to 127
- remap_target: int32 [2, 4, 4, 16, 4], P('comp', 'gy', 'gx'), may hold values from 0 to 127
- remap_count: int32 [2, 4, 4, 16], P('comp', 'gy', 'gx'), may hold values from 0 to 4, as said below
Outputs:
- new_state: float32 [2, 8, 512, 512], P('comp', None, 'gy', 'gx')
- state_adjoint: float32 [2, 8, 512, 512], P('comp', None, 'gy', 'gx')
- grad_w_in: float32 [16, 256], replicated
- grad_b_in: float32 [256], replicated
- grad_w_mid: float32 [256, 256], replicated
- grad_b_mid: float32 [256], replicated
- grad_w_out: float32 [256, 4], replicated
- grad_b_out: float32 [4], replicated
The draws below stay inside these ranges and needn't reach their ends.
Inputs may be any that keep to these rules, and one draw needn't show every extreme that they name: remap_count[c, i, j, q] leading slots of the pair are in use, the rest are padding. A pair has slots in use exactly where receiving tile q lies within 2 tile rows of i and in a tile column within 2 of j (periodic), or, for a sender in the top tile row, where q lies in the top tile row within 1 column (periodic) of column 3 - j; such pairs use 1 slot or more; for each component one receiving tile has all 4 slots in use from every such sending tile.
All inputs are finite; a program needn't handle non-finite values. No bound on the sum of `land_mask` on one device may be relied on, other than what follows from the above.
Results may differ from the reference program's by a relative error of at most 0.0037.
Values may be sent and summed in bfloat16 or wider, within the bound.
No kernel may reach another device: no remote copies, remote signals or barrier semaphores. Data moves between devices by JAX's collectives and lax.ppermute only.
A program may use at most 64 MiB of HBM per device.

```python
import math
import jax
import jax.numpy as jnp
from jax import lax

CH = 8
FIN = 16
HID = 256
FOUT = 4
TR = 128
BW = 128
SLOTS = 4
G = 16
NY = 512
NX = 512
N_GY = 4
N_GX = 4


def draw_remap_count(key, part):
    base_key = jax.random.fold_in(key, 11)
    pick_key = jax.random.fold_in(key, 12)
    base_count = jax.random.randint(base_key, (2, N_GY, N_GX, G), 1, SLOTS + 1)
    chosen = jax.random.randint(pick_key, (2, 1, 1, 1), 0, G)
    tile_row = jnp.arange(N_GY, dtype=jnp.int32).reshape(1, N_GY, 1, 1)
    tile_col = jnp.arange(N_GX, dtype=jnp.int32).reshape(1, 1, N_GX, 1)
    column = jnp.arange(G, dtype=jnp.int32).reshape(1, 1, 1, G)
    recv_row = column // N_GX
    recv_col = column % N_GX
    col_gap = (recv_col - tile_col) % N_GX
    near_col = jnp.logical_or(col_gap <= 2, col_gap >= N_GX - 2)
    near_row = jnp.abs(recv_row - tile_row) <= N_GY // 2
    fold_gap = (recv_col - (N_GX - 1 - tile_col)) % N_GX
    near_fold = jnp.logical_or(fold_gap <= 1, fold_gap >= N_GX - 1)
    top_pair = jnp.logical_and(tile_row == N_GY - 1, recv_row == N_GY - 1)
    live = jnp.logical_or(jnp.logical_and(near_row, near_col), jnp.logical_and(top_pair, near_fold))
    filled = jnp.where(column == chosen, SLOTS, base_count)
    return jnp.where(live, filled, 0).astype(jnp.int32)


def set_ends(drawn, key, low, top_value):
    index_at = [jax.random.randint(jax.random.fold_in(key, axis), (), 0, length) for axis, length in enumerate(drawn.shape)]
    longest = drawn.shape.index(max(drawn.shape))
    next_to = index_at[:longest] + [(index_at[longest] + 1) % drawn.shape[longest]] + index_at[longest + 1:]
    return drawn.at[tuple(index_at)].set(low).at[tuple(next_to)].set(top_value)


def block_scale(rng, extent, shards, least, largest):
    factor_of = 1.0
    for dim, shards_of in shards:
        heights = jax.random.uniform(jax.random.fold_in(jax.random.fold_in(rng, 6), dim), (shards_of,), jnp.float32, least / len(shards), largest / len(shards))
        factor_of = factor_of * jnp.repeat(jnp.exp(heights), extent[dim] // shards_of).reshape((-1,) + (1,) * (len(extent) - 1 - dim))
    return factor_of


def scatter_about(stream_key, extent, width, limit, split=(), kind=jnp.bfloat16):
    gain = block_scale(stream_key, extent, split, -0.22, 0.18) if split else 1.0
    entries = jax.random.normal(stream_key, extent, jnp.float32) * width * gain
    return jnp.minimum(jnp.maximum(entries, -limit), limit).astype(kind)


def setup_inputs(seed: int = 0) -> dict:
    arg_keys = jax.random.split(jax.random.key(seed), 16)
    return {
        "state": scatter_about(arg_keys[0], (2, CH, NY, NX), 1.0, 6.0, ((0, 2), (2, 4), (3, 4)), jnp.float32),
        "target": jnp.clip(-2.5 + 3.0 * jax.random.uniform(arg_keys[1], (2, CH, NY, NX), jnp.float32) ** block_scale(arg_keys[1], (2, CH, NY, NX), ((0, 2), (2, 4), (3, 4)), -0.2, 0.2), -2.5, 0.5),
        "land_mask": set_ends((jax.random.randint(arg_keys[2], (2, NY, NX), 0, 10) < 7).astype(jnp.int32), jax.random.fold_in(arg_keys[2], 1), 0, 1),
        "diffusivity": jnp.clip(jnp.exp(jax.random.uniform(arg_keys[3], (2, CH), jnp.float32, math.log(0.03), math.log(0.24))), 0.03, 0.24),
        "coupling": scatter_about(arg_keys[4], (2, CH, FOUT), 0.5, 3.0, (), jnp.float32),
        "w_in": scatter_about(arg_keys[5], (FIN, HID), FIN ** -0.5, 1.5),
        "b_in": scatter_about(arg_keys[6], (HID,), 0.5, 3.0, (), jnp.float32),
        "w_mid": scatter_about(arg_keys[7], (HID, HID), HID ** -0.5, 0.375),
        "b_mid": scatter_about(arg_keys[8], (HID,), 0.5, 3.0, (), jnp.float32),
        "w_out": scatter_about(arg_keys[9], (HID, FOUT), HID ** -0.5, 0.375),
        "b_out": scatter_about(arg_keys[10], (FOUT,), 0.5, 3.0, (), jnp.float32),
        "remap_weight": scatter_about(arg_keys[11], (2, N_GY, N_GX, G, SLOTS, BW, BW), BW ** -0.5, 0.5, ((0, 2), (1, 4), (2, 4))),
        "remap_source": set_ends(jax.random.randint(arg_keys[12], (2, N_GY, N_GX, G, SLOTS), 0, TR), jax.random.fold_in(arg_keys[12], 1), 0, TR - 1).astype(jnp.int32),
        "remap_target": set_ends(jax.random.randint(arg_keys[13], (2, N_GY, N_GX, G, SLOTS), 0, TR), jax.random.fold_in(arg_keys[13], 1), 0, TR - 1).astype(jnp.int32),
        "remap_count": draw_remap_count(jax.random.fold_in(arg_keys[15], 71), 0),
    }


PRECISE = lax.Precision.HIGHEST


def silu_slope(preact):
    sigmoid_value = jax.nn.sigmoid(preact)
    return sigmoid_value * (1.0 + preact * (1.0 - sigmoid_value))


def laplace(surface, folded):
    east_side = jnp.roll(surface, -1, axis=2)
    west_side = jnp.roll(surface, 1, axis=2)
    zero_row = jnp.zeros_like(surface[:, :1, :])
    south_side = jnp.concatenate([zero_row, surface[:, :-1, :]], axis=1)
    top_row = surface[:, -1:, ::-1] if folded else zero_row
    north_side = jnp.concatenate([surface[:, 1:, :], top_row], axis=1)
    return east_side + west_side + south_side + north_side - 4.0 * surface


def to_tiles(surface):
    shaped = surface.reshape(CH, N_GY, TR, N_GX, BW)
    return shaped.transpose(1, 3, 2, 0, 4).reshape(G, TR, CH, BW)


def from_tiles(tile_stack):
    shaped = tile_stack.reshape(N_GY, N_GX, TR, CH, BW)
    return shaped.transpose(3, 0, 2, 1, 4).reshape(CH, NY, NX)


def live_slots(count_row):
    slot_index = jnp.arange(SLOTS, dtype=jnp.int32)
    return (slot_index[None, :] < count_row[:, None]).astype(jnp.float32)


def remap_forward(tile_stack, weights, sources, targets, counts):
    dest_index = jnp.broadcast_to(jnp.arange(G, dtype=jnp.int32)[:, None], (G, SLOTS))

    def advance(summed, scan_item):
        sender_tile, weight, source, target_rows, count_row = scan_item
        picked = sender_tile[source].astype(jnp.float32)
        products = jnp.einsum("gsci,gsij->gscj", picked, weight.astype(jnp.float32))
        products = products * live_slots(count_row)[:, :, None, None]
        return summed.at[dest_index, target_rows].add(products), None

    initial = jnp.zeros((G, TR, CH, BW), jnp.float32)
    summed, _ = lax.scan(advance, initial, (tile_stack, weights, sources, targets, counts))
    return summed


def remap_adjoint(cot_tiles, weights, sources, targets, counts):
    dest_index = jnp.broadcast_to(jnp.arange(G, dtype=jnp.int32)[:, None], (G, SLOTS))

    def advance(unused, scan_item):
        weight, source, target_rows, count_row = scan_item
        live_mask = live_slots(count_row)[:, :, None, None]
        picked = cot_tiles[dest_index, target_rows] * live_mask
        picked = lax.optimization_barrier(picked.astype(jnp.bfloat16)).astype(jnp.float32)
        spread = jnp.einsum("gscj,gsij->gsci", picked, weight.astype(jnp.float32))
        landed = jnp.zeros((TR, CH, BW), jnp.float32).at[source].add(spread)
        return unused, landed

    _, stacked = lax.scan(advance, jnp.zeros((), jnp.float32), (weights, sources, targets, counts))
    return stacked


def grid_pass(features, surface, laplacian, goal, wet_mask, diff_mask, diffuse_rate, couple,
              w_in, b_in, w_mid, b_mid, w_out, b_out):
    cell_total = NY * NX
    block_size = math.gcd(cell_total, 8192)
    block_count = cell_total // block_size

    def to_blocks(array):
        return array.reshape(array.shape[0], block_count, block_size).transpose(1, 0, 2)

    def advance(gradients, scan_item):
        feature_block, current, lap_block, goal_block, wet_block, diff_block = scan_item
        pre_first = jnp.dot(w_in.T, feature_block, preferred_element_type=jnp.float32) + b_in[:, None]
        hidden_first = jax.nn.silu(pre_first).astype(jnp.bfloat16)
        pre_second = jnp.dot(w_mid.T, hidden_first, preferred_element_type=jnp.float32) + b_mid[:, None]
        hidden_second = jax.nn.silu(pre_second).astype(jnp.bfloat16)
        fluxes = (jnp.dot(w_out.T, hidden_second, preferred_element_type=jnp.float32) + b_out[:, None]) * wet_block
        updated = current + diffuse_rate[:, None] * diff_block * lap_block + jnp.dot(couple, fluxes, precision=PRECISE)
        misfit = updated - goal_block
        flux_cot = (wet_block * jnp.dot(couple.T, misfit, precision=PRECISE)).astype(jnp.bfloat16)
        second_cot = (jnp.dot(w_out, flux_cot, preferred_element_type=jnp.float32) * silu_slope(pre_second)).astype(jnp.bfloat16)
        first_cot = (jnp.dot(w_mid, second_cot, preferred_element_type=jnp.float32) * silu_slope(pre_first)).astype(jnp.bfloat16)
        feature_cot = jnp.dot(w_in, first_cot, preferred_element_type=jnp.float32)
        additions = (
            jnp.dot(feature_block, first_cot.T, preferred_element_type=jnp.float32),
            jnp.sum(first_cot.astype(jnp.float32), axis=1),
            jnp.dot(hidden_first, second_cot.T, preferred_element_type=jnp.float32),
            jnp.sum(second_cot.astype(jnp.float32), axis=1),
            jnp.dot(hidden_second, flux_cot.T, preferred_element_type=jnp.float32),
            jnp.sum(flux_cot.astype(jnp.float32), axis=1),
        )
        return jax.tree.map(jnp.add, gradients, additions), (updated, misfit, feature_cot)

    initial = (jnp.zeros((FIN, HID), jnp.float32), jnp.zeros((HID,), jnp.float32),
               jnp.zeros((HID, HID), jnp.float32), jnp.zeros((HID,), jnp.float32),
               jnp.zeros((HID, FOUT), jnp.float32), jnp.zeros((FOUT,), jnp.float32))
    items = (to_blocks(features), to_blocks(surface), to_blocks(laplacian), to_blocks(goal),
             to_blocks(wet_mask), to_blocks(diff_mask))
    gradients, outputs = lax.scan(advance, initial, items)

    def from_blocks(array):
        return array.transpose(1, 0, 2).reshape(array.shape[1], cell_total)

    return gradients, from_blocks(outputs[0]), from_blocks(outputs[1]), from_blocks(outputs[2])


def reference(state, target, land_mask, diffusivity, coupling, w_in, b_in, w_mid, b_mid, w_out, b_out,
              remap_weight, remap_source, remap_target, remap_count):
    rounded = lax.optimization_barrier(state.astype(jnp.bfloat16))
    weights = remap_weight.reshape(2, G, G, SLOTS, BW, BW)
    sources = remap_source.reshape(2, G, G, SLOTS)
    arrivals = remap_target.reshape(2, G, G, SLOTS)
    counts = remap_count.reshape(2, G, G)
    cell_total = NY * NX
    gradients = (jnp.zeros((FIN, HID), jnp.float32), jnp.zeros((HID,), jnp.float32),
                 jnp.zeros((HID, HID), jnp.float32), jnp.zeros((HID,), jnp.float32),
                 jnp.zeros((HID, FOUT), jnp.float32), jnp.zeros((FOUT,), jnp.float32))
    new_fields = []
    adjoints = []
    other_cots = []
    for component in range(2):
        sender = 1 - component
        targets = arrivals[component].transpose(1, 0, 2)
        summed = remap_forward(to_tiles(rounded[sender]), weights[sender], sources[sender], targets, counts[sender])
        other_fields = from_tiles(summed).astype(jnp.bfloat16).reshape(CH, cell_total)
        own_fields = rounded[component].reshape(CH, cell_total)
        if component == 0:
            features = jnp.concatenate([own_fields, other_fields], axis=0)
        else:
            features = jnp.concatenate([other_fields, own_fields], axis=0)
        wet_mask = land_mask[component].astype(jnp.float32).reshape(1, cell_total)
        diff_mask = wet_mask if component == 1 else jnp.ones_like(wet_mask)
        laplacian = laplace(state[component], component == 1).reshape(CH, cell_total)
        part_grads, updated, misfit, feature_cot = grid_pass(
            features, state[component].reshape(CH, cell_total), laplacian,
            target[component].reshape(CH, cell_total), wet_mask, diff_mask,
            diffusivity[component], coupling[component], w_in, b_in, w_mid, b_mid, w_out, b_out)
        gradients = jax.tree.map(jnp.add, gradients, part_grads)
        back_lap = laplace((diff_mask * misfit).reshape(CH, NY, NX), component == 1)
        if component == 0:
            own_cot = feature_cot[:CH]
            other_cot = feature_cot[CH:]
        else:
            own_cot = feature_cot[CH:]
            other_cot = feature_cot[:CH]
        adjoint_field = (misfit.reshape(CH, NY, NX) + diffusivity[component][:, None, None] * back_lap
                         + own_cot.reshape(CH, NY, NX))
        new_fields.append(updated.reshape(CH, NY, NX))
        adjoints.append(adjoint_field)
        other_cots.append(other_cot.reshape(CH, NY, NX))
    for component in range(2):
        receiver = 1 - component
        targets = arrivals[receiver].transpose(1, 0, 2)
        stacked = remap_adjoint(to_tiles(other_cots[receiver]), weights[component], sources[component],
                                targets, counts[component])
        adjoints[component] = adjoints[component] + from_tiles(stacked)
    inverse = 1.0 / (NY * NX)
    return (jnp.stack(new_fields), jnp.stack(adjoints), gradients[0] * inverse, gradients[1] * inverse,
            gradients[2] * inverse, gradients[3] * inverse, gradients[4] * inverse, gradients[5] * inverse)
```

```python
import math

import jax
import jax.numpy as jnp
from jax import lax
from jax.sharding import PartitionSpec as P

PRECISE = lax.Precision.HIGHEST


def extended(cells, sides, width, closed):
    for axis, dim in sides:
        count = lax.axis_size(axis)
        ends = count if closed else count - 1
        head = lax.slice_in_dim(cells, 0, width, axis=dim)
        tail = lax.slice_in_dim(cells, cells.shape[dim] - width, cells.shape[dim], axis=dim)
        cells = jnp.concatenate(
            [
                lax.ppermute(tail, axis, [(i, (i + 1) % count) for i in range(ends)]),
                cells,
                lax.ppermute(head, axis, [((i + 1) % count, i) for i in range(ends)]),
            ],
            axis=dim,
        )
    return cells


def partner(block, axis, stride):
    count = lax.axis_size(axis)
    route = []
    for low in range(count):
        high = low | 1 << stride
        if high != low and high < count:
            route += [(low, high), (high, low)]
    return lax.ppermute(block, axis, route)


def silu_slope(preact):
    sigmoid_value = jax.nn.sigmoid(preact)
    return sigmoid_value * (1.0 + preact * (1.0 - sigmoid_value))


def laplace(surface, on_fold):
    wide_field = extended(surface, (("gx", 2),), 1, True)
    tall_field = extended(surface, (("gy", 1),), 1, False)
    top_row = surface[:, -1, :]
    mirrored = top_row[:, ::-1]
    for bit_index in range(lax.axis_size("gx").bit_length() - 1):
        mirrored = partner(mirrored, "gx", bit_index)
    north_rows = tall_field[:, 2:, :]
    north_rows = north_rows.at[:, -1, :].add(jnp.where(on_fold, mirrored, 0.0))
    return (
        wide_field[:, :, 2:]
        + wide_field[:, :, :-2]
        + tall_field[:, :-2, :]
        + north_rows
        - 4.0 * surface
    )


def forward_route(outgoing):
    relayed = lax.all_to_all(outgoing, ("gy", "gx"), split_axis=0, concat_axis=0, tiled=True)
    arrived = partner(relayed, "comp", 0)
    return arrived


def return_route(outgoing):
    relayed = lax.all_to_all(outgoing, ("gy", "gx"), split_axis=0, concat_axis=0, tiled=True)
    arrived = partner(relayed, "comp", 0)
    return arrived


def shards(
    state,
    target,
    land_mask,
    diffusivity,
    coupling,
    w_in,
    b_in,
    w_mid,
    b_mid,
    w_out,
    b_out,
    remap_weight,
    remap_source,
    remap_target,
    remap_count,
):
    comp_index = lax.axis_index("comp")
    is_ocean = comp_index == 1
    on_fold = jnp.logical_and(is_ocean, lax.axis_index("gy") == lax.axis_size("gy") - 1)
    surface = state[0]
    channels, tile_rows, tile_width = surface.shape
    cell_count = tile_rows * tile_width
    peer_count = remap_source.shape[3]
    slot_count = remap_source.shape[4]
    pair_count = peer_count * slot_count
    wet_mask = land_mask[0].astype(jnp.float32).reshape(1, cell_count)
    diff_mask = jnp.where(is_ocean, wet_mask, 1.0)
    diffuse_rate = diffusivity[comp_index]
    couple = coupling[comp_index]
    rounded = surface.astype(jnp.bfloat16)
    source = remap_source[0, 0, 0].reshape(pair_count)
    kernels = remap_weight[0, 0, 0].reshape(pair_count, tile_width, tile_width)
    slot_index = lax.broadcasted_iota(jnp.int32, (peer_count, slot_count), 1)
    live_mask = (
        (slot_index < remap_count[0, 0, 0][:, None]).astype(jnp.float32).reshape(pair_count, 1, 1)
    )
    picked = rounded[:, source, :]
    outgoing = (
        jnp.einsum("cki,kij->kcj", picked, kernels, preferred_element_type=jnp.float32) * live_mask
    )
    arrived = forward_route(outgoing.reshape(peer_count, slot_count, channels, tile_width))
    laplacian = laplace(surface, on_fold).reshape(channels, cell_count)
    row_index = lax.broadcasted_iota(jnp.int32, (tile_rows, pair_count), 0)
    landing = (row_index == remap_target[0, 0, 0].reshape(1, pair_count)).astype(jnp.float32)
    remapped = jnp.einsum(
        "tk,kcj->ctj", landing, arrived.reshape(pair_count, channels, tile_width), precision=PRECISE
    )
    own_fields = rounded.reshape(channels, cell_count)
    other_fields = remapped.astype(jnp.bfloat16).reshape(channels, cell_count)
    features = jnp.concatenate(
        [
            jnp.where(is_ocean, other_fields, own_fields),
            jnp.where(is_ocean, own_fields, other_fields),
        ],
        axis=0,
    )
    current = surface.reshape(channels, cell_count)
    goal = target[0].reshape(channels, cell_count)
    block_size = math.gcd(cell_count, 2048)

    def advance(block_index, loop_state):
        new_fields, misfits, feature_cots, gradients = loop_state
        offset = block_index * block_size

        def take_block(array):
            return lax.dynamic_slice_in_dim(array, offset, block_size, 1)

        feature_block = take_block(features)
        wet_block = take_block(wet_mask)
        diff_block = take_block(diff_mask)
        pre_first = (
            jnp.einsum("fh,fn->hn", w_in, feature_block, preferred_element_type=jnp.float32)
            + b_in[:, None]
        )
        hidden_first = jax.nn.silu(pre_first).astype(jnp.bfloat16)
        pre_second = (
            jnp.einsum("hk,hn->kn", w_mid, hidden_first, preferred_element_type=jnp.float32)
            + b_mid[:, None]
        )
        hidden_second = jax.nn.silu(pre_second).astype(jnp.bfloat16)
        fluxes = (
            jnp.einsum("ho,hn->on", w_out, hidden_second, preferred_element_type=jnp.float32)
            + b_out[:, None]
        ) * wet_block
        updated = (
            take_block(current)
            + diffuse_rate[:, None] * diff_block * take_block(laplacian)
            + jnp.dot(couple, fluxes, precision=PRECISE)
        )
        misfit = updated - take_block(goal)
        flux_cot = (wet_block * jnp.dot(couple.T, misfit, precision=PRECISE)).astype(jnp.bfloat16)
        second_cot = (
            jnp.einsum("ho,on->hn", w_out, flux_cot, preferred_element_type=jnp.float32)
            * silu_slope(pre_second)
        ).astype(jnp.bfloat16)
        first_cot = (
            jnp.einsum("hk,kn->hn", w_mid, second_cot, preferred_element_type=jnp.float32)
            * silu_slope(pre_first)
        ).astype(jnp.bfloat16)
        feature_cot = jnp.einsum("fh,hn->fn", w_in, first_cot, preferred_element_type=jnp.float32)
        additions = (
            jnp.einsum("fn,hn->fh", feature_block, first_cot, preferred_element_type=jnp.float32),
            jnp.sum(first_cot.astype(jnp.float32), axis=1),
            jnp.einsum("hn,kn->hk", hidden_first, second_cot, preferred_element_type=jnp.float32),
            jnp.sum(second_cot.astype(jnp.float32), axis=1),
            jnp.einsum("hn,on->ho", hidden_second, flux_cot, preferred_element_type=jnp.float32),
            jnp.sum(flux_cot.astype(jnp.float32), axis=1),
        )
        new_fields = lax.dynamic_update_slice_in_dim(new_fields, updated, offset, 1)
        misfits = lax.dynamic_update_slice_in_dim(misfits, misfit, offset, 1)
        feature_cots = lax.dynamic_update_slice_in_dim(feature_cots, feature_cot, offset, 1)
        return (new_fields, misfits, feature_cots, jax.tree.map(jnp.add, gradients, additions))

    initial = (
        jnp.zeros((channels, cell_count), jnp.float32),
        jnp.zeros((channels, cell_count), jnp.float32),
        jnp.zeros((2 * channels, cell_count), jnp.float32),
        (
            jnp.zeros(w_in.shape, jnp.float32),
            jnp.zeros(b_in.shape, jnp.float32),
            jnp.zeros(w_mid.shape, jnp.float32),
            jnp.zeros(b_mid.shape, jnp.float32),
            jnp.zeros(w_out.shape, jnp.float32),
            jnp.zeros(b_out.shape, jnp.float32),
        ),
    )
    new_fields, misfits, feature_cots, gradients = lax.fori_loop(
        0, cell_count // block_size, advance, initial
    )
    back_lap = laplace((diff_mask * misfits).reshape(channels, tile_rows, tile_width), on_fold)
    own_cot = jnp.where(is_ocean, feature_cots[channels:], feature_cots[:channels]).reshape(
        channels, tile_rows, tile_width
    )
    other_cot = jnp.where(is_ocean, feature_cots[:channels], feature_cots[channels:]).reshape(
        channels, tile_rows, tile_width
    )
    going_back = jnp.einsum("tk,ctj->kcj", landing, other_cot, precision=PRECISE).astype(
        jnp.bfloat16
    )
    returned = return_route(going_back.reshape(peer_count, slot_count, channels, tile_width))
    spread = (
        jnp.einsum(
            "kcj,kij->kci",
            returned.reshape(pair_count, channels, tile_width),
            kernels,
            preferred_element_type=jnp.float32,
        )
        * live_mask
    )
    anchor = (row_index == source.reshape(1, pair_count)).astype(jnp.float32)
    remap_back = jnp.einsum("tk,kci->cti", anchor, spread, precision=PRECISE)
    adjoint_field = (
        misfits.reshape(channels, tile_rows, tile_width)
        + diffuse_rate[:, None, None] * back_lap
        + own_cot
        + remap_back
    )
    grad_first, bias_first, grad_second, bias_second, grad_third, bias_third = gradients
    everywhere = ("comp", "gy", "gx")
    device_count = math.prod(lax.axis_size(axis) for axis in everywhere)
    packed = jnp.concatenate(
        [
            grad_first,
            bias_first[None],
            grad_second,
            bias_second[None],
            grad_third.T,
            jnp.pad(bias_third, (0, w_in.shape[1] - bias_third.shape[0]))[None],
        ],
        axis=0,
    )
    total_rows = packed.shape[0]
    share = -(-total_rows // device_count)
    packed = jnp.pad(packed, ((0, share * device_count - total_rows), (0, 0)))
    pieces = lax.all_to_all(
        packed.reshape(device_count, share, -1), everywhere, 0, 0, tiled=True
    )
    summed = jnp.sum(pieces, axis=0, keepdims=True)
    packed = lax.all_to_all(
        jnp.broadcast_to(summed, pieces.shape), everywhere, 0, 0, tiled=True
    ).reshape(share * device_count, -1)
    inputs, hidden = w_in.shape
    outputs = w_out.shape[1]
    grad_first = packed[:inputs]
    bias_first = packed[inputs]
    grad_second = packed[inputs + 1 : inputs + 1 + hidden]
    bias_second = packed[inputs + 1 + hidden]
    grad_third = packed[inputs + 2 + hidden : inputs + 2 + hidden + outputs].T
    bias_third = packed[inputs + 2 + hidden + outputs, :outputs]
    scale = 1.0 / (cell_count * lax.axis_size("gy") * lax.axis_size("gx"))
    return (
        new_fields.reshape(1, channels, tile_rows, tile_width),
        adjoint_field.reshape(1, channels, tile_rows, tile_width),
        grad_first * scale,
        bias_first * scale,
        grad_second * scale,
        bias_second * scale,
        grad_third * scale,
        bias_third * scale,
    )


def solution(mesh):
    placed = (
        P("comp", None, "gy", "gx"),
        P("comp", None, "gy", "gx"),
        P("comp", "gy", "gx"),
        P(),
        P(),
        P(),
        P(),
        P(),
        P(),
        P(),
        P(),
        P("comp", "gy", "gx", None, None, None, None),
        P("comp", "gy", "gx", None, None),
        P("comp", "gy", "gx", None, None),
        P("comp", "gy", "gx", None),
    )
    return jax.shard_map(
        shards,
        mesh=mesh,
        in_specs=placed,
        out_specs=(
            P("comp", None, "gy", "gx"),
            P("comp", None, "gy", "gx"),
            P(),
            P(),
            P(),
            P(),
            P(),
            P(),
        ),
        check_vma=False,
    )
```

```python
import functools
import math

import jax
import jax.numpy as jnp
from jax import lax
from jax.experimental import pallas as pl
from jax.experimental.pallas import tpu as pltpu
from jax.sharding import PartitionSpec as P

EVERYWHERE = ("comp", "gy", "gx")
BLOCK_ROWS = 8
CHUNK = 256
SUBLANES = 8

OWN, OTHER, WEST, EAST, SOUTH, NORTH, COMP, HAS_SOUTH, HAS_NORTH, ON_FOLD = range(10)

f32 = jnp.float32
bf16 = jnp.bfloat16


def dot(a, b):
    return jnp.dot(a, b, preferred_element_type=f32)


def dot_nt(a, b):
    return lax.dot_general(a, b, (((1,), (1,)), ((), ())), preferred_element_type=f32)


def mirror(tile):
    width = tile.shape[1]
    row = lax.broadcasted_iota(jnp.int32, (width, width), 0)
    col = lax.broadcasted_iota(jnp.int32, (width, width), 1)
    flip = (row + col == width - 1).astype(f32).astype(bf16)
    return dot(tile.astype(bf16), flip)


def edge_columns(read_row, rows, shape):
    lane = lax.broadcasted_iota(jnp.int32, shape, 1)
    width = shape[1]

    def step(r, sides):
        first, last = sides
        tile = read_row(r)
        here = lane == r
        first = jnp.where(here, pltpu.roll(tile, r, 1), first)
        last = jnp.where(here, pltpu.roll(tile, lax.rem(r + 1, width), 1), last)
        return first, last

    zero = jnp.zeros(shape, f32)
    return lax.fori_loop(0, rows, step, (zero, zero), unroll=8)


def put_edges(meta, read_row, rows, shape, stage):
    first, last = edge_columns(read_row, rows, shape)
    stage[meta[EAST], 0:SUBLANES, :] = last
    stage[meta[WEST], SUBLANES : 2 * SUBLANES, :] = first
    top = read_row(rows - 1)
    top = jnp.where(meta[ON_FOLD] == 1, mirror(top), top)
    stage[meta[NORTH], 2 * SUBLANES : 3 * SUBLANES, :] = top
    stage[meta[SOUTH], 3 * SUBLANES : 4 * SUBLANES, :] = read_row(0)


def get_edges(meta, recv):
    west = recv[meta[WEST], 0:32, :].astype(f32)[0:SUBLANES]
    east = recv[meta[EAST], 0:32, :].astype(f32)[SUBLANES : 2 * SUBLANES]
    south = recv[meta[SOUTH], 0:32, :].astype(f32)[2 * SUBLANES : 3 * SUBLANES]
    above = recv[meta[NORTH], 0:32, :].astype(f32)
    north = jnp.where(
        meta[ON_FOLD] == 1,
        above[2 * SUBLANES : 3 * SUBLANES],
        above[3 * SUBLANES : 4 * SUBLANES],
    )
    south = jnp.where(meta[HAS_SOUTH] == 1, south, 0.0)
    north = jnp.where(meta[HAS_NORTH] == 1, north, 0.0)
    return west, east, south, north


def laplace_row(here, below, above, west, east, r, lane):
    width = here.shape[1]
    left = jnp.where(
        lane == 0, pltpu.roll(west, lax.rem(width - r, width), 1), pltpu.roll(here, 1, 1)
    )
    right = jnp.where(
        lane == width - 1, pltpu.roll(east, width - 1 - r, 1), pltpu.roll(here, width - 1, 1)
    )
    return left + right + below + above - 4.0 * here


def send_kernel(rows, peers, slots, meta, source, count, state, kernels, out, stage):
    shape = (SUBLANES, state.shape[1])

    def read_row(r):
        return state[pl.ds(r, SUBLANES, stride=rows), :]

    stage[pl.ds(meta[OWN], peers)] = jnp.zeros((peers,) + stage.shape[1:], f32)

    def peer_step(q, unused):
        for s in range(slots):
            k = q * slots + s
            picked = read_row(source[k]).astype(bf16)
            live = (s < count[q]).astype(f32)
            stage[meta[OTHER] + q, s * SUBLANES : (s + 1) * SUBLANES, :] = (
                dot(picked, kernels[k]) * live
            )
        return unused

    lax.fori_loop(0, peers, peer_step, 0, unroll=4)
    put_edges(meta, read_row, rows, shape, stage)
    out[...] = stage[...].astype(bf16)


def main_kernel(
    rows,
    peers,
    slots,
    share,
    small_share,
    meta,
    landing,
    b_out,
    state,
    goal,
    mask,
    recv,
    rate_ref,
    couple_ref,
    w_first,
    w_second,
    b_second,
    w_third,
    w_third_back,
    w_second_back,
    w_first_back,
    new_out,
    base_out,
    diffuse_out,
    send_out,
    stage,
    other,
    feat,
    hid_first,
    hid_second,
    slope_first,
    slope_second,
    cot_second,
    cot_first,
    flux,
    flux_cot,
    feat_cot,
    g_first,
    g_second,
    g_third,
    g_bias,
    small,
):
    width = state.shape[1]
    hidden = w_second.shape[0]
    shape = (SUBLANES, width)
    cells = BLOCK_ROWS * width
    lane = lax.broadcasted_iota(jnp.int32, shape, 1)
    sub = lax.broadcasted_iota(jnp.int32, shape, 0)
    fluxes = couple_ref.shape[2]

    def read_row(r):
        return state[pl.ds(r, SUBLANES, stride=rows), :]

    other[...] = jnp.zeros(other.shape, f32)

    def land(p, unused):
        block = recv[meta[OTHER] + p, 0:32, :].astype(f32)
        for s in range(slots):
            row = landing[p * slots + s]
            other[row] = other[row] + block[s * SUBLANES : (s + 1) * SUBLANES]
        return unused

    lax.fori_loop(0, peers, land, 0, unroll=2)
    west, east, south, north = get_edges(meta, recv)
    comp = meta[COMP]
    eye = (
        lax.broadcasted_iota(jnp.int32, (SUBLANES, SUBLANES), 0)
        == lax.broadcasted_iota(jnp.int32, (SUBLANES, SUBLANES), 1)
    ).astype(f32)
    rate = jnp.sum(
        jnp.broadcast_to(rate_ref[pl.ds(comp, 1), :], (SUBLANES, SUBLANES)) * eye,
        axis=1,
        keepdims=True,
    )
    rate = jnp.broadcast_to(rate, shape)
    pairs = couple_ref[comp]
    couple = [jnp.broadcast_to(pairs[:, f : f + 1], shape) for f in range(fluxes)]
    ones = (lax.broadcasted_iota(jnp.int32, (16, cells), 0) < 3).astype(f32).astype(bf16)
    feat[16:32, :] = ones
    hid_first[hidden : hidden + 16, :] = ones
    flux_cot[...] = jnp.zeros(flux_cot.shape, bf16)
    g_first[...] = jnp.zeros(g_first.shape, f32)
    g_second[...] = jnp.zeros(g_second.shape, f32)
    g_third[...] = jnp.zeros(g_third.shape, f32)
    g_bias[...] = jnp.zeros(g_bias.shape, f32)
    bias = jnp.broadcast_to(b_second[...], (hidden, CHUNK))
    b_third = jnp.zeros(shape, f32)
    for f in range(fluxes):
        b_third = jnp.where(sub == f, b_out[f], b_third)

    def block_step(block, unused):
        start = block * BLOCK_ROWS
        for i in range(BLOCK_ROWS):
            at = pl.ds(i * width, width)
            r = start + i
            feat[0:16, at] = jnp.concatenate([read_row(r), other[r]], axis=0).astype(bf16)
        for j in range(cells // CHUNK):
            at = pl.ds(j * CHUNK, CHUNK)
            half = dot(w_first[...], feat[:, at])
            turn = jnp.tanh(half)
            up = 1.0 + turn
            hid = half * up
            hid_first[0:hidden, at] = hid.astype(bf16)
            slope_first[:, at] = (up + hid) - hid * turn
        for j in range(cells // CHUNK):
            at = pl.ds(j * CHUNK, CHUNK)
            half = dot(w_second[...], hid_first[0:hidden, at]) + bias
            turn = jnp.tanh(half)
            up = 1.0 + turn
            hid = half * up
            hid_second[:, at] = hid.astype(bf16)
            slope_second[:, at] = (up + hid) - hid * turn
        for j in range(cells // CHUNK):
            at = pl.ds(j * CHUNK, CHUNK)
            flux[:, at] = dot(w_third[...], hid_second[:, at])[0:SUBLANES]
        for i in range(BLOCK_ROWS):
            at = pl.ds(i * width, width)
            r = start + i
            here = read_row(r)
            below = jnp.where(r > 0, read_row(jnp.maximum(r - 1, 0)), south)
            above = jnp.where(r < rows - 1, read_row(jnp.minimum(r + 1, rows - 1)), north)
            lap = laplace_row(here, below, above, west, east, r, lane)
            wet = jnp.broadcast_to(mask[pl.ds(r, 1), :].astype(f32), shape)
            spread_mask = jnp.where(comp == 1, wet, 1.0)
            wet_flux = (flux[:, at] + b_third) * wet
            updated = here + rate * spread_mask * lap
            for f in range(fluxes):
                updated = updated + couple[f] * jnp.broadcast_to(wet_flux[f : f + 1], shape)
            new_out[pl.ds(r, SUBLANES, stride=rows), :] = updated
            misfit = updated - goal[pl.ds(r, SUBLANES, stride=rows), :]
            diffuse_out[r] = spread_mask * misfit
            base_out[r] = misfit
            pulled = jnp.zeros(shape, f32)
            for f in range(fluxes):
                total = jnp.sum(couple[f] * misfit, axis=0, keepdims=True)
                pulled = jnp.where(sub == f, jnp.broadcast_to(total, shape), pulled)
            pulled = (pulled * wet).astype(bf16)
            flux_cot[0:SUBLANES, at] = pulled
            g_bias[...] = g_bias[...] + pulled.astype(f32)
        for j in range(cells // CHUNK):
            at = pl.ds(j * CHUNK, CHUNK)
            cot_second[:, at] = (
                dot(w_third_back[...], flux_cot[:, at]) * slope_second[:, at]
            ).astype(bf16)
        for j in range(cells // CHUNK):
            at = pl.ds(j * CHUNK, CHUNK)
            cot_first[:, at] = (
                dot(w_second_back[...], cot_second[:, at]) * slope_first[:, at]
            ).astype(bf16)
        for j in range(cells // CHUNK):
            at = pl.ds(j * CHUNK, CHUNK)
            feat_cot[:, at] = dot(w_first_back[...], cot_first[:, at])
        for i in range(BLOCK_ROWS):
            at = pl.ds(i * width, width)
            r = start + i
            base_out[r] = base_out[r] + feat_cot[0:SUBLANES, at]
            other[r] = feat_cot[SUBLANES : 2 * SUBLANES, at]
        g_second[...] += dot_nt(hid_first[...], cot_second[...])
        g_first[...] += dot_nt(feat[...], cot_first[...])
        g_third[...] += dot_nt(flux_cot[...], hid_second[...])
        return unused

    lax.fori_loop(0, rows // BLOCK_ROWS, block_step, 0)

    stage[pl.ds(meta[OWN], peers), 0:32, :] = jnp.zeros((peers, 32, width), f32)

    def leave(p, unused):
        for s in range(slots):
            row = landing[p * slots + s]
            stage[meta[OTHER] + p, s * SUBLANES : (s + 1) * SUBLANES, :] = other[row]
        return unused

    lax.fori_loop(0, peers, leave, 0, unroll=2)
    put_edges(meta, lambda r: diffuse_out[r], rows, shape, stage)

    devices = stage.shape[0]
    halves = hidden // width
    inputs = 2 * SUBLANES
    small[...] = jnp.zeros(small.shape, f32)
    low, high = g_first[0:SUBLANES, :], g_first[SUBLANES:inputs, :]
    low, high = jnp.where(comp == 1, high, low), jnp.where(comp == 1, low, high)
    bias_sum = jnp.sum(g_bias[...], axis=1, keepdims=True)
    bias_row = jnp.sum(jnp.where(sub == lane, jnp.broadcast_to(bias_sum, shape), 0.0), axis=0,
                       keepdims=True)
    for h in range(halves):
        cols = slice(h * width, (h + 1) * width)
        top = h * 24
        small[top : top + 8, :] = low[:, cols]
        small[top + 8 : top + 16, :] = high[:, cols]
        small[top + 16 : top + 17, :] = g_first[inputs : inputs + 1, cols]
        small[top + 17 : top + 18, :] = g_second[hidden : hidden + 1, cols]
        if h == 0:
            small[top + 18 : top + 19, :] = bias_row
        small[top + 19 : top + 19 + fluxes, :] = g_third[0:fluxes, cols]
    for d in range(devices):
        done = 0
        while done < share:
            at = d * share + done
            h, row = divmod(at, hidden)
            step = min(share - done, hidden - row)
            if h < halves:
                stage[d, 32 + done : 32 + done + step, :] = g_second[
                    row : row + step, h * width : (h + 1) * width
                ]
            done += step
        stage[d, 32 + share : 32 + share + small_share, :] = small[
            d * small_share : (d + 1) * small_share, :
        ]
    send_out[...] = stage[...].astype(bf16)


def sum_kernel(scale, recv, out):
    devices = recv.shape[0]
    total = recv[0, 32:, :].astype(f32)
    for d in range(1, devices):
        total = total + recv[d, 32:, :].astype(f32)
    total = (total * scale).astype(bf16)
    for d in range(devices):
        out[d] = total


def back_kernel(
    rows, peers, slots, meta, source, count, recv, kernels, base, diffuse, rate_ref, out, total
):
    width = diffuse.shape[2]
    shape = (SUBLANES, width)
    lane = lax.broadcasted_iota(jnp.int32, shape, 1)
    west, east, south, north = get_edges(meta, recv)
    comp = meta[COMP]
    eye = (
        lax.broadcasted_iota(jnp.int32, (SUBLANES, SUBLANES), 0)
        == lax.broadcasted_iota(jnp.int32, (SUBLANES, SUBLANES), 1)
    ).astype(f32)
    rate = jnp.sum(
        jnp.broadcast_to(rate_ref[pl.ds(comp, 1), :], (SUBLANES, SUBLANES)) * eye,
        axis=1,
        keepdims=True,
    )
    rate = jnp.broadcast_to(rate, shape)

    def lap_step(r, unused):
        here = diffuse[r]
        below = jnp.where(r > 0, diffuse[jnp.maximum(r - 1, 0)], south)
        above = jnp.where(r < rows - 1, diffuse[jnp.minimum(r + 1, rows - 1)], north)
        total[r] = base[r] + rate * laplace_row(here, below, above, west, east, r, lane)
        return unused

    lax.fori_loop(0, rows, lap_step, 0, unroll=8)

    def peer_step(q, unused):
        block = recv[meta[OTHER] + q, 0:32, :].astype(f32)
        for s in range(slots):
            k = q * slots + s
            sent = block[s * SUBLANES : (s + 1) * SUBLANES].astype(bf16)
            live = (s < count[q]).astype(f32)
            row = source[k]
            total[row] = total[row] + dot_nt(sent, kernels[k]) * live
        return unused

    lax.fori_loop(0, peers, peer_step, 0, unroll=4)

    def out_step(r, unused):
        out[pl.ds(r, SUBLANES, stride=rows), :] = total[r]
        return unused

    lax.fori_loop(0, rows, out_step, 0, unroll=8)


def unpack_kernel(share, small_share, fluxes, recv, first, bias_one, second, bias_two, third,
                  bias_three, small):
    devices = recv.shape[0]
    width = recv.shape[2]
    hidden = second.shape[0]
    halves = hidden // width
    for d in range(devices):
        block = recv[d].astype(f32)
        done = 0
        while done < share:
            at = d * share + done
            h, row = divmod(at, hidden)
            step = min(share - done, hidden - row)
            if h < halves:
                second[row : row + step, h * width : (h + 1) * width] = block[done : done + step]
            done += step
        small[d * small_share : (d + 1) * small_share, :] = block[share : share + small_share]
    for h in range(halves):
        cols = slice(h * width, (h + 1) * width)
        top = h * 24
        first[:, cols] = small[top : top + 16, :]
        bias_one[:, cols] = small[top + 16 : top + 17, :]
        bias_two[:, cols] = small[top + 17 : top + 18, :]
        third[:, cols] = small[top + 19 : top + 19 + fluxes, :]
    bias_three[...] = small[18:19, :]


def shards(
    state,
    target,
    land_mask,
    diffusivity,
    coupling,
    w_in,
    b_in,
    w_mid,
    b_mid,
    w_out,
    b_out,
    remap_weight,
    remap_source,
    remap_target,
    remap_count,
):
    n_gy, n_gx = lax.axis_size("gy"), lax.axis_size("gx")
    tiles = n_gy * n_gx
    devices = 2 * tiles
    comp, row, col = (lax.axis_index(axis) for axis in EVERYWHERE)
    own, other = comp * tiles, (1 - comp) * tiles
    is_top = row == n_gy - 1
    on_fold = jnp.logical_and(comp == 1, is_top)
    line = own + row * n_gx
    here = line + col
    meta = jnp.stack(
        [
            own,
            other,
            line + (col + n_gx - 1) % n_gx,
            line + (col + 1) % n_gx,
            jnp.where(row > 0, here - n_gx, here),
            jnp.where(on_fold, line + n_gx - 1 - col, jnp.where(is_top, here, here + n_gx)),
            comp,
            (row > 0).astype(jnp.int32),
            jnp.logical_or(on_fold, jnp.logical_not(is_top)).astype(jnp.int32),
            on_fold.astype(jnp.int32),
        ]
    ).astype(jnp.int32)
    channels, rows, width = state.shape[1:]
    hidden = w_mid.shape[0]
    inputs = w_in.shape[0]
    fluxes = w_out.shape[1]
    peers, slots = remap_source.shape[3:]
    surface = state.reshape(channels * rows, width)
    goal = target.reshape(channels * rows, width)
    mask = land_mask[0]
    source = remap_source.reshape(peers * slots)
    landing = remap_target.reshape(peers * slots)
    count = remap_count.reshape(peers)
    kernels = remap_weight.reshape(peers * slots, width, width)
    slot_rows = slots * channels

    smem = pl.BlockSpec(memory_space=pltpu.SMEM)
    vmem = pl.BlockSpec(memory_space=pltpu.VMEM)

    outgoing = pl.pallas_call(
        functools.partial(send_kernel, rows, peers, slots),
        name="send",
        out_shape=jax.ShapeDtypeStruct((devices, slot_rows, width), bf16),
        in_specs=[smem, smem, smem, vmem, vmem],
        out_specs=vmem,
        scratch_shapes=[pltpu.VMEM((devices, slot_rows, width), f32)],
    )(meta, source, count, surface, kernels)
    arrived = lax.all_to_all(outgoing, EVERYWHERE, 0, 0, tiled=True)

    def parts(bias):
        high = bias.astype(bf16)
        rest = bias - high.astype(f32)
        middle = rest.astype(bf16)
        low = (rest - middle.astype(f32)).astype(bf16)
        return jnp.stack([high, middle, low], axis=0)

    local_in = jnp.where(comp == 1, jnp.roll(w_in, channels, axis=0), w_in)
    half = jnp.asarray(0.5, bf16)
    w_first = jnp.concatenate(
        [local_in, parts(b_in), jnp.zeros((13, hidden), bf16)], axis=0
    ).T * half
    w_second = w_mid.T * half
    b_second = (b_mid * 0.5)[:, None]
    w_third = jnp.pad(w_out.T, ((0, 16 - fluxes), (0, 0)))
    w_third_back = jnp.pad(w_out * half, ((0, 0), (0, 16 - fluxes)))
    w_second_back = w_mid * half
    w_first_back = local_in

    share = -(-hidden * hidden // (width * devices))
    small_share = -(-24 * hidden // (width * devices))
    packed = -(-(share + small_share) // 8) * 8
    cells = BLOCK_ROWS * width

    new_state, base, diffuse, leaving = pl.pallas_call(
        functools.partial(main_kernel, rows, peers, slots, share, small_share),
        name="main",
        out_shape=(
            jax.ShapeDtypeStruct((channels * rows, width), f32),
            jax.ShapeDtypeStruct((rows, channels, width), f32),
            jax.ShapeDtypeStruct((rows, channels, width), f32),
            jax.ShapeDtypeStruct((devices, slot_rows + packed, width), bf16),
        ),
        in_specs=[smem, smem, smem] + [vmem] * 13,
        out_specs=(vmem,) * 4,
        scratch_shapes=[
            pltpu.VMEM((devices, slot_rows + packed, width), f32),
            pltpu.VMEM((rows, channels, width), f32),
            pltpu.VMEM((32, cells), bf16),
            pltpu.VMEM((hidden + 16, cells), bf16),
            pltpu.VMEM((hidden, cells), bf16),
            pltpu.VMEM((hidden, cells), f32),
            pltpu.VMEM((hidden, cells), f32),
            pltpu.VMEM((hidden, cells), bf16),
            pltpu.VMEM((hidden, cells), bf16),
            pltpu.VMEM((8, cells), f32),
            pltpu.VMEM((16, cells), bf16),
            pltpu.VMEM((16, cells), f32),
            pltpu.VMEM((32, hidden), f32),
            pltpu.VMEM((hidden + 16, hidden), f32),
            pltpu.VMEM((16, hidden), f32),
            pltpu.VMEM((8, width), f32),
            pltpu.VMEM((max(48, small_share * devices), width), f32),
        ],
    )(
        meta,
        landing,
        b_out,
        surface,
        goal,
        mask,
        arrived,
        diffusivity,
        coupling,
        w_first,
        w_second,
        b_second,
        w_third,
        w_third_back,
        w_second_back,
        w_first_back,
    )
    returned = lax.all_to_all(leaving, EVERYWHERE, 0, 0, tiled=True)
    scale = 1.0 / (rows * width * tiles)
    summed = pl.pallas_call(
        functools.partial(sum_kernel, scale),
        name="sum",
        out_shape=jax.ShapeDtypeStruct((devices, packed, width), bf16),
        in_specs=[vmem],
        out_specs=vmem,
    )(returned)
    gathered = lax.all_to_all(summed, EVERYWHERE, 0, 0, tiled=True)
    adjoint = pl.pallas_call(
        functools.partial(back_kernel, rows, peers, slots),
        name="back",
        out_shape=jax.ShapeDtypeStruct((channels * rows, width), f32),
        in_specs=[smem, smem, smem] + [vmem] * 5,
        out_specs=vmem,
        scratch_shapes=[pltpu.VMEM((rows, channels, width), f32)],
    )(meta, source, count, returned, kernels, base, diffuse, diffusivity)
    first, bias_one, second, bias_two, third, bias_three = pl.pallas_call(
        functools.partial(unpack_kernel, share, small_share, fluxes),
        name="unpack",
        out_shape=(
            jax.ShapeDtypeStruct((inputs, hidden), f32),
            jax.ShapeDtypeStruct((1, hidden), f32),
            jax.ShapeDtypeStruct((hidden, hidden), f32),
            jax.ShapeDtypeStruct((1, hidden), f32),
            jax.ShapeDtypeStruct((fluxes, hidden), f32),
            jax.ShapeDtypeStruct((1, width), f32),
        ),
        in_specs=[vmem],
        out_specs=(vmem,) * 6,
        scratch_shapes=[pltpu.VMEM((max(48, small_share * devices), width), f32)],
    )(gathered)
    return (
        new_state.reshape(state.shape),
        adjoint.reshape(state.shape),
        first,
        bias_one[0],
        second,
        bias_two[0],
        third.T,
        bias_three[0, :fluxes],
    )


def solution(mesh):
    tiles = P("comp", None, "gy", "gx")
    placed = (
        tiles,
        tiles,
        P("comp", "gy", "gx"),
        *(P() for _ in range(8)),
        P("comp", "gy", "gx", None, None, None, None),
        P("comp", "gy", "gx", None, None),
        P("comp", "gy", "gx", None, None),
        P("comp", "gy", "gx", None),
    )
    return jax.shard_map(
        shards,
        mesh=mesh,
        in_specs=placed,
        out_specs=(tiles, tiles, *(P() for _ in range(6))),
        check_vma=False,
    )
```

```python
import functools
import math

import jax
import jax.numpy as jnp
from jax import lax
from jax.experimental import pallas as pl
from jax.experimental.pallas import tpu as pltpu
from jax.sharding import PartitionSpec as P

EVERYWHERE = ("comp", "gy", "gx")
BLOCK_ROWS = 8
CHUNK = 256
SUBLANES = 8

OWN, OTHER, WEST, EAST, SOUTH, NORTH, COMP, HAS_SOUTH, HAS_NORTH, ON_FOLD = range(10)

f32 = jnp.float32
bf16 = jnp.bfloat16


def dot(a, b):
    return jnp.dot(a, b, preferred_element_type=f32)


def dot_nt(a, b):
    return lax.dot_general(a, b, (((1,), (1,)), ((), ())), preferred_element_type=f32)


def mirror(tile):
    width = tile.shape[1]
    row = lax.broadcasted_iota(jnp.int32, (width, width), 0)
    col = lax.broadcasted_iota(jnp.int32, (width, width), 1)
    flip = (row + col == width - 1).astype(f32).astype(bf16)
    return dot(tile.astype(bf16), flip)


def put_edges(meta, first, last, bottom, top, stage):
    stage[meta[EAST], 0:SUBLANES, :] = last
    stage[meta[WEST], SUBLANES : 2 * SUBLANES, :] = first
    top = jnp.where(meta[ON_FOLD] == 1, mirror(top), top)
    stage[meta[NORTH], 2 * SUBLANES : 3 * SUBLANES, :] = top
    stage[meta[SOUTH], 3 * SUBLANES : 4 * SUBLANES, :] = bottom


def take_edges(tile, r, lane, sides):
    width = tile.shape[1]
    here = lane == r
    first, last = sides
    first = jnp.where(here, pltpu.roll(tile, r, 1), first)
    last = jnp.where(here, pltpu.roll(tile, lax.rem(r + 1, width), 1), last)
    return first, last


def get_edges(meta, recv):
    west = recv[meta[WEST], 0:32, :].astype(f32)[0:SUBLANES]
    east = recv[meta[EAST], 0:32, :].astype(f32)[SUBLANES : 2 * SUBLANES]
    south = recv[meta[SOUTH], 0:32, :].astype(f32)[2 * SUBLANES : 3 * SUBLANES]
    above = recv[meta[NORTH], 0:32, :].astype(f32)
    north = jnp.where(
        meta[ON_FOLD] == 1,
        above[2 * SUBLANES : 3 * SUBLANES],
        above[3 * SUBLANES : 4 * SUBLANES],
    )
    south = jnp.where(meta[HAS_SOUTH] == 1, south, 0.0)
    north = jnp.where(meta[HAS_NORTH] == 1, north, 0.0)
    return west, east, south, north


def laplace_row(here, below, above, west, east, r, lane):
    width = here.shape[1]
    left = jnp.where(
        lane == 0, pltpu.roll(west, lax.rem(width - r, width), 1), pltpu.roll(here, 1, 1)
    )
    right = jnp.where(
        lane == width - 1, pltpu.roll(east, width - 1 - r, 1), pltpu.roll(here, width - 1, 1)
    )
    return left + right + below + above - 4.0 * here


def column_of(row, comp):
    eye = (
        lax.broadcasted_iota(jnp.int32, (SUBLANES, SUBLANES), 0)
        == lax.broadcasted_iota(jnp.int32, (SUBLANES, SUBLANES), 1)
    ).astype(f32)
    return jnp.sum(
        jnp.broadcast_to(row[pl.ds(comp, 1), :], (SUBLANES, SUBLANES)) * eye,
        axis=1,
        keepdims=True,
    )


def send_kernel(
    rows, peers, slots, meta, source, count, state, kernels, out, by_row, stage, blocks, sems
):
    width = state.shape[1]
    shape = (SUBLANES, width)
    lane = lax.broadcasted_iota(jnp.int32, shape, 1)
    parts = sems.shape[0]
    part = peers // parts
    copies = [
        pltpu.make_async_copy(
            kernels.at[pl.ds(i * part * slots, part * slots)],
            blocks.at[pl.ds(i * part * slots, part * slots)],
            sems.at[i],
        )
        for i in range(parts)
    ]
    for copy in copies:
        copy.start()
    stage[pl.ds(meta[OWN], peers)] = jnp.zeros((peers,) + stage.shape[1:], f32)

    def row_step(r, sides):
        tile = state[pl.ds(r, SUBLANES, stride=rows), :]
        by_row[r] = tile
        return take_edges(tile, r, lane, sides)

    zero = jnp.zeros(shape, f32)
    first, last = lax.fori_loop(0, rows, row_step, (zero, zero), unroll=8)
    put_edges(meta, first, last, by_row[0], by_row[rows - 1], stage)

    def peer_step(q, unused):
        for s in range(slots):
            k = q * slots + s
            picked = by_row[source[s, q]].astype(bf16)
            live = (s < count[q]).astype(f32)
            stage[meta[OTHER] + q, s * SUBLANES : (s + 1) * SUBLANES, :] = (
                dot(picked, blocks[k]) * live
            )
        return unused

    for i in range(parts):
        copies[i].wait()
        lax.fori_loop(i * part, (i + 1) * part, peer_step, 0, unroll=math.gcd(part, 4))
    out[...] = stage[...].astype(bf16)


def weave(*lists):
    keyed = []
    for order, steps in enumerate(lists):
        for i, step in enumerate(steps):
            keyed.append(((i + 0.5) / len(steps), order, i, step))
    for entry in sorted(keyed, key=lambda e: e[:3]):
        entry[3]()


def main_kernel(
    rows,
    peers,
    slots,
    share,
    small_share,
    meta,
    landing,
    b_out,
    state,
    goal,
    mask,
    recv,
    rate_ref,
    couple_ref,
    w_first,
    w_second,
    b_second,
    w_third,
    w_third_back,
    w_second_back,
    w_first_back,
    new_out,
    base_out,
    diffuse_out,
    send_out,
    grad_out,
    stage,
    grad_stage,
    other,
    misfits,
    feats,
    hid_firsts,
    hid_seconds,
    slope_firsts,
    slope_seconds,
    flux_cots,
    cot_second,
    cot_first,
    flux,
    feat_cot,
    g_first,
    g_second,
    g_third,
    g_bias,
    edges,
    small,
):
    width = state.shape[2]
    hidden = w_second.shape[0]
    shape = (SUBLANES, width)
    cells = BLOCK_ROWS * width
    chunks = cells // CHUNK
    lane = lax.broadcasted_iota(jnp.int32, shape, 1)
    sub = lax.broadcasted_iota(jnp.int32, shape, 0)
    fluxes = couple_ref.shape[2]
    pad = BLOCK_ROWS

    other[...] = jnp.zeros(other.shape, f32)

    def land(p, unused):
        block = recv[meta[OTHER] + p, 0:32, :].astype(f32)
        for s in range(slots):
            row = landing[s, p] + pad
            other[row] = other[row] + block[s * SUBLANES : (s + 1) * SUBLANES]
        return unused

    lax.fori_loop(0, peers, land, 0, unroll=2)
    west, east, south, north = get_edges(meta, recv)
    comp = meta[COMP]
    rate = jnp.broadcast_to(column_of(rate_ref, comp), shape)
    pairs = couple_ref[comp]
    couple = [jnp.broadcast_to(pairs[:, f : f + 1], shape) for f in range(fluxes)]
    ones = (lax.broadcasted_iota(jnp.int32, (16, cells), 0) < 3).astype(f32).astype(bf16)
    for ref in (*hid_firsts, *hid_seconds, *flux_cots, *feats):
        ref[...] = jnp.zeros(ref.shape, bf16)
    for ref in (*slope_firsts, *slope_seconds):
        ref[...] = jnp.zeros(ref.shape, f32)
    for ref in feats:
        ref[16:32, :] = ones
    for ref in hid_firsts:
        ref[hidden : hidden + 16, :] = ones
    for ref in (g_first, g_second, g_third, g_bias, edges):
        ref[...] = jnp.zeros(ref.shape, f32)
    bias = jnp.broadcast_to(b_second[...], (hidden, CHUNK))
    b_third = jnp.zeros(shape, f32)
    for f in range(fluxes):
        b_third = jnp.where(sub == f, b_out[f], b_third)

    def forward(block, feat, hid_first, hid_second, slope_first, slope_second, flux_cot):
        start = block * BLOCK_ROWS

        def take(i):
            at = pl.ds(i * width, width)
            r = start + i
            feat[0:16, at] = jnp.concatenate([state[r], other[r + pad]], axis=0).astype(bf16)

        def layer(net, hid_ref, slope_ref, at):
            turn = jnp.tanh(net)
            up = 1.0 + turn
            hid = net * up
            hid_ref[0:hidden, at] = hid.astype(bf16)
            slope_ref[:, at] = (up + hid) - hid * turn

        def first(j):
            at = pl.ds(j * CHUNK, CHUNK)
            layer(dot(w_first[...], feat[:, at]), hid_first, slope_first, at)

        def second(j):
            at = pl.ds(j * CHUNK, CHUNK)
            net = dot(w_second[...], hid_first[0:hidden, at]) + bias
            layer(net, hid_second, slope_second, at)

        def third(j):
            at = pl.ds(j * CHUNK, CHUNK)
            flux[:, at] = dot(w_third[...], hid_second[:, at])[0:SUBLANES]

        def fields(i):
            at = pl.ds(i * width, width)
            r = start + i
            here = state[r]
            below = jnp.where(r > 0, state[jnp.maximum(r - 1, 0)], south)
            above = jnp.where(r < rows - 1, state[jnp.minimum(r + 1, rows - 1)], north)
            lap = laplace_row(here, below, above, west, east, r, lane)
            wet = jnp.broadcast_to(mask[pl.ds(r, 1), :].astype(f32), shape)
            spread_mask = jnp.where(comp == 1, wet, 1.0)
            wet_flux = (flux[:, at] + b_third) * wet
            updated = here + rate * spread_mask * lap
            for f in range(fluxes):
                updated = updated + couple[f] * jnp.broadcast_to(wet_flux[f : f + 1], shape)
            new_out[pl.ds(r, SUBLANES, stride=rows), :] = updated
            misfit = updated - goal[pl.ds(r, SUBLANES, stride=rows), :]
            diffuse = spread_mask * misfit
            diffuse_out[r] = diffuse
            edges[0], edges[1] = take_edges(diffuse, r, lane, (edges[0], edges[1]))
            misfits[r + pad] = misfit
            pulled = jnp.zeros(shape, f32)
            for f in range(fluxes):
                total = jnp.sum(couple[f] * misfit, axis=0, keepdims=True)
                pulled = jnp.where(sub == f, jnp.broadcast_to(total, shape), pulled)
            pulled = (pulled * wet).astype(bf16)
            flux_cot[0:SUBLANES, at] = pulled
            g_bias[...] = g_bias[...] + pulled.astype(f32)

        steps = [functools.partial(take, i) for i in range(BLOCK_ROWS)]
        for stage_step in (first, second, third):
            steps += [functools.partial(stage_step, j) for j in range(chunks)]
        return steps + [functools.partial(fields, i) for i in range(BLOCK_ROWS)]

    def backward(block, feat, hid_first, hid_second, slope_first, slope_second, flux_cot):
        start = block * BLOCK_ROWS

        def second(j):
            at = pl.ds(j * CHUNK, CHUNK)
            net = dot(w_third_back[...], flux_cot[:, at])
            cot_second[:, at] = (net * slope_second[:, at]).astype(bf16)

        def first(j):
            at = pl.ds(j * CHUNK, CHUNK)
            net = dot(w_second_back[...], cot_second[:, at])
            cot_first[:, at] = (net * slope_first[:, at]).astype(bf16)

        def inputs(j):
            at = pl.ds(j * CHUNK, CHUNK)
            feat_cot[:, at] = dot(w_first_back[...], cot_first[:, at])

        def leave(i):
            at = pl.ds(i * width, width)
            r = start + i + pad
            base_out[r] = misfits[r] + feat_cot[0:SUBLANES, at]
            other[r] = feat_cot[SUBLANES : 2 * SUBLANES, at]

        def grad_second():
            g_second[...] += dot_nt(hid_first[...], cot_second[...])

        def grad_third():
            g_third[...] += dot_nt(flux_cot[...], hid_second[...])

        def grad_first():
            g_first[...] += dot_nt(feat[...], cot_first[...])

        steps = [functools.partial(second, j) for j in range(chunks)]
        steps += [functools.partial(first, j) for j in range(chunks)]
        steps += [grad_third, grad_second]
        steps += [functools.partial(inputs, j) for j in range(chunks)]
        steps += [grad_first]
        return steps + [functools.partial(leave, i) for i in range(BLOCK_ROWS)]

    sets = list(
        zip(feats, hid_firsts, hid_seconds, slope_firsts, slope_seconds, flux_cots, strict=True)
    )
    blocks = rows // BLOCK_ROWS

    def pair_step(pair, unused):
        even = pair * 2
        weave(backward(even - 1, *sets[1]), forward(even, *sets[0]))
        weave(backward(even, *sets[0]), forward(even + 1, *sets[1]))
        return unused

    lax.fori_loop(0, blocks // 2, pair_step, 0)
    weave(backward(blocks - 1, *sets[1]))

    stage[pl.ds(meta[OWN], peers)] = jnp.zeros((peers,) + stage.shape[1:], f32)

    def leave(p, unused):
        for s in range(slots):
            row = landing[s, p] + pad
            stage[meta[OTHER] + p, s * SUBLANES : (s + 1) * SUBLANES, :] = other[row]
        return unused

    lax.fori_loop(0, peers, leave, 0, unroll=2)
    put_edges(meta, edges[0], edges[1], diffuse_out[0], diffuse_out[rows - 1], stage)
    send_out[...] = stage[...].astype(bf16)

    devices = stage.shape[0]
    halves = hidden // width
    inputs = 2 * SUBLANES
    small[...] = jnp.zeros(small.shape, f32)
    low, high = g_first[0:SUBLANES, :], g_first[SUBLANES:inputs, :]
    low, high = jnp.where(comp == 1, high, low), jnp.where(comp == 1, low, high)
    bias_sum = jnp.sum(g_bias[...], axis=1, keepdims=True)
    bias_row = jnp.sum(jnp.where(sub == lane, jnp.broadcast_to(bias_sum, shape), 0.0), axis=0,
                       keepdims=True)
    for h in range(halves):
        cols = slice(h * width, (h + 1) * width)
        top = h * 24
        small[top : top + 8, :] = low[:, cols]
        small[top + 8 : top + 16, :] = high[:, cols]
        small[top + 16 : top + 17, :] = g_first[inputs : inputs + 1, cols]
        small[top + 17 : top + 18, :] = g_second[hidden : hidden + 1, cols]
        if h == 0:
            small[top + 18 : top + 19, :] = bias_row
        small[top + 19 : top + 19 + fluxes, :] = g_third[0:fluxes, cols]
    for d in range(devices):
        done = 0
        while done < share:
            at = d * share + done
            h, row = divmod(at, hidden)
            step = min(share - done, hidden - row)
            if h < halves:
                grad_stage[d, done : done + step, :] = g_second[
                    row : row + step, h * width : (h + 1) * width
                ]
            done += step
        piece = small[d * small_share : (d + 1) * small_share, :]
        head = piece.astype(bf16).astype(f32)
        grad_stage[d, share : share + small_share, :] = head
        grad_stage[d, share + small_share : share + 2 * small_share, :] = piece - head
    grad_out[...] = grad_stage[...].astype(bf16)


def sum_kernel(scale, share, small_share, recv, out, stage):
    devices = recv.shape[0]
    total = recv[0].astype(f32)
    for d in range(1, devices):
        total = total + recv[d].astype(f32)
    stage[...] = total * scale
    low = slice(share + small_share, share + 2 * small_share)
    piece = stage[share : share + small_share, :] + stage[low, :]
    head = piece.astype(bf16).astype(f32)
    stage[share : share + small_share, :] = head
    stage[low, :] = piece - head
    total = stage[...].astype(bf16)
    for d in range(devices):
        out[d] = total


def back_kernel(
    rows, peers, slots, meta, source, count, recv, kernels, base, diffuse, rate_ref, out, total
):
    width = diffuse.shape[2]
    shape = (SUBLANES, width)
    lane = lax.broadcasted_iota(jnp.int32, shape, 1)
    west, east, south, north = get_edges(meta, recv)
    comp = meta[COMP]
    rate = jnp.broadcast_to(column_of(rate_ref, comp), shape)

    def lap_step(r, unused):
        here = diffuse[r]
        below = jnp.where(r > 0, diffuse[jnp.maximum(r - 1, 0)], south)
        above = jnp.where(r < rows - 1, diffuse[jnp.minimum(r + 1, rows - 1)], north)
        total[r] = base[r + BLOCK_ROWS] + rate * laplace_row(here, below, above, west, east, r, lane)
        return unused

    lax.fori_loop(0, rows, lap_step, 0, unroll=8)

    def peer_step(q, unused):
        block = recv[meta[OTHER] + q, 0:32, :].astype(f32)
        for s in range(slots):
            k = q * slots + s
            sent = block[s * SUBLANES : (s + 1) * SUBLANES].astype(bf16)
            live = (s < count[q]).astype(f32)
            row = source[s, q]
            total[row] = total[row] + dot_nt(sent, kernels[k]) * live
        return unused

    lax.fori_loop(0, peers, peer_step, 0, unroll=4)

    def out_step(r, unused):
        out[pl.ds(r, SUBLANES, stride=rows), :] = total[r]
        return unused

    lax.fori_loop(0, rows, out_step, 0, unroll=8)


def unpack_kernel(share, small_share, fluxes, recv, first, bias_one, second, bias_two, third,
                  bias_three, small):
    devices = recv.shape[0]
    width = recv.shape[2]
    hidden = second.shape[0]
    halves = hidden // width
    for d in range(devices):
        block = recv[d].astype(f32)
        done = 0
        while done < share:
            at = d * share + done
            h, row = divmod(at, hidden)
            step = min(share - done, hidden - row)
            if h < halves:
                second[row : row + step, h * width : (h + 1) * width] = block[done : done + step]
            done += step
        small[d * small_share : (d + 1) * small_share, :] = (
            block[share : share + small_share]
            + block[share + small_share : share + 2 * small_share]
        )
    for h in range(halves):
        cols = slice(h * width, (h + 1) * width)
        top = h * 24
        first[:, cols] = small[top : top + 16, :]
        bias_one[:, cols] = small[top + 16 : top + 17, :]
        bias_two[:, cols] = small[top + 17 : top + 18, :]
        third[:, cols] = small[top + 19 : top + 19 + fluxes, :]
    bias_three[...] = small[18:19, 0:fluxes]


def shards(
    state,
    target,
    land_mask,
    diffusivity,
    coupling,
    w_in,
    b_in,
    w_mid,
    b_mid,
    w_out,
    b_out,
    remap_weight,
    remap_source,
    remap_target,
    remap_count,
):
    n_gy, n_gx = lax.axis_size("gy"), lax.axis_size("gx")
    tiles = n_gy * n_gx
    devices = 2 * tiles
    comp, row, col = (lax.axis_index(axis) for axis in EVERYWHERE)
    own, other = comp * tiles, (1 - comp) * tiles
    is_top = row == n_gy - 1
    on_fold = jnp.logical_and(comp == 1, is_top)
    line = own + row * n_gx
    here = line + col
    meta = jnp.stack(
        [
            own,
            other,
            line + (col + n_gx - 1) % n_gx,
            line + (col + 1) % n_gx,
            jnp.where(row > 0, here - n_gx, here),
            jnp.where(on_fold, line + n_gx - 1 - col, jnp.where(is_top, here, here + n_gx)),
            comp,
            (row > 0).astype(jnp.int32),
            jnp.logical_or(on_fold, jnp.logical_not(is_top)).astype(jnp.int32),
            on_fold.astype(jnp.int32),
        ]
    ).astype(jnp.int32)
    channels, rows, width = state.shape[1:]
    hidden = w_mid.shape[0]
    inputs = w_in.shape[0]
    fluxes = w_out.shape[1]
    peers, slots = remap_source.shape[3:]
    surface = state.reshape(channels * rows, width)
    goal = target.reshape(channels * rows, width)
    mask = land_mask[0]
    source = remap_source.reshape(peers, slots).T
    landing = remap_target.reshape(peers, slots).T
    count = remap_count.reshape(peers)
    kernels = remap_weight.reshape(peers * slots, width, width)
    slot_rows = slots * channels

    smem = pl.BlockSpec(memory_space=pltpu.SMEM)
    vmem = pl.BlockSpec(memory_space=pltpu.VMEM)

    anywhere = pl.BlockSpec(memory_space=pl.ANY)
    parts = math.gcd(peers, 4)
    outgoing, by_row = pl.pallas_call(
        functools.partial(send_kernel, rows, peers, slots),
        name="send",
        out_shape=(
            jax.ShapeDtypeStruct((devices, slot_rows, width), bf16),
            jax.ShapeDtypeStruct((rows, channels, width), f32),
        ),
        in_specs=[smem, smem, smem, vmem, anywhere],
        out_specs=(vmem, vmem),
        scratch_shapes=[
            pltpu.VMEM((devices, slot_rows, width), f32),
            pltpu.VMEM(kernels.shape, bf16),
            pltpu.SemaphoreType.DMA((parts,)),
        ],
    )(meta, source, count, surface, kernels)
    arrived = lax.all_to_all(outgoing, EVERYWHERE, 0, 0, tiled=True)

    def pieces(bias):
        high = bias.astype(bf16)
        rest = bias - high.astype(f32)
        middle = rest.astype(bf16)
        low = (rest - middle.astype(f32)).astype(bf16)
        return jnp.stack([high, middle, low], axis=0)

    local_in = jnp.where(comp == 1, jnp.roll(w_in, channels, axis=0), w_in)
    half = jnp.asarray(0.5, bf16)
    w_first = jnp.concatenate(
        [local_in, pieces(b_in), jnp.zeros((13, hidden), bf16)], axis=0
    ).T * half
    w_second = w_mid.T * half
    b_second = (b_mid * 0.5)[:, None]
    w_third = jnp.pad(w_out.T, ((0, 16 - fluxes), (0, 0)))
    w_third_back = jnp.pad(w_out * half, ((0, 0), (0, 16 - fluxes)))
    w_second_back = w_mid * half
    w_first_back = local_in

    share = -(-hidden * hidden // (width * devices))
    small_share = -(-24 * hidden // (width * devices))
    packed = -(-(share + 2 * small_share) // 8) * 8
    cells = BLOCK_ROWS * width

    def twice(*args):
        return (pltpu.VMEM(*args), pltpu.VMEM(*args))

    tall = (rows + BLOCK_ROWS, channels, width)
    new_state, base, diffuse, leaving, gradients = pl.pallas_call(
        functools.partial(main_kernel, rows, peers, slots, share, small_share),
        name="main",
        out_shape=(
            jax.ShapeDtypeStruct((channels * rows, width), f32),
            jax.ShapeDtypeStruct(tall, f32),
            jax.ShapeDtypeStruct((rows, channels, width), f32),
            jax.ShapeDtypeStruct((devices, slot_rows, width), bf16),
            jax.ShapeDtypeStruct((devices, packed, width), bf16),
        ),
        in_specs=[smem, smem, smem] + [vmem] * 13,
        out_specs=(vmem,) * 5,
        scratch_shapes=[
            pltpu.VMEM((devices, slot_rows, width), f32),
            pltpu.VMEM((devices, packed, width), f32),
            pltpu.VMEM(tall, f32),
            pltpu.VMEM(tall, f32),
            twice((32, cells), bf16),
            twice((hidden + 16, cells), bf16),
            twice((hidden, cells), bf16),
            twice((hidden, cells), f32),
            twice((hidden, cells), f32),
            twice((16, cells), bf16),
            pltpu.VMEM((hidden, cells), bf16),
            pltpu.VMEM((hidden, cells), bf16),
            pltpu.VMEM((8, cells), f32),
            pltpu.VMEM((16, cells), f32),
            pltpu.VMEM((32, hidden), f32),
            pltpu.VMEM((hidden + 16, hidden), f32),
            pltpu.VMEM((16, hidden), f32),
            pltpu.VMEM((8, width), f32),
            pltpu.VMEM((2, 8, width), f32),
            pltpu.VMEM((max(48, small_share * devices), width), f32),
        ],
    )(
        meta,
        landing,
        b_out,
        by_row,
        goal,
        mask,
        arrived,
        diffusivity,
        coupling,
        w_first,
        w_second,
        b_second,
        w_third,
        w_third_back,
        w_second_back,
        w_first_back,
    )
    gradients = lax.all_to_all(gradients, EVERYWHERE, 0, 0, tiled=True)
    returned = lax.all_to_all(leaving, EVERYWHERE, 0, 0, tiled=True)
    scale = 1.0 / (rows * width * tiles)
    summed = pl.pallas_call(
        functools.partial(sum_kernel, scale, share, small_share),
        name="sum",
        out_shape=jax.ShapeDtypeStruct((devices, packed, width), bf16),
        in_specs=[vmem],
        out_specs=vmem,
        scratch_shapes=[pltpu.VMEM((packed, width), f32)],
    )(gradients)
    gathered = lax.all_to_all(summed, EVERYWHERE, 0, 0, tiled=True)
    adjoint = pl.pallas_call(
        functools.partial(back_kernel, rows, peers, slots),
        name="back",
        out_shape=jax.ShapeDtypeStruct((channels * rows, width), f32),
        in_specs=[smem, smem, smem] + [vmem] * 5,
        out_specs=vmem,
        scratch_shapes=[pltpu.VMEM((rows, channels, width), f32)],
    )(meta, source, count, returned, kernels, base, diffuse, diffusivity)
    first, bias_one, second, bias_two, third, bias_three = pl.pallas_call(
        functools.partial(unpack_kernel, share, small_share, fluxes),
        name="unpack",
        out_shape=(
            jax.ShapeDtypeStruct((inputs, hidden), f32),
            jax.ShapeDtypeStruct((1, hidden), f32),
            jax.ShapeDtypeStruct((hidden, hidden), f32),
            jax.ShapeDtypeStruct((1, hidden), f32),
            jax.ShapeDtypeStruct((fluxes, hidden), f32),
            jax.ShapeDtypeStruct((1, fluxes), f32),
        ),
        in_specs=[vmem],
        out_specs=(vmem,) * 6,
        scratch_shapes=[pltpu.VMEM((max(48, small_share * devices), width), f32)],
    )(gathered)
    return (
        new_state.reshape(state.shape),
        adjoint.reshape(state.shape),
        first,
        bias_one[0],
        second,
        bias_two[0],
        third.T,
        bias_three[0],
    )


def solution(mesh):
    tiles = P("comp", None, "gy", "gx")
    placed = (
        tiles,
        tiles,
        P("comp", "gy", "gx"),
        *(P() for _ in range(8)),
        P("comp", "gy", "gx", None, None, None, None),
        P("comp", "gy", "gx", None, None),
        P("comp", "gy", "gx", None, None),
        P("comp", "gy", "gx", None),
    )
    return jax.shard_map(
        shards,
        mesh=mesh,
        in_specs=placed,
        out_specs=(tiles, tiles, *(P() for _ in range(6))),
        check_vma=False,
    )
```

```python
import functools
import math

import jax
import jax.numpy as jnp
from jax import lax
from jax.experimental import pallas as pl
from jax.experimental.pallas import tpu as pltpu
from jax.sharding import PartitionSpec as P

EVERYWHERE = ("comp", "gy", "gx")
BLOCK_ROWS = 8
CHUNK = 256
SUBLANES = 8

KEYS = {
    "take": (0.0, 0.05),
    "first": (0.05, 0.3),
    "second": (0.3, 0.6),
    "third": (0.6, 0.65),
    "fields": (0.65, 1.0),
    "cot_second": (0.05, 0.3),
    "cot_first": (0.3, 0.6),
    "cot_inputs": (0.62, 0.7),
    "leave": (0.9, 1.0),
    "grad_second": 0.61,
    "grad_third": 0.605,
    "grad_first": 0.71,
}

OWN, OTHER, WEST, EAST, SOUTH, NORTH, COMP, HAS_SOUTH, HAS_NORTH, ON_FOLD = range(10)

f32 = jnp.float32
bf16 = jnp.bfloat16


def place():
    n_gy, n_gx = lax.axis_size("gy"), lax.axis_size("gx")
    comp, row, col = (lax.axis_index(axis) for axis in EVERYWHERE)
    tiles = n_gy * n_gx
    own = comp * tiles
    line = own + row * n_gx
    here = line + col
    is_top = row == n_gy - 1
    on_fold = jnp.logical_and(comp == 1, is_top)
    up = jnp.where(is_top, here, here + n_gx)
    return (
        own,
        (1 - comp) * tiles,
        line + lax.rem(col + (n_gx - 1), n_gx),
        line + lax.rem(col + 1, n_gx),
        jnp.where(row > 0, here - n_gx, here),
        jnp.where(on_fold, line + (n_gx - 1) - col, up),
        comp,
        (row > 0).astype(jnp.int32),
        jnp.logical_or(on_fold, jnp.logical_not(is_top)).astype(jnp.int32),
        on_fold.astype(jnp.int32),
    )


def dot(a, b):
    return jnp.dot(a, b, preferred_element_type=f32)


def dot_nt(a, b):
    return lax.dot_general(a, b, (((1,), (1,)), ((), ())), preferred_element_type=f32)


def mirror(tile):
    width = tile.shape[1]
    row = lax.broadcasted_iota(jnp.int32, (width, width), 0)
    col = lax.broadcasted_iota(jnp.int32, (width, width), 1)
    flip = (row + col == width - 1).astype(f32).astype(bf16)
    return dot(tile.astype(bf16), flip)


def put_edges(meta, first, last, bottom, top, stage):
    stage[meta[EAST], 0:SUBLANES, :] = last
    stage[meta[WEST], SUBLANES : 2 * SUBLANES, :] = first
    top = jnp.where(meta[ON_FOLD] == 1, mirror(top), top)
    stage[meta[NORTH], 2 * SUBLANES : 3 * SUBLANES, :] = top
    stage[meta[SOUTH], 3 * SUBLANES : 4 * SUBLANES, :] = bottom


def take_edges(tile, r, lane, sides):
    width = tile.shape[1]
    here = lane == r
    first, last = sides
    first = jnp.where(here, pltpu.roll(tile, r, 1), first)
    last = jnp.where(here, pltpu.roll(tile, lax.rem(r + 1, width), 1), last)
    return first, last


def get_edges(meta, recv):
    west = recv[meta[WEST]].astype(f32)[0:SUBLANES]
    east = recv[meta[EAST]].astype(f32)[SUBLANES : 2 * SUBLANES]
    south = recv[meta[SOUTH]].astype(f32)[2 * SUBLANES : 3 * SUBLANES]
    above = recv[meta[NORTH]].astype(f32)
    north = jnp.where(
        meta[ON_FOLD] == 1,
        above[2 * SUBLANES : 3 * SUBLANES],
        above[3 * SUBLANES : 4 * SUBLANES],
    )
    south = jnp.where(meta[HAS_SOUTH] == 1, south, 0.0)
    north = jnp.where(meta[HAS_NORTH] == 1, north, 0.0)
    return west, east, south, north


def laplace_row(here, below, above, west, east, r, lane):
    width = here.shape[1]
    left = jnp.where(
        lane == 0, pltpu.roll(west, lax.rem(width - r, width), 1), pltpu.roll(here, 1, 1)
    )
    right = jnp.where(
        lane == width - 1, pltpu.roll(east, width - 1 - r, 1), pltpu.roll(here, width - 1, 1)
    )
    return left + right + below + above - 4.0 * here


def column_of(row, comp):
    eye = (
        lax.broadcasted_iota(jnp.int32, (SUBLANES, SUBLANES), 0)
        == lax.broadcasted_iota(jnp.int32, (SUBLANES, SUBLANES), 1)
    ).astype(f32)
    return jnp.sum(
        jnp.broadcast_to(row[pl.ds(comp, 1), :], (SUBLANES, SUBLANES)) * eye,
        axis=1,
        keepdims=True,
    )


def send_kernel(
    rows, peers, slots, source, count, state, kernels, out, by_row, stage, blocks, sems
):
    meta = place()
    width = state.shape[1]
    shape = (SUBLANES, width)
    lane = lax.broadcasted_iota(jnp.int32, shape, 1)
    parts = sems.shape[0]
    part = peers // parts
    copies = [
        pltpu.make_async_copy(
            kernels.at[pl.ds(i * part * slots, part * slots)],
            blocks.at[pl.ds(i * part * slots, part * slots)],
            sems.at[i],
        )
        for i in range(parts)
    ]
    for copy in copies:
        copy.start()
    stage[pl.ds(meta[OWN], peers)] = jnp.zeros((peers,) + stage.shape[1:], f32)

    def row_step(r, sides):
        tile = state[pl.ds(r, SUBLANES, stride=rows), :]
        by_row[r] = tile
        return take_edges(tile, r, lane, sides)

    zero = jnp.zeros(shape, f32)
    first, last = lax.fori_loop(0, rows, row_step, (zero, zero), unroll=32)
    put_edges(meta, first, last, by_row[0], by_row[rows - 1], stage)

    def peer_step(q, unused):
        for s in range(slots):
            k = q * slots + s
            picked = by_row[source[s, q]].astype(bf16)
            live = (s < count[q]).astype(f32)
            stage[meta[OTHER] + q, s * SUBLANES : (s + 1) * SUBLANES, :] = (
                dot(picked, blocks[k]) * live
            )
        return unused

    for i in range(parts):
        copies[i].wait()
        lax.fori_loop(i * part, (i + 1) * part, peer_step, 0, unroll=math.gcd(part, 4))
    out[...] = stage[...].astype(bf16)


def spread(low, high, step, count):
    return [
        (low + (high - low) * (i + 0.5) / count, functools.partial(step, i)) for i in range(count)
    ]


def weave(*lists):
    for entry in sorted((e for steps in lists for e in steps), key=lambda e: e[0]):
        entry[1]()


def main_kernel(
    rows,
    peers,
    slots,
    share,
    small_share,
    landing,
    b_out,
    state_in,
    goal_in,
    mask,
    recv_in,
    rate_ref,
    couple_ref,
    w_first,
    w_second,
    b_second,
    w_third,
    w_third_back,
    w_second_back,
    w_first_back,
    new_hbm,
    base_hbm,
    diffuse_hbm,
    send_out,
    state,
    goal,
    recv,
    new_out,
    base_out,
    diffuse_out,
    sems,
    stage,
    other,
    misfits,
    feats,
    hid_firsts,
    hid_seconds,
    slope_firsts,
    slope_seconds,
    flux_cots,
    cot_second,
    cot_first,
    flux,
    feat_cot,
    g_first,
    g_second,
    g_third,
    g_bias,
    edges,
    small,
):
    width = state.shape[2]
    hidden = w_second.shape[0]
    shape = (SUBLANES, width)
    cells = BLOCK_ROWS * width
    chunks = cells // CHUNK
    lane = lax.broadcasted_iota(jnp.int32, shape, 1)
    sub = lax.broadcasted_iota(jnp.int32, shape, 0)
    fluxes = couple_ref.shape[2]
    meta = place()
    slot_rows = recv.shape[1]
    fetches = [
        pltpu.make_async_copy(recv_in, recv, sems.at[0]),
        pltpu.make_async_copy(state_in, state, sems.at[1]),
        pltpu.make_async_copy(goal_in, goal, sems.at[2]),
    ]
    for fetch in fetches:
        fetch.start()

    other[...] = jnp.zeros(other.shape, f32)

    fetches[0].wait()

    def land(p, unused):
        block = recv[meta[OTHER] + p].astype(f32)
        for s in range(slots):
            row = landing[s, p]
            other[row] = other[row] + block[s * SUBLANES : (s + 1) * SUBLANES]
        return unused

    lax.fori_loop(0, peers, land, 0, unroll=2)
    west, east, south, north = get_edges(meta, recv)
    comp = meta[COMP]
    rate = jnp.broadcast_to(column_of(rate_ref, comp), shape)
    pairs = couple_ref[comp]
    couple = [jnp.broadcast_to(pairs[:, f : f + 1], shape) for f in range(fluxes)]
    ones = (lax.broadcasted_iota(jnp.int32, (16, cells), 0) < 3).astype(f32).astype(bf16)
    for ref in flux_cots:
        ref[...] = jnp.zeros(ref.shape, bf16)
    for ref in feats:
        ref[16:32, :] = ones
    for ref in hid_firsts:
        ref[hidden : hidden + 16, :] = ones
    for ref in (g_first, g_second, g_third, g_bias, edges):
        ref[...] = jnp.zeros(ref.shape, f32)
    bias = jnp.broadcast_to(b_second[...], (hidden, CHUNK))
    fetches[1].wait()
    fetches[2].wait()
    b_third = jnp.zeros(shape, f32)
    for f in range(fluxes):
        b_third = jnp.where(sub == f, b_out[f], b_third)

    def forward(block, feat, hid_first, hid_second, slope_first, slope_second, flux_cot):
        start = block * BLOCK_ROWS

        def take(i):
            at = pl.ds(i * width, width)
            r = start + i
            feat[0:16, at] = jnp.concatenate([state[r], other[r]], axis=0).astype(bf16)

        def layer(net, hid_ref, slope_ref, at):
            turn = jnp.tanh(net)
            up = 1.0 + turn
            hid = net * up
            hid_ref[0:hidden, at] = hid.astype(bf16)
            slope_ref[:, at] = (up + hid) - hid * turn

        def first(j):
            at = pl.ds(j * CHUNK, CHUNK)
            layer(dot(w_first[...], feat[:, at]), hid_first, slope_first, at)

        def second(j):
            at = pl.ds(j * CHUNK, CHUNK)
            net = dot(w_second[...], hid_first[0:hidden, at]) + bias
            layer(net, hid_second, slope_second, at)

        def third(j):
            at = pl.ds(j * CHUNK, CHUNK)
            flux[:, at] = dot(w_third[...], hid_second[:, at])[0:SUBLANES]

        def fields(i):
            at = pl.ds(i * width, width)
            r = start + i
            here = state[r]
            below = jnp.where(r > 0, state[jnp.maximum(r - 1, 0)], south)
            above = jnp.where(r < rows - 1, state[jnp.minimum(r + 1, rows - 1)], north)
            lap = laplace_row(here, below, above, west, east, r, lane)
            wet = jnp.broadcast_to(mask[pl.ds(r, 1), :].astype(f32), shape)
            spread_mask = jnp.where(comp == 1, wet, 1.0)
            wet_flux = (flux[:, at] + b_third) * wet
            updated = here + rate * spread_mask * lap
            for f in range(fluxes):
                updated = updated + couple[f] * jnp.broadcast_to(wet_flux[f : f + 1], shape)
            new_out[pl.ds(r, SUBLANES, stride=rows), :] = updated
            misfit = updated - goal[pl.ds(r, SUBLANES, stride=rows), :]
            diffuse = spread_mask * misfit
            diffuse_out[r] = diffuse
            edges[0], edges[1] = take_edges(diffuse, r, lane, (edges[0], edges[1]))
            misfits[r] = misfit
            pulled = jnp.zeros(shape, f32)
            for f in range(fluxes):
                total = jnp.sum(couple[f] * misfit, axis=0, keepdims=True)
                pulled = jnp.where(sub == f, jnp.broadcast_to(total, shape), pulled)
            pulled = (pulled * wet).astype(bf16)
            flux_cot[0:SUBLANES, at] = pulled
            g_bias[...] = g_bias[...] + pulled.astype(f32)

        return (
            spread(*KEYS["take"], take, BLOCK_ROWS)
            + spread(*KEYS["first"], first, chunks)
            + spread(*KEYS["second"], second, chunks)
            + spread(*KEYS["third"], third, chunks)
            + spread(*KEYS["fields"], fields, BLOCK_ROWS)
        )

    def backward(block, feat, hid_first, hid_second, slope_first, slope_second, flux_cot):
        start = block * BLOCK_ROWS

        def second(j):
            at = pl.ds(j * CHUNK, CHUNK)
            net = dot(w_third_back[...], flux_cot[:, at])
            cot_second[:, at] = (net * slope_second[:, at]).astype(bf16)

        def first(j):
            at = pl.ds(j * CHUNK, CHUNK)
            net = dot(w_second_back[...], cot_second[:, at])
            cot_first[:, at] = (net * slope_first[:, at]).astype(bf16)

        def inputs(j):
            at = pl.ds(j * CHUNK, CHUNK)
            feat_cot[:, at] = dot(w_first_back[...], cot_first[:, at])

        def leave(i):
            at = pl.ds(i * width, width)
            r = start + i
            base_out[r] = misfits[r] + feat_cot[0:SUBLANES, at]
            other[r] = feat_cot[SUBLANES : 2 * SUBLANES, at]

        def grad_second():
            g_second[...] += dot_nt(hid_first[...], cot_second[...])

        def grad_third():
            g_third[...] += dot_nt(flux_cot[...], hid_second[...])

        def grad_first():
            g_first[...] += dot_nt(feat[...], cot_first[...])

        return (
            spread(*KEYS["cot_second"], second, chunks)
            + spread(*KEYS["cot_first"], first, chunks)
            + spread(*KEYS["cot_inputs"], inputs, chunks)
            + spread(*KEYS["leave"], leave, BLOCK_ROWS)
            + [
                (KEYS["grad_second"], grad_second),
                (KEYS["grad_third"], grad_third),
                (KEYS["grad_first"], grad_first),
            ]
        )

    sets = list(
        zip(feats, hid_firsts, hid_seconds, slope_firsts, slope_seconds, flux_cots, strict=True)
    )
    blocks = rows // BLOCK_ROWS

    def beside(block, this, that):
        weave(backward(block, *this), forward(block + 1, *that))

    def pair_step(pair, unused):
        beside(2 * pair, *sets)
        beside(2 * pair + 1, *sets[::-1])
        return unused

    weave(forward(0, *sets[0]))
    lax.fori_loop(0, blocks // 2 - 1, pair_step, 0)
    beside(blocks - 2, *sets)
    ready = rows - BLOCK_ROWS
    stores = [
        pltpu.make_async_copy(new_out, new_hbm, sems.at[3]),
        pltpu.make_async_copy(diffuse_out, diffuse_hbm, sems.at[4]),
        pltpu.make_async_copy(
            base_out.at[pl.ds(0, ready)], base_hbm.at[pl.ds(0, ready)], sems.at[5]
        ),
    ]
    for store in stores:
        store.start()
    weave(backward(blocks - 1, *sets[1]))
    rest = pltpu.make_async_copy(
        base_out.at[pl.ds(ready, BLOCK_ROWS)], base_hbm.at[pl.ds(ready, BLOCK_ROWS)], sems.at[6]
    )
    rest.start()
    stage[pl.ds(meta[OWN], peers), 0:slot_rows, :] = jnp.zeros((peers, slot_rows, width), f32)

    def leave(p, unused):
        for s in range(slots):
            row = landing[s, p]
            stage[meta[OTHER] + p, s * SUBLANES : (s + 1) * SUBLANES, :] = other[row]
        return unused

    lax.fori_loop(0, peers, leave, 0, unroll=2)
    put_edges(meta, edges[0], edges[1], diffuse_out[0], diffuse_out[rows - 1], stage)
    devices = stage.shape[0]
    halves = hidden // width
    inputs = 2 * SUBLANES
    small[...] = jnp.zeros(small.shape, f32)
    low, high = g_first[0:SUBLANES, :], g_first[SUBLANES:inputs, :]
    low, high = jnp.where(comp == 1, high, low), jnp.where(comp == 1, low, high)
    bias_sum = jnp.sum(g_bias[...], axis=1, keepdims=True)
    bias_row = jnp.sum(jnp.where(sub == lane, jnp.broadcast_to(bias_sum, shape), 0.0), axis=0,
                       keepdims=True)
    for h in range(halves):
        cols = slice(h * width, (h + 1) * width)
        top = h * 24
        small[top : top + 8, :] = low[:, cols]
        small[top + 8 : top + 16, :] = high[:, cols]
        small[top + 16 : top + 17, :] = g_first[inputs : inputs + 1, cols]
        small[top + 17 : top + 18, :] = g_second[hidden : hidden + 1, cols]
        if h == 0:
            small[top + 18 : top + 19, :] = bias_row
        small[top + 19 : top + 19 + fluxes, :] = g_third[0:fluxes, cols]
    for d in range(devices):
        done = 0
        while done < share:
            at = d * share + done
            h, row = divmod(at, hidden)
            step = min(share - done, hidden - row)
            if h < halves:
                stage[d, slot_rows + done : slot_rows + done + step, :] = g_second[
                    row : row + step, h * width : (h + 1) * width
                ]
            done += step
        piece = small[d * small_share : (d + 1) * small_share, :]
        head = piece.astype(bf16).astype(f32)
        top = slot_rows + share
        stage[d, top : top + small_share, :] = head
        stage[d, top + small_share : top + 2 * small_share, :] = piece - head
    send_out[...] = stage[...].astype(bf16)
    for store in stores:
        store.wait()
    rest.wait()


def sum_kernel(scale, share, small_share, recv_in, out, recv, stage, sem):
    devices, packed = recv.shape[:2]
    fetch = pltpu.make_async_copy(
        recv_in.at[:, pl.ds(recv_in.shape[1] - packed, packed), :], recv, sem
    )
    fetch.start()
    fetch.wait()
    total = recv[0].astype(f32)
    for d in range(1, devices):
        total = total + recv[d].astype(f32)
    stage[...] = total * scale
    low = slice(share + small_share, share + 2 * small_share)
    piece = stage[share : share + small_share, :] + stage[low, :]
    head = piece.astype(bf16).astype(f32)
    stage[share : share + small_share, :] = head
    stage[low, :] = piece - head
    total = stage[...].astype(bf16)
    for d in range(devices):
        out[d] = total


def back_kernel(
    rows, peers, slots, source, count, recv_in, kernels, base, diffuse, rate_ref, out, total, recv,
    sem,
):
    meta = place()
    fetch = pltpu.make_async_copy(recv_in.at[:, pl.ds(0, recv.shape[1]), :], recv, sem)
    fetch.start()
    fetch.wait()
    width = diffuse.shape[2]
    shape = (SUBLANES, width)
    lane = lax.broadcasted_iota(jnp.int32, shape, 1)
    west, east, south, north = get_edges(meta, recv)
    comp = meta[COMP]
    rate = jnp.broadcast_to(column_of(rate_ref, comp), shape)

    def lap_step(r, unused):
        here = diffuse[r]
        below = jnp.where(r > 0, diffuse[jnp.maximum(r - 1, 0)], south)
        above = jnp.where(r < rows - 1, diffuse[jnp.minimum(r + 1, rows - 1)], north)
        total[r] = base[r] + rate * laplace_row(here, below, above, west, east, r, lane)
        return unused

    lax.fori_loop(0, rows, lap_step, 0, unroll=8)

    def peer_step(q, unused):
        block = recv[meta[OTHER] + q].astype(f32)
        for s in range(slots):
            k = q * slots + s
            sent = block[s * SUBLANES : (s + 1) * SUBLANES].astype(bf16)
            live = (s < count[q]).astype(f32)
            row = source[s, q]
            total[row] = total[row] + dot_nt(sent, kernels[k]) * live
        return unused

    lax.fori_loop(0, peers, peer_step, 0, unroll=4)

    def out_step(r, unused):
        out[pl.ds(r, SUBLANES, stride=rows), :] = total[r]
        return unused

    lax.fori_loop(0, rows, out_step, 0, unroll=8)


def unpack_kernel(share, small_share, fluxes, recv_in, first, bias_one, second, bias_two, third,
                  bias_three, recv, small, sem):
    fetch = pltpu.make_async_copy(recv_in, recv, sem)
    fetch.start()
    fetch.wait()
    devices = recv.shape[0]
    width = recv.shape[2]
    hidden = second.shape[0]
    halves = hidden // width
    for d in range(devices):
        block = recv[d].astype(f32)
        done = 0
        while done < share:
            at = d * share + done
            h, row = divmod(at, hidden)
            step = min(share - done, hidden - row)
            if h < halves:
                second[row : row + step, h * width : (h + 1) * width] = block[done : done + step]
            done += step
        small[d * small_share : (d + 1) * small_share, :] = (
            block[share : share + small_share]
            + block[share + small_share : share + 2 * small_share]
        )
    for h in range(halves):
        cols = slice(h * width, (h + 1) * width)
        top = h * 24
        first[:, cols] = small[top : top + 16, :]
        bias_one[:, cols] = small[top + 16 : top + 17, :]
        bias_two[:, cols] = small[top + 17 : top + 18, :]
        third[:, cols] = small[top + 19 : top + 19 + fluxes, :]
    bias_three[...] = small[18:19, 0:fluxes]


def shards(
    state,
    target,
    land_mask,
    diffusivity,
    coupling,
    w_in,
    b_in,
    w_mid,
    b_mid,
    w_out,
    b_out,
    remap_weight,
    remap_source,
    remap_target,
    remap_count,
):
    n_gy, n_gx = lax.axis_size("gy"), lax.axis_size("gx")
    tiles = n_gy * n_gx
    devices = 2 * tiles
    comp = lax.axis_index("comp")
    channels, rows, width = state.shape[1:]
    hidden = w_mid.shape[0]
    inputs = w_in.shape[0]
    fluxes = w_out.shape[1]
    peers, slots = remap_source.shape[3:]
    surface = state.reshape(channels * rows, width)
    goal = target.reshape(channels * rows, width)
    mask = land_mask[0]
    source = remap_source.reshape(peers, slots).T
    landing = remap_target.reshape(peers, slots).T
    count = remap_count.reshape(peers)
    kernels = remap_weight.reshape(peers * slots, width, width)
    slot_rows = slots * channels

    smem = pl.BlockSpec(memory_space=pltpu.SMEM)
    vmem = pl.BlockSpec(memory_space=pltpu.VMEM)

    anywhere = pl.BlockSpec(memory_space=pl.ANY)
    parts = math.gcd(peers, 4)
    outgoing, by_row = pl.pallas_call(
        functools.partial(send_kernel, rows, peers, slots),
        name="send",
        out_shape=(
            jax.ShapeDtypeStruct((devices, slot_rows, width), bf16),
            jax.ShapeDtypeStruct((rows, channels, width), f32),
        ),
        in_specs=[smem, smem, vmem, anywhere],
        out_specs=(vmem, vmem),
        scratch_shapes=[
            pltpu.VMEM((devices, slot_rows, width), f32),
            pltpu.VMEM(kernels.shape, bf16),
            pltpu.SemaphoreType.DMA((parts,)),
        ],
    )(source, count, surface, kernels)
    arrived = lax.all_to_all(outgoing, EVERYWHERE, 0, 0, tiled=True)

    def pieces(bias):
        high = bias.astype(bf16)
        rest = bias - high.astype(f32)
        middle = rest.astype(bf16)
        low = (rest - middle.astype(f32)).astype(bf16)
        return jnp.stack([high, middle, low], axis=0)

    local_in = jnp.where(comp == 1, jnp.roll(w_in, channels, axis=0), w_in)
    half = jnp.asarray(0.5, bf16)
    w_first = jnp.concatenate(
        [local_in, pieces(b_in), jnp.zeros((13, hidden), bf16)], axis=0
    ).T * half
    w_second = w_mid.T * half
    b_second = (b_mid * 0.5)[:, None]
    w_third = jnp.pad(w_out.T, ((0, 16 - fluxes), (0, 0)))
    w_third_back = jnp.pad(w_out * half, ((0, 0), (0, 16 - fluxes)))
    w_second_back = w_mid * half
    w_first_back = local_in

    share = -(-hidden * hidden // (width * devices))
    small_share = -(-24 * hidden // (width * devices))
    packed = -(-(share + 2 * small_share) // 8) * 8
    cells = BLOCK_ROWS * width

    def twice(*args):
        return (pltpu.VMEM(*args), pltpu.VMEM(*args))

    tall = (rows, channels, width)
    new_state, base, diffuse, leaving = pl.pallas_call(
        functools.partial(main_kernel, rows, peers, slots, share, small_share),
        name="main",
        out_shape=(
            jax.ShapeDtypeStruct((channels * rows, width), f32),
            jax.ShapeDtypeStruct(tall, f32),
            jax.ShapeDtypeStruct((rows, channels, width), f32),
            jax.ShapeDtypeStruct((devices, slot_rows + packed, width), bf16),
        ),
        in_specs=[smem, smem, anywhere, anywhere, vmem, anywhere] + [vmem] * 9,
        out_specs=(anywhere,) * 3 + (vmem,),
        scratch_shapes=[
            pltpu.VMEM((rows, channels, width), f32),
            pltpu.VMEM((channels * rows, width), f32),
            pltpu.VMEM((devices, slot_rows, width), bf16),
            pltpu.VMEM((channels * rows, width), f32),
            pltpu.VMEM(tall, f32),
            pltpu.VMEM((rows, channels, width), f32),
            pltpu.SemaphoreType.DMA((7,)),
            pltpu.VMEM((devices, slot_rows + packed, width), f32),
            pltpu.VMEM(tall, f32),
            pltpu.VMEM(tall, f32),
            twice((32, cells), bf16),
            twice((hidden + 16, cells), bf16),
            twice((hidden, cells), bf16),
            twice((hidden, cells), f32),
            twice((hidden, cells), f32),
            twice((16, cells), bf16),
            pltpu.VMEM((hidden, cells), bf16),
            pltpu.VMEM((hidden, cells), bf16),
            pltpu.VMEM((8, cells), f32),
            pltpu.VMEM((16, cells), f32),
            pltpu.VMEM((32, hidden), f32),
            pltpu.VMEM((hidden + 16, hidden), f32),
            pltpu.VMEM((16, hidden), f32),
            pltpu.VMEM((8, width), f32),
            pltpu.VMEM((2, 8, width), f32),
            pltpu.VMEM((max(48, small_share * devices), width), f32),
        ],
    )(
        landing,
        b_out,
        by_row,
        goal,
        mask,
        arrived,
        diffusivity,
        coupling,
        w_first,
        w_second,
        b_second,
        w_third,
        w_third_back,
        w_second_back,
        w_first_back,
    )
    returned = lax.all_to_all(leaving, EVERYWHERE, 0, 0, tiled=True)
    scale = 1.0 / (rows * width * tiles)
    summed = pl.pallas_call(
        functools.partial(sum_kernel, scale, share, small_share),
        name="sum",
        out_shape=jax.ShapeDtypeStruct((devices, packed, width), bf16),
        in_specs=[anywhere],
        out_specs=vmem,
        scratch_shapes=[
            pltpu.VMEM((devices, packed, width), bf16),
            pltpu.VMEM((packed, width), f32),
            pltpu.SemaphoreType.DMA,
        ],
    )(returned)
    gathered = lax.all_to_all(summed, EVERYWHERE, 0, 0, tiled=True)
    adjoint = pl.pallas_call(
        functools.partial(back_kernel, rows, peers, slots),
        name="back",
        out_shape=jax.ShapeDtypeStruct((channels * rows, width), f32),
        in_specs=[smem, smem, anywhere] + [vmem] * 4,
        out_specs=vmem,
        scratch_shapes=[
            pltpu.VMEM((rows, channels, width), f32),
            pltpu.VMEM((devices, slot_rows, width), bf16),
            pltpu.SemaphoreType.DMA,
        ],
    )(source, count, returned, kernels, base, diffuse, diffusivity)
    first, bias_one, second, bias_two, third, bias_three = pl.pallas_call(
        functools.partial(unpack_kernel, share, small_share, fluxes),
        name="unpack",
        out_shape=(
            jax.ShapeDtypeStruct((inputs, hidden), f32),
            jax.ShapeDtypeStruct((1, hidden), f32),
            jax.ShapeDtypeStruct((hidden, hidden), f32),
            jax.ShapeDtypeStruct((1, hidden), f32),
            jax.ShapeDtypeStruct((fluxes, hidden), f32),
            jax.ShapeDtypeStruct((1, fluxes), f32),
        ),
        in_specs=[anywhere],
        out_specs=(vmem,) * 6,
        scratch_shapes=[
            pltpu.VMEM((devices, packed, width), bf16),
            pltpu.VMEM((max(48, small_share * devices), width), f32),
            pltpu.SemaphoreType.DMA,
        ],
    )(gathered)
    return (
        new_state.reshape(state.shape),
        adjoint.reshape(state.shape),
        first,
        bias_one[0],
        second,
        bias_two[0],
        third.T,
        bias_three[0],
    )


def solution(mesh):
    tiles = P("comp", None, "gy", "gx")
    placed = (
        tiles,
        tiles,
        P("comp", "gy", "gx"),
        *(P() for _ in range(8)),
        P("comp", "gy", "gx", None, None, None, None),
        P("comp", "gy", "gx", None, None),
        P("comp", "gy", "gx", None, None),
        P("comp", "gy", "gx", None),
    )
    return jax.shard_map(
        shards,
        mesh=mesh,
        in_specs=placed,
        out_specs=(tiles, tiles, *(P() for _ in range(6))),
        check_vma=False,
    )
```

```python
import functools
import math

import jax
import jax.numpy as jnp
from jax import lax
from jax.experimental import pallas as pl
from jax.experimental.pallas import tpu as pltpu
from jax.sharding import PartitionSpec as P

EVERYWHERE = ("comp", "gy", "gx")
BLOCK_ROWS = 8
CHUNK = 256
SUBLANES = 8

KEYS = {
    "take": (0.0, 0.05),
    "first": (0.05, 0.3),
    "second": (0.3, 0.6),
    "third": (0.6, 0.65),
    "fields": (0.65, 1.0),
    "cot_second": (0.05, 0.3),
    "cot_first": (0.3, 0.6),
    "cot_inputs": (0.62, 0.7),
    "leave": (0.9, 1.0),
    "grad_second": 0.61,
    "grad_third": 0.605,
    "grad_first": 0.71,
}

OWN, OTHER, WEST, EAST, SOUTH, NORTH, COMP, HAS_SOUTH, HAS_NORTH, ON_FOLD = range(10)

f32 = jnp.float32
bf16 = jnp.bfloat16


def side_by_side(ref, first, count, low, high):
    return jnp.concatenate([ref[first + i, low:high, :] for i in range(count)], axis=1)


def place():
    n_gy, n_gx = lax.axis_size("gy"), lax.axis_size("gx")
    comp, row, col = (lax.axis_index(axis) for axis in EVERYWHERE)
    tiles = n_gy * n_gx
    own = comp * tiles
    line = own + row * n_gx
    here = line + col
    is_top = row == n_gy - 1
    on_fold = jnp.logical_and(comp == 1, is_top)
    up = jnp.where(is_top, here, here + n_gx)
    return (
        own,
        (1 - comp) * tiles,
        line + lax.rem(col + (n_gx - 1), n_gx),
        line + lax.rem(col + 1, n_gx),
        jnp.where(row > 0, here - n_gx, here),
        jnp.where(on_fold, line + (n_gx - 1) - col, up),
        comp,
        (row > 0).astype(jnp.int32),
        jnp.logical_or(on_fold, jnp.logical_not(is_top)).astype(jnp.int32),
        on_fold.astype(jnp.int32),
    )


def dot(a, b):
    return jnp.dot(a, b, preferred_element_type=f32)


def dot_nt(a, b):
    return lax.dot_general(a, b, (((1,), (1,)), ((), ())), preferred_element_type=f32)


def mirror(tile):
    width = tile.shape[1]
    row = lax.broadcasted_iota(jnp.int32, (width, width), 0)
    col = lax.broadcasted_iota(jnp.int32, (width, width), 1)
    flip = (row + col == width - 1).astype(f32).astype(bf16)
    return dot(tile.astype(bf16), flip)


def put_edges(meta, first, last, bottom, top, stage):
    stage[meta[EAST], 0:SUBLANES, :] = last
    stage[meta[WEST], SUBLANES : 2 * SUBLANES, :] = first
    top = jnp.where(meta[ON_FOLD] == 1, mirror(top), top)
    stage[meta[NORTH], 2 * SUBLANES : 3 * SUBLANES, :] = top
    stage[meta[SOUTH], 3 * SUBLANES : 4 * SUBLANES, :] = bottom


def take_edges(tile, r, lane, sides):
    width = tile.shape[1]
    here = lane == r
    first, last = sides
    first = jnp.where(here, pltpu.roll(tile, r, 1), first)
    last = jnp.where(here, pltpu.roll(tile, lax.rem(r + 1, width), 1), last)
    return first, last


def get_edges(meta, recv):
    west = recv[meta[WEST]].astype(f32)[0:SUBLANES]
    east = recv[meta[EAST]].astype(f32)[SUBLANES : 2 * SUBLANES]
    south = recv[meta[SOUTH]].astype(f32)[2 * SUBLANES : 3 * SUBLANES]
    above = recv[meta[NORTH]].astype(f32)
    north = jnp.where(
        meta[ON_FOLD] == 1,
        above[2 * SUBLANES : 3 * SUBLANES],
        above[3 * SUBLANES : 4 * SUBLANES],
    )
    south = jnp.where(meta[HAS_SOUTH] == 1, south, 0.0)
    north = jnp.where(meta[HAS_NORTH] == 1, north, 0.0)
    return west, east, south, north


def laplace_row(here, below, above, west, east, r, lane):
    width = here.shape[1]
    left = jnp.where(
        lane == 0, pltpu.roll(west, lax.rem(width - r, width), 1), pltpu.roll(here, 1, 1)
    )
    right = jnp.where(
        lane == width - 1, pltpu.roll(east, width - 1 - r, 1), pltpu.roll(here, width - 1, 1)
    )
    return left + right + below + above - 4.0 * here


def column_of(row, comp):
    eye = (
        lax.broadcasted_iota(jnp.int32, (SUBLANES, SUBLANES), 0)
        == lax.broadcasted_iota(jnp.int32, (SUBLANES, SUBLANES), 1)
    ).astype(f32)
    return jnp.sum(
        jnp.broadcast_to(row[pl.ds(comp, 1), :], (SUBLANES, SUBLANES)) * eye,
        axis=1,
        keepdims=True,
    )


def send_kernel(
    rows, peers, slots, source, count, state, kernels, out, by_row, stage, blocks, sems
):
    meta = place()
    width = state.shape[1]
    shape = (SUBLANES, width)
    lane = lax.broadcasted_iota(jnp.int32, shape, 1)
    parts = sems.shape[0]
    part = peers // parts
    copies = [
        pltpu.make_async_copy(
            kernels.at[pl.ds(i * part * slots, part * slots)],
            blocks.at[pl.ds(i * part * slots, part * slots)],
            sems.at[i],
        )
        for i in range(parts)
    ]
    for copy in copies:
        copy.start()
    stage[pl.ds(meta[OWN], peers)] = jnp.zeros((peers,) + stage.shape[1:], f32)

    def row_step(r, sides):
        tile = state[pl.ds(r, SUBLANES, stride=rows), :]
        by_row[r] = tile
        return take_edges(tile, r, lane, sides)

    zero = jnp.zeros(shape, f32)
    first, last = lax.fori_loop(0, rows, row_step, (zero, zero), unroll=32)
    put_edges(meta, first, last, by_row[0], by_row[rows - 1], stage)

    def peer_step(q, unused):
        for s in range(slots):
            k = q * slots + s
            picked = by_row[source[s, q]].astype(bf16)
            live = (s < count[q]).astype(f32)
            stage[meta[OTHER] + q, s * SUBLANES : (s + 1) * SUBLANES, :] = (
                dot(picked, blocks[k]) * live
            )
        return unused

    for i in range(parts):
        copies[i].wait()
        lax.fori_loop(i * part, (i + 1) * part, peer_step, 0, unroll=math.gcd(part, 4))
    out[...] = stage[...].astype(bf16)


def spread(low, high, step, count):
    return [
        (low + (high - low) * (i + 0.5) / count, functools.partial(step, i)) for i in range(count)
    ]


def weave(*lists):
    for entry in sorted((e for steps in lists for e in steps), key=lambda e: e[0]):
        entry[1]()


def main_kernel(
    rows,
    peers,
    slots,
    share,
    small_share,
    landing,
    b_out,
    state_in,
    goal_in,
    mask,
    recv_in,
    rate_ref,
    couple_ref,
    w_first,
    w_second,
    b_second,
    w_third,
    w_third_back,
    w_second_back,
    w_first_back,
    new_hbm,
    base_hbm,
    diffuse_hbm,
    send_out,
    state,
    goal,
    recv,
    new_out,
    base_out,
    diffuse_out,
    sems,
    stage,
    other,
    misfits,
    feats,
    hid_firsts,
    hid_seconds,
    slope_firsts,
    slope_seconds,
    flux_cots,
    cot_second,
    cot_first,
    flux,
    feat_cot,
    g_first,
    g_second,
    g_third,
    g_bias,
    edges,
    small,
):
    width = state.shape[2]
    hidden = w_second.shape[0]
    shape = (SUBLANES, width)
    cells = BLOCK_ROWS * width
    chunks = cells // CHUNK
    lane = lax.broadcasted_iota(jnp.int32, shape, 1)
    sub = lax.broadcasted_iota(jnp.int32, shape, 0)
    fluxes = couple_ref.shape[2]
    meta = place()
    slot_rows = recv.shape[1]
    fetches = [
        pltpu.make_async_copy(recv_in, recv, sems.at[0]),
        pltpu.make_async_copy(state_in, state, sems.at[1]),
        pltpu.make_async_copy(goal_in, goal, sems.at[2]),
    ]
    for fetch in fetches:
        fetch.start()

    other[...] = jnp.zeros(other.shape, f32)

    fetches[0].wait()

    def land(p, unused):
        block = recv[meta[OTHER] + p].astype(f32)
        for s in range(slots):
            row = landing[s, p]
            other[row] = other[row] + block[s * SUBLANES : (s + 1) * SUBLANES]
        return unused

    lax.fori_loop(0, peers, land, 0, unroll=2)
    west, east, south, north = get_edges(meta, recv)
    comp = meta[COMP]
    rate = jnp.broadcast_to(column_of(rate_ref, comp), shape)
    pairs = couple_ref[comp]
    couple = [jnp.broadcast_to(pairs[:, f : f + 1], shape) for f in range(fluxes)]
    ones = (lax.broadcasted_iota(jnp.int32, (16, width), 0) < 3).astype(f32).astype(bf16)
    lanes = CHUNK // width
    for ref in flux_cots:
        ref[...] = jnp.zeros(ref.shape, bf16)
    for ref in feats:
        for i in range(BLOCK_ROWS):
            ref[i, 16:32, :] = ones
    for ref in hid_firsts:
        for i in range(BLOCK_ROWS):
            ref[i, hidden : hidden + 16, :] = ones
    for ref in (g_first, g_second, g_third, g_bias, edges):
        ref[...] = jnp.zeros(ref.shape, f32)
    bias = jnp.broadcast_to(b_second[...], (hidden, CHUNK))
    fetches[1].wait()
    fetches[2].wait()
    b_third = jnp.zeros(shape, f32)
    for f in range(fluxes):
        b_third = jnp.where(sub == f, b_out[f], b_third)

    def forward(block, feat, hid_first, hid_second, slope_first, slope_second, flux_cot):
        start = block * BLOCK_ROWS

        def take(i):
            r = start + i
            feat[i, 0:16, :] = jnp.concatenate([state[r], other[r]], axis=0).astype(bf16)

        def layer(net, hid_ref, slope_ref, j):
            turn = jnp.tanh(net)
            up = 1.0 + turn
            hid = net * up
            slope = (up + hid) - hid * turn
            hid = hid.astype(bf16)
            for i in range(lanes):
                cols = slice(i * width, (i + 1) * width)
                hid_ref[j * lanes + i, 0:hidden, :] = hid[:, cols]
                slope_ref[j * lanes + i] = slope[:, cols]

        def first(j):
            net = dot(w_first[...], side_by_side(feat, j * lanes, lanes, 0, 32))
            layer(net, hid_first, slope_first, j)

        def second(j):
            net = dot(w_second[...], side_by_side(hid_first, j * lanes, lanes, 0, hidden)) + bias
            layer(net, hid_second, slope_second, j)

        def third(j):
            at = pl.ds(j * CHUNK, CHUNK)
            hid = side_by_side(hid_second, j * lanes, lanes, 0, hidden)
            flux[:, at] = dot(w_third[...], hid)[0:SUBLANES]

        def fields(i):
            at = pl.ds(i * width, width)
            r = start + i
            here = state[r]
            below = jnp.where(r > 0, state[jnp.maximum(r - 1, 0)], south)
            above = jnp.where(r < rows - 1, state[jnp.minimum(r + 1, rows - 1)], north)
            lap = laplace_row(here, below, above, west, east, r, lane)
            wet = jnp.broadcast_to(mask[pl.ds(r, 1), :].astype(f32), shape)
            spread_mask = jnp.where(comp == 1, wet, 1.0)
            wet_flux = (flux[:, at] + b_third) * wet
            updated = here + rate * spread_mask * lap
            for f in range(fluxes):
                updated = updated + couple[f] * jnp.broadcast_to(wet_flux[f : f + 1], shape)
            new_out[pl.ds(r, SUBLANES, stride=rows), :] = updated
            misfit = updated - goal[pl.ds(r, SUBLANES, stride=rows), :]
            diffuse = spread_mask * misfit
            diffuse_out[r] = diffuse
            edges[0], edges[1] = take_edges(diffuse, r, lane, (edges[0], edges[1]))
            misfits[r] = misfit
            pulled = jnp.zeros(shape, f32)
            for f in range(fluxes):
                total = jnp.sum(couple[f] * misfit, axis=0, keepdims=True)
                pulled = jnp.where(sub == f, jnp.broadcast_to(total, shape), pulled)
            pulled = (pulled * wet).astype(bf16)
            flux_cot[i, 0:SUBLANES, :] = pulled
            g_bias[...] = g_bias[...] + pulled.astype(f32)

        return (
            spread(*KEYS["take"], take, BLOCK_ROWS)
            + spread(*KEYS["first"], first, chunks)
            + spread(*KEYS["second"], second, chunks)
            + spread(*KEYS["third"], third, chunks)
            + spread(*KEYS["fields"], fields, BLOCK_ROWS)
        )

    def backward(block, feat, hid_first, hid_second, slope_first, slope_second, flux_cot):
        start = block * BLOCK_ROWS

        def pull(net, slope_ref, cot_ref, j):
            for i in range(lanes):
                cols = slice(i * width, (i + 1) * width)
                cot_ref[j * lanes + i] = (net[:, cols] * slope_ref[j * lanes + i]).astype(bf16)

        def second(j):
            net = dot(w_third_back[...], side_by_side(flux_cot, j * lanes, lanes, 0, 16))
            pull(net, slope_second, cot_second, j)

        def first(j):
            net = dot(w_second_back[...], side_by_side(cot_second, j * lanes, lanes, 0, hidden))
            pull(net, slope_first, cot_first, j)

        def inputs(j):
            at = pl.ds(j * CHUNK, CHUNK)
            cot = side_by_side(cot_first, j * lanes, lanes, 0, hidden)
            feat_cot[:, at] = dot(w_first_back[...], cot)

        def whole(ref):
            return side_by_side(ref, 0, BLOCK_ROWS, 0, ref.shape[1])

        def leave(i):
            at = pl.ds(i * width, width)
            r = start + i
            base_out[r] = misfits[r] + feat_cot[0:SUBLANES, at]
            other[r] = feat_cot[SUBLANES : 2 * SUBLANES, at]

        def grad_second():
            g_second[...] += dot_nt(whole(hid_first), whole(cot_second))

        def grad_third():
            g_third[...] += dot_nt(whole(flux_cot), whole(hid_second))

        def grad_first():
            g_first[...] += dot_nt(whole(feat), whole(cot_first))

        return (
            spread(*KEYS["cot_second"], second, chunks)
            + spread(*KEYS["cot_first"], first, chunks)
            + spread(*KEYS["cot_inputs"], inputs, chunks)
            + spread(*KEYS["leave"], leave, BLOCK_ROWS)
            + [
                (KEYS["grad_second"], grad_second),
                (KEYS["grad_third"], grad_third),
                (KEYS["grad_first"], grad_first),
            ]
        )

    sets = list(
        zip(feats, hid_firsts, hid_seconds, slope_firsts, slope_seconds, flux_cots, strict=True)
    )
    blocks = rows // BLOCK_ROWS

    def beside(block, this, that):
        weave(backward(block, *this), forward(block + 1, *that))

    def pair_step(pair, unused):
        beside(2 * pair, *sets)
        beside(2 * pair + 1, *sets[::-1])
        return unused

    weave(forward(0, *sets[0]))
    lax.fori_loop(0, blocks // 2 - 1, pair_step, 0)
    beside(blocks - 2, *sets)
    ready = rows - BLOCK_ROWS
    stores = [
        pltpu.make_async_copy(new_out, new_hbm, sems.at[3]),
        pltpu.make_async_copy(diffuse_out, diffuse_hbm, sems.at[4]),
        pltpu.make_async_copy(
            base_out.at[pl.ds(0, ready)], base_hbm.at[pl.ds(0, ready)], sems.at[5]
        ),
    ]
    for store in stores:
        store.start()
    weave(backward(blocks - 1, *sets[1]))
    rest = pltpu.make_async_copy(
        base_out.at[pl.ds(ready, BLOCK_ROWS)], base_hbm.at[pl.ds(ready, BLOCK_ROWS)], sems.at[6]
    )
    rest.start()
    stage[pl.ds(meta[OWN], peers), 0:slot_rows, :] = jnp.zeros((peers, slot_rows, width), f32)

    def leave(p, unused):
        for s in range(slots):
            row = landing[s, p]
            stage[meta[OTHER] + p, s * SUBLANES : (s + 1) * SUBLANES, :] = other[row]
        return unused

    lax.fori_loop(0, peers, leave, 0, unroll=2)
    put_edges(meta, edges[0], edges[1], diffuse_out[0], diffuse_out[rows - 1], stage)
    devices = stage.shape[0]
    halves = hidden // width
    inputs = 2 * SUBLANES
    small[...] = jnp.zeros(small.shape, f32)
    low, high = g_first[0:SUBLANES, :], g_first[SUBLANES:inputs, :]
    low, high = jnp.where(comp == 1, high, low), jnp.where(comp == 1, low, high)
    bias_sum = jnp.sum(g_bias[...], axis=1, keepdims=True)
    bias_row = jnp.sum(jnp.where(sub == lane, jnp.broadcast_to(bias_sum, shape), 0.0), axis=0,
                       keepdims=True)
    for h in range(halves):
        cols = slice(h * width, (h + 1) * width)
        top = h * 24
        small[top : top + 8, :] = low[:, cols]
        small[top + 8 : top + 16, :] = high[:, cols]
        small[top + 16 : top + 17, :] = g_first[inputs : inputs + 1, cols]
        small[top + 17 : top + 18, :] = g_second[hidden : hidden + 1, cols]
        if h == 0:
            small[top + 18 : top + 19, :] = bias_row
        small[top + 19 : top + 19 + fluxes, :] = g_third[0:fluxes, cols]
    for d in range(devices):
        done = 0
        while done < share:
            at = d * share + done
            h, row = divmod(at, hidden)
            step = min(share - done, hidden - row)
            if h < halves:
                stage[d, slot_rows + done : slot_rows + done + step, :] = g_second[
                    row : row + step, h * width : (h + 1) * width
                ]
            done += step
        piece = small[d * small_share : (d + 1) * small_share, :]
        head = piece.astype(bf16).astype(f32)
        top = slot_rows + share
        stage[d, top : top + small_share, :] = head
        stage[d, top + small_share : top + 2 * small_share, :] = piece - head
    send_out[...] = stage[...].astype(bf16)
    for store in stores:
        store.wait()
    rest.wait()


def sum_kernel(scale, share, small_share, recv_in, out, recv, stage, sem):
    devices, packed = recv.shape[:2]
    fetch = pltpu.make_async_copy(
        recv_in.at[:, pl.ds(recv_in.shape[1] - packed, packed), :], recv, sem
    )
    fetch.start()
    fetch.wait()
    total = recv[0].astype(f32)
    for d in range(1, devices):
        total = total + recv[d].astype(f32)
    stage[...] = total * scale
    low = slice(share + small_share, share + 2 * small_share)
    piece = stage[share : share + small_share, :] + stage[low, :]
    head = piece.astype(bf16).astype(f32)
    stage[share : share + small_share, :] = head
    stage[low, :] = piece - head
    total = stage[...].astype(bf16)
    for d in range(devices):
        out[d] = total


def back_kernel(
    rows, peers, slots, source, count, recv_in, kernels, base, diffuse, rate_ref, out, total, recv,
    sem,
):
    meta = place()
    fetch = pltpu.make_async_copy(recv_in.at[:, pl.ds(0, recv.shape[1]), :], recv, sem)
    fetch.start()
    fetch.wait()
    width = diffuse.shape[2]
    shape = (SUBLANES, width)
    lane = lax.broadcasted_iota(jnp.int32, shape, 1)
    west, east, south, north = get_edges(meta, recv)
    comp = meta[COMP]
    rate = jnp.broadcast_to(column_of(rate_ref, comp), shape)

    def lap_step(r, unused):
        here = diffuse[r]
        below = jnp.where(r > 0, diffuse[jnp.maximum(r - 1, 0)], south)
        above = jnp.where(r < rows - 1, diffuse[jnp.minimum(r + 1, rows - 1)], north)
        total[r] = base[r] + rate * laplace_row(here, below, above, west, east, r, lane)
        return unused

    lax.fori_loop(0, rows, lap_step, 0, unroll=8)

    def peer_step(q, unused):
        block = recv[meta[OTHER] + q].astype(f32)
        for s in range(slots):
            k = q * slots + s
            sent = block[s * SUBLANES : (s + 1) * SUBLANES].astype(bf16)
            live = (s < count[q]).astype(f32)
            row = source[s, q]
            total[row] = total[row] + dot_nt(sent, kernels[k]) * live
        return unused

    lax.fori_loop(0, peers, peer_step, 0, unroll=4)

    def out_step(r, unused):
        out[pl.ds(r, SUBLANES, stride=rows), :] = total[r]
        return unused

    lax.fori_loop(0, rows, out_step, 0, unroll=8)


def unpack_kernel(share, small_share, fluxes, recv_in, first, bias_one, second, bias_two, third,
                  bias_three, recv, small, sem):
    fetch = pltpu.make_async_copy(recv_in, recv, sem)
    fetch.start()
    fetch.wait()
    devices = recv.shape[0]
    width = recv.shape[2]
    hidden = second.shape[0]
    halves = hidden // width
    for d in range(devices):
        block = recv[d].astype(f32)
        done = 0
        while done < share:
            at = d * share + done
            h, row = divmod(at, hidden)
            step = min(share - done, hidden - row)
            if h < halves:
                second[row : row + step, h * width : (h + 1) * width] = block[done : done + step]
            done += step
        small[d * small_share : (d + 1) * small_share, :] = (
            block[share : share + small_share]
            + block[share + small_share : share + 2 * small_share]
        )
    for h in range(halves):
        cols = slice(h * width, (h + 1) * width)
        top = h * 24
        first[:, cols] = small[top : top + 16, :]
        bias_one[:, cols] = small[top + 16 : top + 17, :]
        bias_two[:, cols] = small[top + 17 : top + 18, :]
        third[:, cols] = small[top + 19 : top + 19 + fluxes, :]
    bias_three[...] = small[18:19, 0:fluxes]


def shards(
    state,
    target,
    land_mask,
    diffusivity,
    coupling,
    w_in,
    b_in,
    w_mid,
    b_mid,
    w_out,
    b_out,
    remap_weight,
    remap_source,
    remap_target,
    remap_count,
):
    n_gy, n_gx = lax.axis_size("gy"), lax.axis_size("gx")
    tiles = n_gy * n_gx
    devices = 2 * tiles
    comp = lax.axis_index("comp")
    channels, rows, width = state.shape[1:]
    hidden = w_mid.shape[0]
    inputs = w_in.shape[0]
    fluxes = w_out.shape[1]
    peers, slots = remap_source.shape[3:]
    surface = state.reshape(channels * rows, width)
    goal = target.reshape(channels * rows, width)
    mask = land_mask[0]
    source = remap_source.reshape(peers, slots).T
    landing = remap_target.reshape(peers, slots).T
    count = remap_count.reshape(peers)
    kernels = remap_weight.reshape(peers * slots, width, width)
    slot_rows = slots * channels

    smem = pl.BlockSpec(memory_space=pltpu.SMEM)
    vmem = pl.BlockSpec(memory_space=pltpu.VMEM)

    anywhere = pl.BlockSpec(memory_space=pl.ANY)
    parts = math.gcd(peers, 4)
    outgoing, by_row = pl.pallas_call(
        functools.partial(send_kernel, rows, peers, slots),
        name="send",
        out_shape=(
            jax.ShapeDtypeStruct((devices, slot_rows, width), bf16),
            jax.ShapeDtypeStruct((rows, channels, width), f32),
        ),
        in_specs=[smem, smem, vmem, anywhere],
        out_specs=(vmem, vmem),
        scratch_shapes=[
            pltpu.VMEM((devices, slot_rows, width), f32),
            pltpu.VMEM(kernels.shape, bf16),
            pltpu.SemaphoreType.DMA((parts,)),
        ],
    )(source, count, surface, kernels)
    arrived = lax.all_to_all(outgoing, EVERYWHERE, 0, 0, tiled=True)

    def pieces(bias):
        high = bias.astype(bf16)
        rest = bias - high.astype(f32)
        middle = rest.astype(bf16)
        low = (rest - middle.astype(f32)).astype(bf16)
        return jnp.stack([high, middle, low], axis=0)

    local_in = jnp.where(comp == 1, jnp.roll(w_in, channels, axis=0), w_in)
    half = jnp.asarray(0.5, bf16)
    w_first = jnp.concatenate(
        [local_in, pieces(b_in), jnp.zeros((13, hidden), bf16)], axis=0
    ).T * half
    w_second = w_mid.T * half
    b_second = (b_mid * 0.5)[:, None]
    w_third = jnp.pad(w_out.T, ((0, 16 - fluxes), (0, 0)))
    w_third_back = jnp.pad(w_out * half, ((0, 0), (0, 16 - fluxes)))
    w_second_back = w_mid * half
    w_first_back = local_in

    share = -(-hidden * hidden // (width * devices))
    small_share = -(-24 * hidden // (width * devices))
    packed = -(-(share + 2 * small_share) // 8) * 8
    cells = BLOCK_ROWS * width

    def twice(*args):
        return (pltpu.VMEM(*args), pltpu.VMEM(*args))

    tall = (rows, channels, width)
    new_state, base, diffuse, leaving = pl.pallas_call(
        functools.partial(main_kernel, rows, peers, slots, share, small_share),
        name="main",
        out_shape=(
            jax.ShapeDtypeStruct((channels * rows, width), f32),
            jax.ShapeDtypeStruct(tall, f32),
            jax.ShapeDtypeStruct((rows, channels, width), f32),
            jax.ShapeDtypeStruct((devices, slot_rows + packed, width), bf16),
        ),
        in_specs=[smem, smem, anywhere, anywhere, vmem, anywhere] + [vmem] * 9,
        out_specs=(anywhere,) * 3 + (vmem,),
        scratch_shapes=[
            pltpu.VMEM((rows, channels, width), f32),
            pltpu.VMEM((channels * rows, width), f32),
            pltpu.VMEM((devices, slot_rows, width), bf16),
            pltpu.VMEM((channels * rows, width), f32),
            pltpu.VMEM(tall, f32),
            pltpu.VMEM((rows, channels, width), f32),
            pltpu.SemaphoreType.DMA((7,)),
            pltpu.VMEM((devices, slot_rows + packed, width), f32),
            pltpu.VMEM(tall, f32),
            pltpu.VMEM(tall, f32),
            twice((BLOCK_ROWS, 32, width), bf16),
            twice((BLOCK_ROWS, hidden + 16, width), bf16),
            twice((BLOCK_ROWS, hidden, width), bf16),
            twice((BLOCK_ROWS, hidden, width), f32),
            twice((BLOCK_ROWS, hidden, width), f32),
            twice((BLOCK_ROWS, 16, width), bf16),
            pltpu.VMEM((BLOCK_ROWS, hidden, width), bf16),
            pltpu.VMEM((BLOCK_ROWS, hidden, width), bf16),
            pltpu.VMEM((8, cells), f32),
            pltpu.VMEM((16, cells), f32),
            pltpu.VMEM((32, hidden), f32),
            pltpu.VMEM((hidden + 16, hidden), f32),
            pltpu.VMEM((16, hidden), f32),
            pltpu.VMEM((8, width), f32),
            pltpu.VMEM((2, 8, width), f32),
            pltpu.VMEM((max(48, small_share * devices), width), f32),
        ],
    )(
        landing,
        b_out,
        by_row,
        goal,
        mask,
        arrived,
        diffusivity,
        coupling,
        w_first,
        w_second,
        b_second,
        w_third,
        w_third_back,
        w_second_back,
        w_first_back,
    )
    returned = lax.all_to_all(leaving, EVERYWHERE, 0, 0, tiled=True)
    scale = 1.0 / (rows * width * tiles)
    summed = pl.pallas_call(
        functools.partial(sum_kernel, scale, share, small_share),
        name="sum",
        out_shape=jax.ShapeDtypeStruct((devices, packed, width), bf16),
        in_specs=[anywhere],
        out_specs=vmem,
        scratch_shapes=[
            pltpu.VMEM((devices, packed, width), bf16),
            pltpu.VMEM((packed, width), f32),
            pltpu.SemaphoreType.DMA,
        ],
    )(returned)
    gathered = lax.all_to_all(summed, EVERYWHERE, 0, 0, tiled=True)
    adjoint = pl.pallas_call(
        functools.partial(back_kernel, rows, peers, slots),
        name="back",
        out_shape=jax.ShapeDtypeStruct((channels * rows, width), f32),
        in_specs=[smem, smem, anywhere] + [vmem] * 4,
        out_specs=vmem,
        scratch_shapes=[
            pltpu.VMEM((rows, channels, width), f32),
            pltpu.VMEM((devices, slot_rows, width), bf16),
            pltpu.SemaphoreType.DMA,
        ],
    )(source, count, returned, kernels, base, diffuse, diffusivity)
    first, bias_one, second, bias_two, third, bias_three = pl.pallas_call(
        functools.partial(unpack_kernel, share, small_share, fluxes),
        name="unpack",
        out_shape=(
            jax.ShapeDtypeStruct((inputs, hidden), f32),
            jax.ShapeDtypeStruct((1, hidden), f32),
            jax.ShapeDtypeStruct((hidden, hidden), f32),
            jax.ShapeDtypeStruct((1, hidden), f32),
            jax.ShapeDtypeStruct((fluxes, hidden), f32),
            jax.ShapeDtypeStruct((1, fluxes), f32),
        ),
        in_specs=[anywhere],
        out_specs=(vmem,) * 6,
        scratch_shapes=[
            pltpu.VMEM((devices, packed, width), bf16),
            pltpu.VMEM((max(48, small_share * devices), width), f32),
            pltpu.SemaphoreType.DMA,
        ],
    )(gathered)
    return (
        new_state.reshape(state.shape),
        adjoint.reshape(state.shape),
        first,
        bias_one[0],
        second,
        bias_two[0],
        third.T,
        bias_three[0],
    )


def solution(mesh):
    tiles = P("comp", None, "gy", "gx")
    placed = (
        tiles,
        tiles,
        P("comp", "gy", "gx"),
        *(P() for _ in range(8)),
        P("comp", "gy", "gx", None, None, None, None),
        P("comp", "gy", "gx", None, None),
        P("comp", "gy", "gx", None, None),
        P("comp", "gy", "gx", None),
    )
    return jax.shard_map(
        shards,
        mesh=mesh,
        in_specs=placed,
        out_specs=(tiles, tiles, *(P() for _ in range(6))),
        check_vma=False,
    )
```

```python
import functools
import math

import jax
import jax.numpy as jnp
from jax import lax
from jax.experimental import pallas as pl
from jax.experimental.pallas import tpu as pltpu
from jax.sharding import PartitionSpec as P

EVERYWHERE = ("comp", "gy", "gx")
BLOCK_ROWS = 8
CHUNK = 256
FETCHED = 12
SUBLANES = 8

KEYS = {
    "take": (0.0, 0.05),
    "first": (0.05, 0.3),
    "second": (0.3, 0.6),
    "third": (0.6, 0.65),
    "fields": (0.65, 1.0),
    "cot_second": (0.05, 0.3),
    "cot_first": (0.3, 0.6),
    "cot_inputs": (0.62, 0.7),
    "leave": (0.9, 1.0),
    "grad_second": 0.61,
    "grad_third": 0.605,
    "grad_first": 0.71,
}

OWN, OTHER, WEST, EAST, SOUTH, NORTH, COMP, HAS_SOUTH, HAS_NORTH, ON_FOLD = range(10)

f32 = jnp.float32
bf16 = jnp.bfloat16


def fetch_all(pairs, sems):
    copies = [
        pltpu.make_async_copy(src, dst, sems.at[i])
        for i, (src, dst) in enumerate(pairs)
    ]
    for copy in copies:
        copy.start()
    return copies


def side_by_side(ref, first, count, low, high):
    return jnp.concatenate([ref[first + i, low:high, :] for i in range(count)], axis=1)


def place():
    n_gy, n_gx = lax.axis_size("gy"), lax.axis_size("gx")
    comp, row, col = (lax.axis_index(axis) for axis in EVERYWHERE)
    tiles = n_gy * n_gx
    own = comp * tiles
    line = own + row * n_gx
    here = line + col
    is_top = row == n_gy - 1
    on_fold = jnp.logical_and(comp == 1, is_top)
    up = jnp.where(is_top, here, here + n_gx)
    return (
        own,
        (1 - comp) * tiles,
        line + lax.rem(col + (n_gx - 1), n_gx),
        line + lax.rem(col + 1, n_gx),
        jnp.where(row > 0, here - n_gx, here),
        jnp.where(on_fold, line + (n_gx - 1) - col, up),
        comp,
        (row > 0).astype(jnp.int32),
        jnp.logical_or(on_fold, jnp.logical_not(is_top)).astype(jnp.int32),
        on_fold.astype(jnp.int32),
    )


def dot(a, b):
    return jnp.dot(a, b, preferred_element_type=f32)


def dot_nt(a, b):
    return lax.dot_general(a, b, (((1,), (1,)), ((), ())), preferred_element_type=f32)


def mirror(tile):
    width = tile.shape[1]
    row = lax.broadcasted_iota(jnp.int32, (width, width), 0)
    col = lax.broadcasted_iota(jnp.int32, (width, width), 1)
    flip = (row + col == width - 1).astype(f32).astype(bf16)
    return dot(tile.astype(bf16), flip)


def put_edges(meta, first, last, bottom, top, stage):
    stage[meta[EAST], 0:SUBLANES, :] = last
    stage[meta[WEST], SUBLANES : 2 * SUBLANES, :] = first
    top = jnp.where(meta[ON_FOLD] == 1, mirror(top), top)
    stage[meta[NORTH], 2 * SUBLANES : 3 * SUBLANES, :] = top
    stage[meta[SOUTH], 3 * SUBLANES : 4 * SUBLANES, :] = bottom


def take_edges(tile, r, lane, sides):
    width = tile.shape[1]
    here = lane == r
    first, last = sides
    first = jnp.where(here, pltpu.roll(tile, r, 1), first)
    last = jnp.where(here, pltpu.roll(tile, lax.rem(r + 1, width), 1), last)
    return first, last


def get_edges(meta, recv):
    west = recv[meta[WEST], 0 : 4 * SUBLANES, :].astype(f32)[0:SUBLANES]
    east = recv[meta[EAST], 0 : 4 * SUBLANES, :].astype(f32)[SUBLANES : 2 * SUBLANES]
    south = recv[meta[SOUTH], 0 : 4 * SUBLANES, :].astype(f32)[2 * SUBLANES : 3 * SUBLANES]
    above = recv[meta[NORTH], 0 : 4 * SUBLANES, :].astype(f32)
    north = jnp.where(
        meta[ON_FOLD] == 1,
        above[2 * SUBLANES : 3 * SUBLANES],
        above[3 * SUBLANES : 4 * SUBLANES],
    )
    south = jnp.where(meta[HAS_SOUTH] == 1, south, 0.0)
    north = jnp.where(meta[HAS_NORTH] == 1, north, 0.0)
    return west, east, south, north


def laplace_row(here, below, above, west, east, r, lane):
    width = here.shape[1]
    left = jnp.where(
        lane == 0, pltpu.roll(west, lax.rem(width - r, width), 1), pltpu.roll(here, 1, 1)
    )
    right = jnp.where(
        lane == width - 1, pltpu.roll(east, width - 1 - r, 1), pltpu.roll(here, width - 1, 1)
    )
    return left + right + below + above - 4.0 * here


def column_of(row, comp):
    eye = (
        lax.broadcasted_iota(jnp.int32, (SUBLANES, SUBLANES), 0)
        == lax.broadcasted_iota(jnp.int32, (SUBLANES, SUBLANES), 1)
    ).astype(f32)
    return jnp.sum(
        jnp.broadcast_to(row[pl.ds(comp, 1), :], (SUBLANES, SUBLANES)) * eye,
        axis=1,
        keepdims=True,
    )


def send_kernel(
    rows, peers, slots, source_in, count_in, state_in, kernels, out, by_row, stage, blocks, sems,
    source, count, state, small_sems,
):
    meta = place()
    small = fetch_all([(state_in, state), (source_in, source), (count_in, count)], small_sems)
    width = state.shape[1]
    shape = (SUBLANES, width)
    lane = lax.broadcasted_iota(jnp.int32, shape, 1)
    parts = sems.shape[0]
    part = peers // parts
    copies = [
        pltpu.make_async_copy(
            kernels.at[pl.ds(i * part * slots, part * slots)],
            blocks.at[pl.ds(i * part * slots, part * slots)],
            sems.at[i],
        )
        for i in range(parts)
    ]
    for copy in copies:
        copy.start()
    stage[pl.ds(meta[OWN], peers)] = jnp.zeros((peers,) + stage.shape[1:], f32)

    for copy in small:
        copy.wait()

    def row_step(r, sides):
        tile = state[pl.ds(r, SUBLANES, stride=rows), :]
        by_row[r] = tile
        return take_edges(tile, r, lane, sides)

    zero = jnp.zeros(shape, f32)
    first, last = lax.fori_loop(0, rows, row_step, (zero, zero), unroll=32)
    put_edges(meta, first, last, by_row[0], by_row[rows - 1], stage)

    def peer_step(q, unused):
        for s in range(slots):
            k = q * slots + s
            picked = by_row[source[s, q]].astype(bf16)
            live = (s < count[q]).astype(f32)
            stage[meta[OTHER] + q, s * SUBLANES : (s + 1) * SUBLANES, :] = (
                dot(picked, blocks[k]) * live
            )
        return unused

    for i in range(parts):
        copies[i].wait()
        lax.fori_loop(i * part, (i + 1) * part, peer_step, 0, unroll=math.gcd(part, 4))
    out[...] = stage[...].astype(bf16)


def spread(low, high, step, count):
    return [
        (low + (high - low) * (i + 0.5) / count, functools.partial(step, i)) for i in range(count)
    ]


def weave(*lists):
    for entry in sorted((e for steps in lists for e in steps), key=lambda e: e[0]):
        entry[1]()


def main_kernel(
    rows,
    peers,
    slots,
    share,
    small_share,
    state,
    goal,
    recv,
    *refs,
):
    fetched, refs = refs[:FETCHED], refs[FETCHED:]
    (new_hbm, base_hbm, diffuse_hbm, send_out), refs = refs[:4], refs[4:]
    kept, refs = refs[:FETCHED], refs[FETCHED:]
    fetch_sems, store_sems, new_out, base_out, diffuse_out = refs[:5]
    copies = fetch_all(list(zip(fetched, kept, strict=True)), fetch_sems)
    main_steps(
        rows,
        peers,
        slots,
        share,
        small_share,
        copies,
        state,
        goal,
        recv,
        *kept,
        new_hbm,
        base_hbm,
        diffuse_hbm,
        send_out,
        store_sems,
        new_out,
        base_out,
        diffuse_out,
        *refs[5:],
    )


def main_steps(
    rows,
    peers,
    slots,
    share,
    small_share,
    copies,
    state,
    goal,
    recv,
    landing,
    b_out,
    mask,
    rate_ref,
    couple_ref,
    w_first,
    w_second,
    b_second,
    w_third,
    w_third_back,
    w_second_back,
    w_first_back,
    new_hbm,
    base_hbm,
    diffuse_hbm,
    send_out,
    store_sems,
    new_out,
    base_out,
    diffuse_out,
    stage,
    other,
    misfits,
    feats,
    hid_firsts,
    hid_seconds,
    slope_firsts,
    slope_seconds,
    flux_cots,
    cot_second,
    cot_first,
    flux,
    feat_cot,
    g_first,
    g_second,
    g_third,
    g_bias,
    edges,
    small,
):
    width = state.shape[2]
    hidden = w_second.shape[0]
    shape = (SUBLANES, width)
    cells = BLOCK_ROWS * width
    chunks = cells // CHUNK
    lane = lax.broadcasted_iota(jnp.int32, shape, 1)
    sub = lax.broadcasted_iota(jnp.int32, shape, 0)
    fluxes = couple_ref.shape[2]
    meta = place()
    slot_rows = recv.shape[1]
    other[...] = jnp.zeros(other.shape, f32)
    for copy in copies:
        copy.wait()

    def land(p, unused):
        block = recv[meta[OTHER] + p].astype(f32)
        for s in range(slots):
            row = landing[s, p]
            other[row] = other[row] + block[s * SUBLANES : (s + 1) * SUBLANES]
        return unused

    lax.fori_loop(0, peers, land, 0, unroll=2)
    west, east, south, north = get_edges(meta, recv)
    comp = meta[COMP]
    rate = jnp.broadcast_to(column_of(rate_ref, comp), shape)
    pairs = couple_ref[comp]
    couple = [jnp.broadcast_to(pairs[:, f : f + 1], shape) for f in range(fluxes)]
    ones = (lax.broadcasted_iota(jnp.int32, (16, width), 0) < 3).astype(f32).astype(bf16)
    lanes = CHUNK // width
    for ref in flux_cots:
        ref[...] = jnp.zeros(ref.shape, bf16)
    for ref in feats:
        for i in range(BLOCK_ROWS):
            ref[i, 16:32, :] = ones
    for ref in hid_firsts:
        for i in range(BLOCK_ROWS):
            ref[i, hidden : hidden + 16, :] = ones
    for ref in (g_first, g_second, g_third, g_bias, edges):
        ref[...] = jnp.zeros(ref.shape, f32)
    bias = jnp.broadcast_to(b_second[...], (hidden, CHUNK))
    b_third = jnp.zeros(shape, f32)
    for f in range(fluxes):
        b_third = jnp.where(sub == f, b_out[f], b_third)

    def forward(block, feat, hid_first, hid_second, slope_first, slope_second, flux_cot):
        start = block * BLOCK_ROWS

        def take(i):
            r = start + i
            feat[i, 0:16, :] = jnp.concatenate([state[r], other[r]], axis=0).astype(bf16)

        def layer(net, hid_ref, slope_ref, j):
            turn = jnp.tanh(net)
            up = 1.0 + turn
            hid = net * up
            slope = (up + hid) - hid * turn
            hid = hid.astype(bf16)
            for i in range(lanes):
                cols = slice(i * width, (i + 1) * width)
                hid_ref[j * lanes + i, 0:hidden, :] = hid[:, cols]
                slope_ref[j * lanes + i] = slope[:, cols]

        def first(j):
            net = dot(w_first[...], side_by_side(feat, j * lanes, lanes, 0, 32))
            layer(net, hid_first, slope_first, j)

        def second(j):
            net = dot(w_second[...], side_by_side(hid_first, j * lanes, lanes, 0, hidden)) + bias
            layer(net, hid_second, slope_second, j)

        def third(j):
            at = pl.ds(j * CHUNK, CHUNK)
            hid = side_by_side(hid_second, j * lanes, lanes, 0, hidden)
            flux[:, at] = dot(w_third[...], hid)[0:SUBLANES]

        def fields(i):
            at = pl.ds(i * width, width)
            r = start + i
            here = state[r]
            below = jnp.where(r > 0, state[jnp.maximum(r - 1, 0)], south)
            above = jnp.where(r < rows - 1, state[jnp.minimum(r + 1, rows - 1)], north)
            lap = laplace_row(here, below, above, west, east, r, lane)
            wet = jnp.broadcast_to(mask[pl.ds(r, 1), :].astype(f32), shape)
            spread_mask = jnp.where(comp == 1, wet, 1.0)
            wet_flux = (flux[:, at] + b_third) * wet
            updated = here + rate * spread_mask * lap
            for f in range(fluxes):
                updated = updated + couple[f] * jnp.broadcast_to(wet_flux[f : f + 1], shape)
            new_out[pl.ds(r, SUBLANES, stride=rows), :] = updated
            misfit = updated - goal[pl.ds(r, SUBLANES, stride=rows), :]
            diffuse = spread_mask * misfit
            diffuse_out[r] = diffuse
            edges[0], edges[1] = take_edges(diffuse, r, lane, (edges[0], edges[1]))
            misfits[r] = misfit
            pulled = jnp.zeros(shape, f32)
            for f in range(fluxes):
                total = jnp.sum(couple[f] * misfit, axis=0, keepdims=True)
                pulled = jnp.where(sub == f, jnp.broadcast_to(total, shape), pulled)
            pulled = (pulled * wet).astype(bf16)
            flux_cot[i, 0:SUBLANES, :] = pulled
            g_bias[...] = g_bias[...] + pulled.astype(f32)

        return (
            spread(*KEYS["take"], take, BLOCK_ROWS)
            + spread(*KEYS["first"], first, chunks)
            + spread(*KEYS["second"], second, chunks)
            + spread(*KEYS["third"], third, chunks)
            + spread(*KEYS["fields"], fields, BLOCK_ROWS)
        )

    def backward(block, feat, hid_first, hid_second, slope_first, slope_second, flux_cot):
        start = block * BLOCK_ROWS

        def pull(net, slope_ref, cot_ref, j):
            for i in range(lanes):
                cols = slice(i * width, (i + 1) * width)
                cot_ref[j * lanes + i] = (net[:, cols] * slope_ref[j * lanes + i]).astype(bf16)

        def second(j):
            net = dot(w_third_back[...], side_by_side(flux_cot, j * lanes, lanes, 0, 16))
            pull(net, slope_second, cot_second, j)

        def first(j):
            net = dot(w_second_back[...], side_by_side(cot_second, j * lanes, lanes, 0, hidden))
            pull(net, slope_first, cot_first, j)

        def inputs(j):
            at = pl.ds(j * CHUNK, CHUNK)
            cot = side_by_side(cot_first, j * lanes, lanes, 0, hidden)
            feat_cot[:, at] = dot(w_first_back[...], cot)

        def whole(ref):
            return side_by_side(ref, 0, BLOCK_ROWS, 0, ref.shape[1])

        def leave(i):
            at = pl.ds(i * width, width)
            r = start + i
            base_out[r] = misfits[r] + feat_cot[0:SUBLANES, at]
            other[r] = feat_cot[SUBLANES : 2 * SUBLANES, at]

        def grad_second():
            g_second[...] += dot_nt(whole(hid_first), whole(cot_second))

        def grad_third():
            g_third[...] += dot_nt(whole(flux_cot), whole(hid_second))

        def grad_first():
            g_first[...] += dot_nt(whole(feat), whole(cot_first))

        return (
            spread(*KEYS["cot_second"], second, chunks)
            + spread(*KEYS["cot_first"], first, chunks)
            + spread(*KEYS["cot_inputs"], inputs, chunks)
            + spread(*KEYS["leave"], leave, BLOCK_ROWS)
            + [
                (KEYS["grad_second"], grad_second),
                (KEYS["grad_third"], grad_third),
                (KEYS["grad_first"], grad_first),
            ]
        )

    sets = list(
        zip(feats, hid_firsts, hid_seconds, slope_firsts, slope_seconds, flux_cots, strict=True)
    )
    blocks = rows // BLOCK_ROWS

    def beside(block, this, that):
        weave(backward(block, *this), forward(block + 1, *that))

    def pair_step(pair, unused):
        beside(2 * pair, *sets)
        beside(2 * pair + 1, *sets[::-1])
        return unused

    weave(forward(0, *sets[0]))
    lax.fori_loop(0, blocks // 2 - 1, pair_step, 0)
    beside(blocks - 2, *sets)
    ready = rows - BLOCK_ROWS
    stores = fetch_all(
        [
            (new_out, new_hbm),
            (diffuse_out, diffuse_hbm),
            (base_out.at[pl.ds(0, ready)], base_hbm.at[pl.ds(0, ready)]),
        ],
        store_sems,
    )
    weave(backward(blocks - 1, *sets[1]))
    rest = pltpu.make_async_copy(
        base_out.at[pl.ds(ready, BLOCK_ROWS)],
        base_hbm.at[pl.ds(ready, BLOCK_ROWS)],
        store_sems.at[3],
    )
    rest.start()
    stage[pl.ds(meta[OWN], peers), 0:slot_rows, :] = jnp.zeros((peers, slot_rows, width), f32)

    def leave(p, unused):
        for s in range(slots):
            row = landing[s, p]
            stage[meta[OTHER] + p, s * SUBLANES : (s + 1) * SUBLANES, :] = other[row]
        return unused

    lax.fori_loop(0, peers, leave, 0, unroll=2)
    put_edges(meta, edges[0], edges[1], diffuse_out[0], diffuse_out[rows - 1], stage)
    devices = stage.shape[0]
    halves = hidden // width
    inputs = 2 * SUBLANES
    small[...] = jnp.zeros(small.shape, f32)
    low, high = g_first[0:SUBLANES, :], g_first[SUBLANES:inputs, :]
    low, high = jnp.where(comp == 1, high, low), jnp.where(comp == 1, low, high)
    bias_sum = jnp.sum(g_bias[...], axis=1, keepdims=True)
    bias_row = jnp.sum(jnp.where(sub == lane, jnp.broadcast_to(bias_sum, shape), 0.0), axis=0,
                       keepdims=True)
    for h in range(halves):
        cols = slice(h * width, (h + 1) * width)
        top = h * 24
        small[top : top + 8, :] = low[:, cols]
        small[top + 8 : top + 16, :] = high[:, cols]
        small[top + 16 : top + 17, :] = g_first[inputs : inputs + 1, cols]
        small[top + 17 : top + 18, :] = g_second[hidden : hidden + 1, cols]
        if h == 0:
            small[top + 18 : top + 19, :] = bias_row
        small[top + 19 : top + 19 + fluxes, :] = g_third[0:fluxes, cols]
    for d in range(devices):
        done = 0
        while done < share:
            at = d * share + done
            h, row = divmod(at, hidden)
            step = min(share - done, hidden - row)
            if h < halves:
                stage[d, slot_rows + done : slot_rows + done + step, :] = g_second[
                    row : row + step, h * width : (h + 1) * width
                ]
            done += step
        piece = small[d * small_share : (d + 1) * small_share, :]
        head = piece.astype(bf16).astype(f32)
        top = slot_rows + share
        stage[d, top : top + small_share, :] = head
        stage[d, top + small_share : top + 2 * small_share, :] = piece - head
    send_out[...] = stage[...].astype(bf16)
    for copy in (*stores, rest):
        copy.wait()


def sum_kernel(scale, share, small_share, recv, out, stage):
    devices = recv.shape[0]
    packed = stage.shape[0]
    at = slice(recv.shape[1] - packed, recv.shape[1])
    total = recv[0, at, :].astype(f32)
    for d in range(1, devices):
        total = total + recv[d, at, :].astype(f32)
    stage[...] = total * scale
    low = slice(share + small_share, share + 2 * small_share)
    piece = stage[share : share + small_share, :] + stage[low, :]
    head = piece.astype(bf16).astype(f32)
    stage[share : share + small_share, :] = head
    stage[low, :] = piece - head
    total = stage[...].astype(bf16)
    for d in range(devices):
        out[d] = total


def back_kernel(
    rows, peers, slots, recv, kernels, source_in, count_in, rate_in, base_in, diffuse_in, out,
    source, count, rate_ref, base, diffuse, total, sems,
):
    meta = place()
    copies = fetch_all(
        [
            (diffuse_in, diffuse),
            (base_in, base),
            (source_in, source),
            (count_in, count),
            (rate_in, rate_ref),
        ],
        sems,
    )
    for copy in copies:
        copy.wait()
    width = kernels.shape[2]
    width = diffuse.shape[2]
    shape = (SUBLANES, width)
    lane = lax.broadcasted_iota(jnp.int32, shape, 1)
    west, east, south, north = get_edges(meta, recv)
    comp = meta[COMP]
    rate = jnp.broadcast_to(column_of(rate_ref, comp), shape)

    def lap_step(r, unused):
        here = diffuse[r]
        below = jnp.where(r > 0, diffuse[jnp.maximum(r - 1, 0)], south)
        above = jnp.where(r < rows - 1, diffuse[jnp.minimum(r + 1, rows - 1)], north)
        total[r] = base[r] + rate * laplace_row(here, below, above, west, east, r, lane)
        return unused

    lax.fori_loop(0, rows, lap_step, 0, unroll=8)

    def peer_step(q, unused):
        block = recv[meta[OTHER] + q, 0 : slots * SUBLANES, :].astype(f32)
        for s in range(slots):
            k = q * slots + s
            sent = block[s * SUBLANES : (s + 1) * SUBLANES].astype(bf16)
            live = (s < count[q]).astype(f32)
            row = source[s, q]
            total[row] = total[row] + dot_nt(sent, kernels[k]) * live
        return unused

    lax.fori_loop(0, peers, peer_step, 0, unroll=4)

    def out_step(r, unused):
        out[pl.ds(r, SUBLANES, stride=rows), :] = total[r]
        return unused

    lax.fori_loop(0, rows, out_step, 0, unroll=8)


def unpack_kernel(share, small_share, fluxes, recv, first, bias_one, second, bias_two, third,
                  bias_three, small):
    devices = recv.shape[0]
    width = recv.shape[2]
    hidden = second.shape[0]
    halves = hidden // width
    for d in range(devices):
        block = recv[d].astype(f32)
        done = 0
        while done < share:
            at = d * share + done
            h, row = divmod(at, hidden)
            step = min(share - done, hidden - row)
            if h < halves:
                second[row : row + step, h * width : (h + 1) * width] = block[done : done + step]
            done += step
        small[d * small_share : (d + 1) * small_share, :] = (
            block[share : share + small_share]
            + block[share + small_share : share + 2 * small_share]
        )
    for h in range(halves):
        cols = slice(h * width, (h + 1) * width)
        top = h * 24
        first[:, cols] = small[top : top + 16, :]
        bias_one[:, cols] = small[top + 16 : top + 17, :]
        bias_two[:, cols] = small[top + 17 : top + 18, :]
        third[:, cols] = small[top + 19 : top + 19 + fluxes, :]
    bias_three[...] = small[18:19, 0:fluxes]


def shards(
    state,
    target,
    land_mask,
    diffusivity,
    coupling,
    w_in,
    b_in,
    w_mid,
    b_mid,
    w_out,
    b_out,
    remap_weight,
    remap_source,
    remap_target,
    remap_count,
):
    n_gy, n_gx = lax.axis_size("gy"), lax.axis_size("gx")
    tiles = n_gy * n_gx
    devices = 2 * tiles
    comp = lax.axis_index("comp")
    channels, rows, width = state.shape[1:]
    hidden = w_mid.shape[0]
    inputs = w_in.shape[0]
    fluxes = w_out.shape[1]
    peers, slots = remap_source.shape[3:]
    surface = state.reshape(channels * rows, width)
    goal = target.reshape(channels * rows, width)
    mask = land_mask[0]
    source = remap_source.reshape(peers, slots).T
    landing = remap_target.reshape(peers, slots).T
    count = remap_count.reshape(peers)
    kernels = remap_weight.reshape(peers * slots, width, width)
    slot_rows = slots * channels

    vmem = pl.BlockSpec(memory_space=pltpu.VMEM)

    far = pl.BlockSpec(memory_space=pltpu.HBM)
    parts = math.gcd(peers, 4)
    outgoing, by_row = pl.pallas_call(
        functools.partial(send_kernel, rows, peers, slots),
        name="send",
        out_shape=(
            jax.ShapeDtypeStruct((devices, slot_rows, width), bf16),
            jax.ShapeDtypeStruct((rows, channels, width), f32),
        ),
        in_specs=[far] * 4,
        out_specs=(vmem, vmem),
        scratch_shapes=[
            pltpu.VMEM((devices, slot_rows, width), f32),
            pltpu.VMEM(kernels.shape, bf16),
            pltpu.SemaphoreType.DMA((parts,)),
            pltpu.SMEM(source.shape, jnp.int32),
            pltpu.SMEM(count.shape, jnp.int32),
            pltpu.VMEM(surface.shape, f32),
            pltpu.SemaphoreType.DMA((3,)),
        ],
    )(source, count, surface, kernels)
    arrived = lax.all_to_all(outgoing, EVERYWHERE, 0, 0, tiled=True)

    def pieces(bias):
        high = bias.astype(bf16)
        rest = bias - high.astype(f32)
        middle = rest.astype(bf16)
        low = (rest - middle.astype(f32)).astype(bf16)
        return jnp.stack([high, middle, low], axis=0)

    local_in = jnp.where(comp == 1, jnp.roll(w_in, channels, axis=0), w_in)
    half = jnp.asarray(0.5, bf16)
    w_first = jnp.concatenate(
        [local_in, pieces(b_in), jnp.zeros((13, hidden), bf16)], axis=0
    ).T * half
    w_second = w_mid.T * half
    b_second = (b_mid * 0.5)[:, None]
    w_third = jnp.pad(w_out.T, ((0, 16 - fluxes), (0, 0)))
    w_third_back = jnp.pad(w_out * half, ((0, 0), (0, 16 - fluxes)))
    w_second_back = w_mid * half
    w_first_back = local_in

    share = -(-hidden * hidden // (width * devices))
    small_share = -(-24 * hidden // (width * devices))
    packed = -(-(share + 2 * small_share) // 8) * 8
    cells = BLOCK_ROWS * width

    def twice(*args):
        return (pltpu.VMEM(*args), pltpu.VMEM(*args))

    tall = (rows, channels, width)
    tables = (
        mask,
        diffusivity,
        coupling,
        w_first,
        w_second,
        b_second,
        w_third,
        w_third_back,
        w_second_back,
        w_first_back,
    )
    new_state, base, diffuse, leaving = pl.pallas_call(
        functools.partial(main_kernel, rows, peers, slots, share, small_share),
        name="main",
        out_shape=(
            jax.ShapeDtypeStruct((channels * rows, width), f32),
            jax.ShapeDtypeStruct(tall, f32),
            jax.ShapeDtypeStruct((rows, channels, width), f32),
            jax.ShapeDtypeStruct((devices, slot_rows + packed, width), bf16),
        ),
        in_specs=[vmem] * 3 + [far] * FETCHED,
        out_specs=(far,) * 3 + (vmem,),
        scratch_shapes=[
            pltpu.SMEM(landing.shape, jnp.int32),
            pltpu.SMEM(b_out.shape, f32),
            *(pltpu.VMEM(array.shape, array.dtype) for array in tables),
            pltpu.SemaphoreType.DMA((FETCHED,)),
            pltpu.SemaphoreType.DMA((4,)),
            pltpu.VMEM((channels * rows, width), f32),
            pltpu.VMEM(tall, f32),
            pltpu.VMEM((rows, channels, width), f32),
            pltpu.VMEM((devices, slot_rows + packed, width), f32),
            pltpu.VMEM(tall, f32),
            pltpu.VMEM(tall, f32),
            twice((BLOCK_ROWS, 32, width), bf16),
            twice((BLOCK_ROWS, hidden + 16, width), bf16),
            twice((BLOCK_ROWS, hidden, width), bf16),
            twice((BLOCK_ROWS, hidden, width), f32),
            twice((BLOCK_ROWS, hidden, width), f32),
            twice((BLOCK_ROWS, 16, width), bf16),
            pltpu.VMEM((BLOCK_ROWS, hidden, width), bf16),
            pltpu.VMEM((BLOCK_ROWS, hidden, width), bf16),
            pltpu.VMEM((8, cells), f32),
            pltpu.VMEM((16, cells), f32),
            pltpu.VMEM((32, hidden), f32),
            pltpu.VMEM((hidden + 16, hidden), f32),
            pltpu.VMEM((16, hidden), f32),
            pltpu.VMEM((8, width), f32),
            pltpu.VMEM((2, 8, width), f32),
            pltpu.VMEM((max(48, small_share * devices), width), f32),
        ],
    )(
        near(by_row),
        near(goal),
        near(arrived),
        landing,
        b_out,
        *tables,
    )
    returned = lax.all_to_all(leaving, EVERYWHERE, 0, 0, tiled=True)
    scale = 1.0 / (rows * width * tiles)
    summed = pl.pallas_call(
        functools.partial(sum_kernel, scale, share, small_share),
        name="sum",
        out_shape=jax.ShapeDtypeStruct((devices, packed, width), bf16),
        in_specs=[vmem],
        out_specs=vmem,
        scratch_shapes=[pltpu.VMEM((packed, width), f32)],
    )(near(returned))
    gathered = lax.all_to_all(summed, EVERYWHERE, 0, 0, tiled=True)
    adjoint = pl.pallas_call(
        functools.partial(back_kernel, rows, peers, slots),
        name="back",
        out_shape=jax.ShapeDtypeStruct((channels * rows, width), f32),
        in_specs=[vmem] * 2 + [far] * 5,
        out_specs=vmem,
        scratch_shapes=[
            pltpu.SMEM(source.shape, jnp.int32),
            pltpu.SMEM(count.shape, jnp.int32),
            pltpu.VMEM(diffusivity.shape, f32),
            pltpu.VMEM(tall, f32),
            pltpu.VMEM(tall, f32),
            pltpu.VMEM(tall, f32),
            pltpu.SemaphoreType.DMA((5,)),
        ],
    )(near(returned), kernels, source, count, diffusivity, base, diffuse)
    first, bias_one, second, bias_two, third, bias_three = pl.pallas_call(
        functools.partial(unpack_kernel, share, small_share, fluxes),
        name="unpack",
        out_shape=(
            jax.ShapeDtypeStruct((inputs, hidden), f32),
            jax.ShapeDtypeStruct((1, hidden), f32),
            jax.ShapeDtypeStruct((hidden, hidden), f32),
            jax.ShapeDtypeStruct((1, hidden), f32),
            jax.ShapeDtypeStruct((fluxes, hidden), f32),
            jax.ShapeDtypeStruct((1, fluxes), f32),
        ),
        in_specs=[vmem],
        out_specs=(vmem,) * 6,
        scratch_shapes=[pltpu.VMEM((max(48, small_share * devices), width), f32)],
    )(near(gathered))
    return (
        new_state.reshape(state.shape),
        adjoint.reshape(state.shape),
        first,
        bias_one[0],
        second,
        bias_two[0],
        third.T,
        bias_three[0],
    )


def near(array):
    return pltpu.with_memory_space_constraint(array, pltpu.VMEM)


def solution(mesh):
    tiles = P("comp", None, "gy", "gx")
    placed = (
        tiles,
        tiles,
        P("comp", "gy", "gx"),
        *(P() for _ in range(8)),
        P("comp", "gy", "gx", None, None, None, None),
        P("comp", "gy", "gx", None, None),
        P("comp", "gy", "gx", None, None),
        P("comp", "gy", "gx", None),
    )
    return jax.shard_map(
        shards,
        mesh=mesh,
        in_specs=placed,
        out_specs=(tiles, tiles, *(P() for _ in range(6))),
        check_vma=False,
    )
```

```python
import functools
import math

import jax
import jax.numpy as jnp
from jax import lax
from jax.experimental import pallas as pl
from jax.experimental.pallas import tpu as pltpu
from jax.sharding import PartitionSpec as P

EVERYWHERE = ("comp", "gy", "gx")
BLOCK_ROWS = 8
CHUNK = 256
FETCHED = 12
SMALL_PLANE = 3
SUBLANES = 8

KEYS = {
    "take": (0.0, 0.05),
    "first": (0.05, 0.3),
    "second": (0.3, 0.6),
    "third": (0.6, 0.65),
    "fields": (0.65, 1.0),
    "cot_second": (0.05, 0.3),
    "cot_first": (0.3, 0.6),
    "cot_inputs": (0.62, 0.7),
    "leave": (0.9, 1.0),
    "grad_second": 0.61,
    "grad_third": 0.605,
    "grad_first": 0.71,
}

OWN, OTHER, WEST, EAST, SOUTH, NORTH, COMP, HAS_SOUTH, HAS_NORTH, ON_FOLD = range(10)

f32 = jnp.float32
bf16 = jnp.bfloat16


def fetch_all(pairs, sems):
    copies = [
        pltpu.make_async_copy(src, dst, sems.at[i])
        for i, (src, dst) in enumerate(pairs)
    ]
    for copy in copies:
        copy.start()
    return copies


def side_by_side(ref, first, count, low, high):
    return jnp.concatenate([ref[first + i, low:high, :] for i in range(count)], axis=1)


def place():
    n_gy, n_gx = lax.axis_size("gy"), lax.axis_size("gx")
    comp, row, col = (lax.axis_index(axis) for axis in EVERYWHERE)
    tiles = n_gy * n_gx
    own = comp * tiles
    line = own + row * n_gx
    here = line + col
    is_top = row == n_gy - 1
    on_fold = jnp.logical_and(comp == 1, is_top)
    up = jnp.where(is_top, here, here + n_gx)
    return (
        own,
        (1 - comp) * tiles,
        line + lax.rem(col + (n_gx - 1), n_gx),
        line + lax.rem(col + 1, n_gx),
        jnp.where(row > 0, here - n_gx, here),
        jnp.where(on_fold, line + (n_gx - 1) - col, up),
        comp,
        (row > 0).astype(jnp.int32),
        jnp.logical_or(on_fold, jnp.logical_not(is_top)).astype(jnp.int32),
        on_fold.astype(jnp.int32),
    )


def dot(a, b):
    return jnp.dot(a, b, preferred_element_type=f32)


def dot_nt(a, b):
    return lax.dot_general(a, b, (((1,), (1,)), ((), ())), preferred_element_type=f32)


def mirror(tile):
    width = tile.shape[1]
    row = lax.broadcasted_iota(jnp.int32, (width, width), 0)
    col = lax.broadcasted_iota(jnp.int32, (width, width), 1)
    flip = (row + col == width - 1).astype(f32).astype(bf16)
    return dot(tile.astype(bf16), flip)


def put_edges(meta, first, last, bottom, top, stage):
    stage[meta[EAST], 0:SUBLANES, :] = last
    stage[meta[WEST], SUBLANES : 2 * SUBLANES, :] = first
    top = jnp.where(meta[ON_FOLD] == 1, mirror(top), top)
    straight = jnp.logical_and(meta[HAS_NORTH] == 1, meta[ON_FOLD] == 0)
    up = pl.multiple_of(jnp.where(straight, 0, 2 * SUBLANES), SUBLANES)
    down = pl.multiple_of(jnp.where(meta[HAS_SOUTH] == 1, SUBLANES, 2 * SUBLANES), SUBLANES)
    stage[meta[SOUTH], pl.ds(down, SUBLANES), :] = bottom
    stage[meta[NORTH], pl.ds(up, SUBLANES), :] = top


def take_edges(tile, r, lane, sides):
    width = tile.shape[1]
    here = lane == r
    first, last = sides
    first = jnp.where(here, pltpu.roll(tile, r, 1), first)
    last = jnp.where(here, pltpu.roll(tile, lax.rem(r + 1, width), 1), last)
    return first, last


def get_edges(meta, recv):
    west = recv[meta[WEST], 0 : 4 * SUBLANES, :].astype(f32)[0:SUBLANES]
    east = recv[meta[EAST], 0 : 4 * SUBLANES, :].astype(f32)[SUBLANES : 2 * SUBLANES]
    south = recv[meta[SOUTH], 0 : 4 * SUBLANES, :].astype(f32)[0:SUBLANES]
    above = recv[meta[NORTH], 0 : 4 * SUBLANES, :].astype(f32)
    north = jnp.where(
        meta[ON_FOLD] == 1,
        above[2 * SUBLANES : 3 * SUBLANES],
        above[SUBLANES : 2 * SUBLANES],
    )
    south = jnp.where(meta[HAS_SOUTH] == 1, south, 0.0)
    north = jnp.where(meta[HAS_NORTH] == 1, north, 0.0)
    return west, east, south, north


def laplace_row(here, below, above, west, east, r, lane):
    width = here.shape[1]
    left = jnp.where(
        lane == 0, pltpu.roll(west, lax.rem(width - r, width), 1), pltpu.roll(here, 1, 1)
    )
    right = jnp.where(
        lane == width - 1, pltpu.roll(east, width - 1 - r, 1), pltpu.roll(here, width - 1, 1)
    )
    return left + right + below + above - 4.0 * here


def column_of(row, comp):
    eye = (
        lax.broadcasted_iota(jnp.int32, (SUBLANES, SUBLANES), 0)
        == lax.broadcasted_iota(jnp.int32, (SUBLANES, SUBLANES), 1)
    ).astype(f32)
    return jnp.sum(
        jnp.broadcast_to(row[pl.ds(comp, 1), :], (SUBLANES, SUBLANES)) * eye,
        axis=1,
        keepdims=True,
    )


def send_kernel(
    rows, peers, slots, source_in, count_in, state_in, kernels, out, by_row, stage, blocks, sems,
    source, count, state, small_sems,
):
    meta = place()
    small = fetch_all([(state_in, state), (source_in, source), (count_in, count)], small_sems)
    width = state.shape[1]
    shape = (SUBLANES, width)
    sub = lax.broadcasted_iota(jnp.int32, shape, 0)
    parts = sems.shape[0]
    part = peers // parts
    copies = [
        pltpu.make_async_copy(
            kernels.at[pl.ds(i * part * slots, part * slots)],
            blocks.at[pl.ds(i * part * slots, part * slots)],
            sems.at[i],
        )
        for i in range(parts)
    ]
    for copy in copies:
        copy.start()
    stage[pl.ds(meta[OWN], peers)] = jnp.zeros((peers,) + stage.shape[1:], f32)

    for copy in small:
        copy.wait()

    def row_step(r, unused):
        by_row[r] = state[pl.ds(r, SUBLANES, stride=rows), :]
        return unused

    lax.fori_loop(0, rows, row_step, 0, unroll=32)
    wide = (16, width)
    which = lax.broadcasted_iota(jnp.int32, wide, 0)
    place_of = lax.broadcasted_iota(jnp.int32, wide, 1)
    unit = jnp.logical_or(
        jnp.logical_and(which == 0, place_of == 0),
        jnp.logical_and(which == 1, place_of == width - 1),
    )
    unit = unit.astype(f32).astype(bf16)
    first = jnp.zeros(shape, f32)
    last = jnp.zeros(shape, f32)
    for ch in range(SUBLANES):
        both = dot_nt(unit, state[ch * rows : (ch + 1) * rows, :].astype(bf16))
        first = jnp.where(sub == ch, jnp.broadcast_to(both[0:1], shape), first)
        last = jnp.where(sub == ch, jnp.broadcast_to(both[1:2], shape), last)
    put_edges(meta, first, last, by_row[0], by_row[rows - 1], stage)

    def peer_step(q, unused):
        for s in range(slots):
            k = q * slots + s
            picked = by_row[source[s, q]].astype(bf16)
            live = (s < count[q]).astype(f32)
            stage[meta[OTHER] + q, s * SUBLANES : (s + 1) * SUBLANES, :] = (
                dot(picked, blocks[k]) * live
            )
        return unused

    for i in range(parts):
        copies[i].wait()
        lax.fori_loop(i * part, (i + 1) * part, peer_step, 0, unroll=math.gcd(part, 4))
    out[...] = stage[...].astype(bf16)


def spread(low, high, step, count):
    return [
        (low + (high - low) * (i + 0.5) / count, functools.partial(step, i)) for i in range(count)
    ]


def weave(*lists):
    for entry in sorted((e for steps in lists for e in steps), key=lambda e: e[0]):
        entry[1]()


def main_kernel(
    rows,
    peers,
    slots,
    share,
    small_share,
    state,
    goal,
    recv,
    *refs,
):
    fetched, refs = refs[:FETCHED], refs[FETCHED:]
    (new_hbm, base_hbm, diffuse_hbm, send_out), refs = refs[:4], refs[4:]
    kept, refs = refs[:FETCHED], refs[FETCHED:]
    fetch_sems, store_sems, new_out, base_out, diffuse_out = refs[:5]
    copies = fetch_all(list(zip(fetched, kept, strict=True)), fetch_sems)
    main_steps(
        rows,
        peers,
        slots,
        share,
        small_share,
        copies,
        state,
        goal,
        recv,
        *kept,
        new_hbm,
        base_hbm,
        diffuse_hbm,
        send_out,
        store_sems,
        new_out,
        base_out,
        diffuse_out,
        *refs[5:],
    )


def main_steps(
    rows,
    peers,
    slots,
    share,
    small_share,
    copies,
    state,
    goal,
    recv,
    landing,
    b_out,
    mask,
    rate_ref,
    couple_ref,
    w_first,
    w_second,
    b_second,
    w_third,
    w_third_back,
    w_second_back,
    w_first_back,
    new_hbm,
    base_hbm,
    diffuse_hbm,
    send_out,
    store_sems,
    new_out,
    base_out,
    diffuse_out,
    stage,
    other,
    misfits,
    feats,
    hid_firsts,
    hid_seconds,
    slope_firsts,
    slope_seconds,
    flux_cots,
    cot_second,
    cot_first,
    flux,
    feat_cot,
    g_first,
    g_second,
    g_third,
    g_bias,
    edges,
    small,
):
    width = state.shape[2]
    hidden = w_second.shape[0]
    shape = (SUBLANES, width)
    cells = BLOCK_ROWS * width
    chunks = cells // CHUNK
    lane = lax.broadcasted_iota(jnp.int32, shape, 1)
    sub = lax.broadcasted_iota(jnp.int32, shape, 0)
    fluxes = couple_ref.shape[2]
    meta = place()
    slot_rows = recv.shape[1]
    assert 2 * small_share <= SUBLANES
    other[...] = jnp.zeros(other.shape, f32)
    for copy in copies:
        copy.wait()

    def land(p, unused):
        block = recv[meta[OTHER] + p].astype(f32)
        for s in range(slots):
            row = landing[s, p]
            other[row] = other[row] + block[s * SUBLANES : (s + 1) * SUBLANES]
        return unused

    lax.fori_loop(0, peers, land, 0, unroll=2)
    west, east, south, north = get_edges(meta, recv)
    comp = meta[COMP]
    rate = jnp.broadcast_to(column_of(rate_ref, comp), shape)
    pairs = couple_ref[comp]
    couple = [jnp.broadcast_to(pairs[:, f : f + 1], shape) for f in range(fluxes)]
    ones = (lax.broadcasted_iota(jnp.int32, (16, width), 0) < 3).astype(f32).astype(bf16)
    lanes = CHUNK // width
    for ref in flux_cots:
        ref[...] = jnp.zeros(ref.shape, bf16)
    for ref in feats:
        for i in range(BLOCK_ROWS):
            ref[i, 16:32, :] = ones
    for ref in hid_firsts:
        for i in range(BLOCK_ROWS):
            ref[i, hidden : hidden + 16, :] = ones
    for ref in (g_first, g_second, g_third, g_bias, edges):
        ref[...] = jnp.zeros(ref.shape, f32)
    bias = jnp.broadcast_to(b_second[...], (hidden, CHUNK))
    b_third = jnp.zeros(shape, f32)
    for f in range(fluxes):
        b_third = jnp.where(sub == f, b_out[f], b_third)

    def forward(block, feat, hid_first, hid_second, slope_first, slope_second, flux_cot):
        start = block * BLOCK_ROWS

        def take(i):
            r = start + i
            feat[i, 0:16, :] = jnp.concatenate([state[r], other[r]], axis=0).astype(bf16)

        def layer(net, hid_ref, slope_ref, j):
            turn = jnp.tanh(net)
            up = 1.0 + turn
            hid = net * up
            slope = (up + hid) - hid * turn
            hid = hid.astype(bf16)
            for i in range(lanes):
                cols = slice(i * width, (i + 1) * width)
                hid_ref[j * lanes + i, 0:hidden, :] = hid[:, cols]
                slope_ref[j * lanes + i] = slope[:, cols]

        def first(j):
            net = dot(w_first[...], side_by_side(feat, j * lanes, lanes, 0, 32))
            layer(net, hid_first, slope_first, j)

        def second(j):
            net = dot(w_second[...], side_by_side(hid_first, j * lanes, lanes, 0, hidden)) + bias
            layer(net, hid_second, slope_second, j)

        def third(j):
            at = pl.ds(j * CHUNK, CHUNK)
            hid = side_by_side(hid_second, j * lanes, lanes, 0, hidden)
            flux[:, at] = dot(w_third[...], hid)[0:SUBLANES]

        def fields(i):
            at = pl.ds(i * width, width)
            r = start + i
            here = state[r]
            below = jnp.where(r > 0, state[jnp.maximum(r - 1, 0)], south)
            above = jnp.where(r < rows - 1, state[jnp.minimum(r + 1, rows - 1)], north)
            lap = laplace_row(here, below, above, west, east, r, lane)
            wet = jnp.broadcast_to(mask[pl.ds(r, 1), :].astype(f32), shape)
            spread_mask = jnp.where(comp == 1, wet, 1.0)
            wet_flux = (flux[:, at] + b_third) * wet
            updated = here + rate * spread_mask * lap
            for f in range(fluxes):
                updated = updated + couple[f] * jnp.broadcast_to(wet_flux[f : f + 1], shape)
            new_out[pl.ds(r, SUBLANES, stride=rows), :] = updated
            misfit = updated - goal[pl.ds(r, SUBLANES, stride=rows), :]
            diffuse = spread_mask * misfit
            diffuse_out[r] = diffuse
            edges[0], edges[1] = take_edges(diffuse, r, lane, (edges[0], edges[1]))
            misfits[r] = misfit
            pulled = jnp.zeros(shape, f32)
            for f in range(fluxes):
                total = jnp.sum(couple[f] * misfit, axis=0, keepdims=True)
                pulled = jnp.where(sub == f, jnp.broadcast_to(total, shape), pulled)
            pulled = (pulled * wet).astype(bf16)
            flux_cot[i, 0:SUBLANES, :] = pulled
            g_bias[...] = g_bias[...] + pulled.astype(f32)

        return (
            spread(*KEYS["take"], take, BLOCK_ROWS)
            + spread(*KEYS["first"], first, chunks)
            + spread(*KEYS["second"], second, chunks)
            + spread(*KEYS["third"], third, chunks)
            + spread(*KEYS["fields"], fields, BLOCK_ROWS)
        )

    def backward(block, feat, hid_first, hid_second, slope_first, slope_second, flux_cot):
        start = block * BLOCK_ROWS

        def pull(net, slope_ref, cot_ref, j):
            for i in range(lanes):
                cols = slice(i * width, (i + 1) * width)
                cot_ref[j * lanes + i] = (net[:, cols] * slope_ref[j * lanes + i]).astype(bf16)

        def second(j):
            net = dot(w_third_back[...], side_by_side(flux_cot, j * lanes, lanes, 0, 16))
            pull(net, slope_second, cot_second, j)

        def first(j):
            net = dot(w_second_back[...], side_by_side(cot_second, j * lanes, lanes, 0, hidden))
            pull(net, slope_first, cot_first, j)

        def inputs(j):
            at = pl.ds(j * CHUNK, CHUNK)
            cot = side_by_side(cot_first, j * lanes, lanes, 0, hidden)
            feat_cot[:, at] = dot(w_first_back[...], cot)

        def whole(ref):
            return side_by_side(ref, 0, BLOCK_ROWS, 0, ref.shape[1])

        def leave(i):
            at = pl.ds(i * width, width)
            r = start + i
            base_out[r] = misfits[r] + feat_cot[0:SUBLANES, at]
            other[r] = feat_cot[SUBLANES : 2 * SUBLANES, at]

        def grad_second():
            g_second[...] += dot_nt(whole(hid_first), whole(cot_second))

        def grad_third():
            g_third[...] += dot_nt(whole(flux_cot), whole(hid_second))

        def grad_first():
            g_first[...] += dot_nt(whole(feat), whole(cot_first))

        return (
            spread(*KEYS["cot_second"], second, chunks)
            + spread(*KEYS["cot_first"], first, chunks)
            + spread(*KEYS["cot_inputs"], inputs, chunks)
            + spread(*KEYS["leave"], leave, BLOCK_ROWS)
            + [
                (KEYS["grad_second"], grad_second),
                (KEYS["grad_third"], grad_third),
                (KEYS["grad_first"], grad_first),
            ]
        )

    sets = list(
        zip(feats, hid_firsts, hid_seconds, slope_firsts, slope_seconds, flux_cots, strict=True)
    )
    blocks = rows // BLOCK_ROWS

    def beside(block, this, that):
        weave(backward(block, *this), forward(block + 1, *that))

    def pair_step(pair, unused):
        beside(2 * pair, *sets)
        beside(2 * pair + 1, *sets[::-1])
        return unused

    weave(forward(0, *sets[0]))
    lax.fori_loop(0, blocks // 2 - 1, pair_step, 0)
    beside(blocks - 2, *sets)
    ready = rows - BLOCK_ROWS
    stores = fetch_all(
        [
            (new_out, new_hbm),
            (diffuse_out, diffuse_hbm),
            (base_out.at[pl.ds(0, ready)], base_hbm.at[pl.ds(0, ready)]),
        ],
        store_sems,
    )
    weave(backward(blocks - 1, *sets[1]))
    rest = pltpu.make_async_copy(
        base_out.at[pl.ds(ready, BLOCK_ROWS)],
        base_hbm.at[pl.ds(ready, BLOCK_ROWS)],
        store_sems.at[3],
    )
    rest.start()
    stage[pl.ds(meta[OWN], peers), 0:slot_rows, :] = jnp.zeros((peers, slot_rows, width), f32)

    def leave(p, unused):
        for s in range(slots):
            row = landing[s, p]
            stage[meta[OTHER] + p, s * SUBLANES : (s + 1) * SUBLANES, :] = other[row]
        return unused

    lax.fori_loop(0, peers, leave, 0, unroll=2)
    put_edges(meta, edges[0], edges[1], diffuse_out[0], diffuse_out[rows - 1], stage)
    devices = stage.shape[0]
    halves = hidden // width
    inputs = 2 * SUBLANES
    small[...] = jnp.zeros(small.shape, f32)
    low, high = g_first[0:SUBLANES, :], g_first[SUBLANES:inputs, :]
    low, high = jnp.where(comp == 1, high, low), jnp.where(comp == 1, low, high)
    bias_sum = jnp.sum(g_bias[...], axis=1, keepdims=True)
    bias_row = jnp.sum(jnp.where(sub == lane, jnp.broadcast_to(bias_sum, shape), 0.0), axis=0,
                       keepdims=True)
    for h in range(halves):
        cols = slice(h * width, (h + 1) * width)
        top = h * 24
        small[top : top + 8, :] = low[:, cols]
        small[top + 8 : top + 16, :] = high[:, cols]
        small[top + 16 : top + 17, :] = g_first[inputs : inputs + 1, cols]
        small[top + 17 : top + 18, :] = g_second[hidden : hidden + 1, cols]
        if h == 0:
            small[top + 18 : top + 19, :] = bias_row
        small[top + 19 : top + 19 + fluxes, :] = g_third[0:fluxes, cols]
    for d in range(devices):
        done = 0
        while done < share:
            at = d * share + done
            h, row = divmod(at, hidden)
            step = min(share - done, hidden - row)
            if h < halves:
                stage[d, slot_rows + done : slot_rows + done + step, :] = g_second[
                    row : row + step, h * width : (h + 1) * width
                ]
            done += step
    top = SMALL_PLANE * SUBLANES
    for p in range(peers):
        piece = small[p * small_share : (p + 1) * small_share, :]
        head = piece.astype(bf16).astype(f32)
        stage[meta[OWN] + p, top : top + small_share, :] = head
        stage[meta[OWN] + p, top + small_share : top + 2 * small_share, :] = piece - head
    send_out[...] = stage[...].astype(bf16)
    for copy in (*stores, rest):
        copy.wait()


def sum_kernel(scale, peers, share, small_share, recv, out, stage):
    devices = recv.shape[0]
    own = lax.axis_index("comp") * peers
    slot_rows = 4 * SUBLANES
    planes = slice(SMALL_PLANE * SUBLANES, (SMALL_PLANE + 1) * SUBLANES)
    at = slice(slot_rows, slot_rows + -(-share // SUBLANES) * SUBLANES)
    total = recv[0, at, :].astype(f32)
    for d in range(1, devices):
        total = total + recv[d, at, :].astype(f32)
    part = recv[own, planes, :].astype(f32)
    for p in range(1, peers):
        part = part + recv[own + p, planes, :].astype(f32)
    part = part * scale
    piece = part[0:small_share] + part[small_share : 2 * small_share]
    head = piece.astype(bf16).astype(f32)
    stage[0:share, :] = total[0:share] * scale
    stage[share : share + small_share, :] = head
    stage[share + small_share : share + 2 * small_share, :] = piece - head
    total = stage[...].astype(bf16)
    for d in range(devices):
        out[d] = total


def back_kernel(
    rows, peers, slots, recv, kernels, source_in, count_in, rate_in, base_in, diffuse_in, out,
    source, count, rate_ref, base, diffuse, total, blocks, sems, block_sems,
):
    meta = place()
    copies = fetch_all(
        [
            (diffuse_in, diffuse),
            (base_in, base),
            (source_in, source),
            (count_in, count),
            (rate_in, rate_ref),
        ],
        sems,
    )
    parts = block_sems.shape[0]
    part = peers // parts
    steps = [pl.ds(i * part * slots, part * slots) for i in range(parts)]
    block_copies = fetch_all([(kernels.at[at], blocks.at[at]) for at in steps], block_sems)
    for copy in copies:
        copy.wait()
    width = diffuse.shape[2]
    shape = (SUBLANES, width)
    lane = lax.broadcasted_iota(jnp.int32, shape, 1)
    west, east, south, north = get_edges(meta, recv)
    comp = meta[COMP]
    rate = jnp.broadcast_to(column_of(rate_ref, comp), shape)

    def lap_step(r, unused):
        here = diffuse[r]
        below = jnp.where(r > 0, diffuse[jnp.maximum(r - 1, 0)], south)
        above = jnp.where(r < rows - 1, diffuse[jnp.minimum(r + 1, rows - 1)], north)
        total[r] = base[r] + rate * laplace_row(here, below, above, west, east, r, lane)
        return unused

    lax.fori_loop(0, rows, lap_step, 0, unroll=32)

    def peer_step(q, unused):
        block = recv[meta[OTHER] + q, 0 : slots * SUBLANES, :].astype(f32)
        for s in range(slots):
            k = q * slots + s
            sent = block[s * SUBLANES : (s + 1) * SUBLANES].astype(bf16)
            live = (s < count[q]).astype(f32)
            row = source[s, q]
            total[row] = total[row] + dot_nt(sent, blocks[k]) * live
        return unused

    for i in range(parts):
        block_copies[i].wait()
        lax.fori_loop(i * part, (i + 1) * part, peer_step, 0, unroll=math.gcd(part, 4))

    def out_step(r, unused):
        out[pl.ds(r, SUBLANES, stride=rows), :] = total[r]
        return unused

    lax.fori_loop(0, rows, out_step, 0, unroll=32)


def unpack_kernel(share, small_share, fluxes, recv, first, bias_one, second, bias_two, third,
                  bias_three, small):
    devices = recv.shape[0]
    peers = devices // 2
    width = recv.shape[2]
    hidden = second.shape[0]
    halves = hidden // width
    for d in range(devices):
        block = recv[d].astype(f32)
        done = 0
        while done < share:
            at = d * share + done
            h, row = divmod(at, hidden)
            step = min(share - done, hidden - row)
            if h < halves:
                second[row : row + step, h * width : (h + 1) * width] = block[done : done + step]
            done += step
        piece = (
            block[share : share + small_share]
            + block[share + small_share : share + 2 * small_share]
        )
        at = d % peers * small_share
        if d >= peers:
            piece = piece + small[at : at + small_share, :]
        small[at : at + small_share, :] = piece
    for h in range(halves):
        cols = slice(h * width, (h + 1) * width)
        top = h * 24
        first[:, cols] = small[top : top + 16, :]
        bias_one[:, cols] = small[top + 16 : top + 17, :]
        bias_two[:, cols] = small[top + 17 : top + 18, :]
        third[:, cols] = small[top + 19 : top + 19 + fluxes, :]
    bias_three[...] = small[18:19, 0:fluxes]


def shards(
    state,
    target,
    land_mask,
    diffusivity,
    coupling,
    w_in,
    b_in,
    w_mid,
    b_mid,
    w_out,
    b_out,
    remap_weight,
    remap_source,
    remap_target,
    remap_count,
):
    n_gy, n_gx = lax.axis_size("gy"), lax.axis_size("gx")
    tiles = n_gy * n_gx
    devices = 2 * tiles
    comp = lax.axis_index("comp")
    channels, rows, width = state.shape[1:]
    hidden = w_mid.shape[0]
    inputs = w_in.shape[0]
    fluxes = w_out.shape[1]
    peers, slots = remap_source.shape[3:]
    surface = state.reshape(channels * rows, width)
    goal = target.reshape(channels * rows, width)
    mask = land_mask[0]
    source = remap_source.reshape(peers, slots).T
    landing = remap_target.reshape(peers, slots).T
    count = remap_count.reshape(peers)
    kernels = remap_weight.reshape(peers * slots, width, width)
    slot_rows = slots * channels

    vmem = pl.BlockSpec(memory_space=pltpu.VMEM)

    far = pl.BlockSpec(memory_space=pltpu.HBM)
    parts = math.gcd(peers, 4)
    outgoing, by_row = pl.pallas_call(
        functools.partial(send_kernel, rows, peers, slots),
        name="send",
        out_shape=(
            jax.ShapeDtypeStruct((devices, slot_rows, width), bf16),
            jax.ShapeDtypeStruct((rows, channels, width), f32),
        ),
        in_specs=[far] * 4,
        out_specs=(vmem, vmem),
        scratch_shapes=[
            pltpu.VMEM((devices, slot_rows, width), f32),
            pltpu.VMEM(kernels.shape, bf16),
            pltpu.SemaphoreType.DMA((parts,)),
            pltpu.SMEM(source.shape, jnp.int32),
            pltpu.SMEM(count.shape, jnp.int32),
            pltpu.VMEM(surface.shape, f32),
            pltpu.SemaphoreType.DMA((3,)),
        ],
    )(source, count, surface, kernels)
    arrived = lax.all_to_all(outgoing, EVERYWHERE, 0, 0, tiled=True)

    def pieces(bias):
        high = bias.astype(bf16)
        rest = bias - high.astype(f32)
        middle = rest.astype(bf16)
        low = (rest - middle.astype(f32)).astype(bf16)
        return jnp.stack([high, middle, low], axis=0)

    local_in = jnp.where(comp == 1, jnp.roll(w_in, channels, axis=0), w_in)
    half = jnp.asarray(0.5, bf16)
    w_first = jnp.concatenate(
        [local_in, pieces(b_in), jnp.zeros((13, hidden), bf16)], axis=0
    ).T * half
    w_second = w_mid.T * half
    b_second = (b_mid * 0.5)[:, None]
    w_third = jnp.pad(w_out.T, ((0, 16 - fluxes), (0, 0)))
    w_third_back = jnp.pad(w_out * half, ((0, 0), (0, 16 - fluxes)))
    w_second_back = w_mid * half
    w_first_back = local_in

    share = -(-hidden * hidden // (width * devices))
    small_share = -(-24 * hidden // (width * tiles))
    sent = -(-share // 8) * 8
    packed = -(-(share + 2 * small_share) // 8) * 8
    cells = BLOCK_ROWS * width

    def twice(*args):
        return (pltpu.VMEM(*args), pltpu.VMEM(*args))

    tall = (rows, channels, width)
    tables = (
        mask,
        diffusivity,
        coupling,
        w_first,
        w_second,
        b_second,
        w_third,
        w_third_back,
        w_second_back,
        w_first_back,
    )
    new_state, base, diffuse, leaving = pl.pallas_call(
        functools.partial(main_kernel, rows, peers, slots, share, small_share),
        name="main",
        out_shape=(
            jax.ShapeDtypeStruct((channels * rows, width), f32),
            jax.ShapeDtypeStruct(tall, f32),
            jax.ShapeDtypeStruct((rows, channels, width), f32),
            jax.ShapeDtypeStruct((devices, slot_rows + sent, width), bf16),
        ),
        in_specs=[vmem] * 3 + [far] * FETCHED,
        out_specs=(far,) * 3 + (vmem,),
        scratch_shapes=[
            pltpu.SMEM(landing.shape, jnp.int32),
            pltpu.SMEM(b_out.shape, f32),
            *(pltpu.VMEM(array.shape, array.dtype) for array in tables),
            pltpu.SemaphoreType.DMA((FETCHED,)),
            pltpu.SemaphoreType.DMA((4,)),
            pltpu.VMEM((channels * rows, width), f32),
            pltpu.VMEM(tall, f32),
            pltpu.VMEM((rows, channels, width), f32),
            pltpu.VMEM((devices, slot_rows + sent, width), f32),
            pltpu.VMEM(tall, f32),
            pltpu.VMEM(tall, f32),
            twice((BLOCK_ROWS, 32, width), bf16),
            twice((BLOCK_ROWS, hidden + 16, width), bf16),
            twice((BLOCK_ROWS, hidden, width), bf16),
            twice((BLOCK_ROWS, hidden, width), f32),
            twice((BLOCK_ROWS, hidden, width), f32),
            twice((BLOCK_ROWS, 16, width), bf16),
            pltpu.VMEM((BLOCK_ROWS, hidden, width), bf16),
            pltpu.VMEM((BLOCK_ROWS, hidden, width), bf16),
            pltpu.VMEM((8, cells), f32),
            pltpu.VMEM((16, cells), f32),
            pltpu.VMEM((32, hidden), f32),
            pltpu.VMEM((hidden + 16, hidden), f32),
            pltpu.VMEM((16, hidden), f32),
            pltpu.VMEM((8, width), f32),
            pltpu.VMEM((2, 8, width), f32),
            pltpu.VMEM((max(48, small_share * tiles), width), f32),
        ],
    )(
        near(by_row),
        near(goal),
        near(arrived),
        landing,
        b_out,
        *tables,
    )
    returned = lax.all_to_all(leaving, EVERYWHERE, 0, 0, tiled=True)
    scale = 1.0 / (rows * width * tiles)
    summed = pl.pallas_call(
        functools.partial(sum_kernel, scale, peers, share, small_share),
        name="sum",
        out_shape=jax.ShapeDtypeStruct((devices, packed, width), bf16),
        in_specs=[vmem],
        out_specs=vmem,
        scratch_shapes=[pltpu.VMEM((packed, width), f32)],
    )(near(returned))
    gathered = lax.all_to_all(summed, EVERYWHERE, 0, 0, tiled=True)
    adjoint = pl.pallas_call(
        functools.partial(back_kernel, rows, peers, slots),
        name="back",
        out_shape=jax.ShapeDtypeStruct((channels * rows, width), f32),
        in_specs=[vmem] + [far] * 6,
        out_specs=vmem,
        scratch_shapes=[
            pltpu.SMEM(source.shape, jnp.int32),
            pltpu.SMEM(count.shape, jnp.int32),
            pltpu.VMEM(diffusivity.shape, f32),
            pltpu.VMEM(tall, f32),
            pltpu.VMEM(tall, f32),
            pltpu.VMEM(tall, f32),
            pltpu.VMEM(kernels.shape, bf16),
            pltpu.SemaphoreType.DMA((5,)),
            pltpu.SemaphoreType.DMA((parts,)),
        ],
    )(near(returned), kernels, source, count, diffusivity, base, diffuse)
    first, bias_one, second, bias_two, third, bias_three = pl.pallas_call(
        functools.partial(unpack_kernel, share, small_share, fluxes),
        name="unpack",
        out_shape=(
            jax.ShapeDtypeStruct((inputs, hidden), f32),
            jax.ShapeDtypeStruct((1, hidden), f32),
            jax.ShapeDtypeStruct((hidden, hidden), f32),
            jax.ShapeDtypeStruct((1, hidden), f32),
            jax.ShapeDtypeStruct((fluxes, hidden), f32),
            jax.ShapeDtypeStruct((1, fluxes), f32),
        ),
        in_specs=[vmem],
        out_specs=(vmem,) * 6,
        scratch_shapes=[pltpu.VMEM((max(48, small_share * tiles), width), f32)],
    )(near(gathered))
    return (
        new_state.reshape(state.shape),
        adjoint.reshape(state.shape),
        first,
        bias_one[0],
        second,
        bias_two[0],
        third.T,
        bias_three[0],
    )


def near(array):
    return pltpu.with_memory_space_constraint(array, pltpu.VMEM)


def solution(mesh):
    tiles = P("comp", None, "gy", "gx")
    placed = (
        tiles,
        tiles,
        P("comp", "gy", "gx"),
        *(P() for _ in range(8)),
        P("comp", "gy", "gx", None, None, None, None),
        P("comp", "gy", "gx", None, None),
        P("comp", "gy", "gx", None, None),
        P("comp", "gy", "gx", None),
    )
    return jax.shard_map(
        shards,
        mesh=mesh,
        in_specs=placed,
        out_specs=(tiles, tiles, *(P() for _ in range(6))),
        check_vma=False,
    )
```

```python
import functools
import math

import jax
import jax.numpy as jnp
from jax import lax
from jax.experimental import pallas as pl
from jax.experimental.pallas import tpu as pltpu
from jax.sharding import PartitionSpec as P

EVERYWHERE = ("comp", "gy", "gx")
BLOCK_ROWS = 16
CHUNK = 256
FETCHED = 12
SMALL_PLANE = 3
SUBLANES = 8

KEYS = {
    "take": (0.0, 0.05),
    "first": (0, 0.267),
    "second": (0.3, 0.6),
    "third": (0.6, 0.65),
    "fields": (0.65, 1.0),
    "cot_second": (0.05, 0.3),
    "cot_first": (0.3, 0.6),
    "cot_inputs": (0.62, 0.7),
    "leave": (0.837, 1.099),
    "grad_second": 0.61,
    "grad_third": 0.749,
    "grad_first": 0.71,
}

OWN, OTHER, WEST, EAST, SOUTH, NORTH, COMP, HAS_SOUTH, HAS_NORTH, ON_FOLD = range(10)

f32 = jnp.float32
bf16 = jnp.bfloat16


def fetch_all(pairs, sems):
    copies = [
        pltpu.make_async_copy(src, dst, sems.at[i])
        for i, (src, dst) in enumerate(pairs)
    ]
    for copy in copies:
        copy.start()
    return copies


def side_by_side(ref, first, count, low, high):
    return jnp.concatenate([ref[first + i, low:high, :] for i in range(count)], axis=1)


def place():
    n_gy, n_gx = lax.axis_size("gy"), lax.axis_size("gx")
    comp, row, col = (lax.axis_index(axis) for axis in EVERYWHERE)
    tiles = n_gy * n_gx
    own = comp * tiles
    line = own + row * n_gx
    here = line + col
    is_top = row == n_gy - 1
    on_fold = jnp.logical_and(comp == 1, is_top)
    up = jnp.where(is_top, here, here + n_gx)
    return (
        own,
        (1 - comp) * tiles,
        line + lax.rem(col + (n_gx - 1), n_gx),
        line + lax.rem(col + 1, n_gx),
        jnp.where(row > 0, here - n_gx, here),
        jnp.where(on_fold, line + (n_gx - 1) - col, up),
        comp,
        (row > 0).astype(jnp.int32),
        jnp.logical_or(on_fold, jnp.logical_not(is_top)).astype(jnp.int32),
        on_fold.astype(jnp.int32),
    )


def dot(a, b):
    return jnp.dot(a, b, preferred_element_type=f32)


def dot_nt(a, b):
    return lax.dot_general(a, b, (((1,), (1,)), ((), ())), preferred_element_type=f32)


def mirror(tile):
    width = tile.shape[1]
    row = lax.broadcasted_iota(jnp.int32, (width, width), 0)
    col = lax.broadcasted_iota(jnp.int32, (width, width), 1)
    flip = (row + col == width - 1).astype(f32).astype(bf16)
    return dot(tile.astype(bf16), flip)


def put_edges(meta, first, last, bottom, top, stage):
    stage[meta[EAST], 0:SUBLANES, :] = last
    stage[meta[WEST], SUBLANES : 2 * SUBLANES, :] = first
    top = jnp.where(meta[ON_FOLD] == 1, mirror(top), top)
    straight = jnp.logical_and(meta[HAS_NORTH] == 1, meta[ON_FOLD] == 0)
    up = pl.multiple_of(jnp.where(straight, 0, 2 * SUBLANES), SUBLANES)
    down = pl.multiple_of(jnp.where(meta[HAS_SOUTH] == 1, SUBLANES, 2 * SUBLANES), SUBLANES)
    stage[meta[SOUTH], pl.ds(down, SUBLANES), :] = bottom
    stage[meta[NORTH], pl.ds(up, SUBLANES), :] = top


def take_edges(tile, r, lane, sides):
    width = tile.shape[1]
    here = lane == r
    first, last = sides
    first = jnp.where(here, pltpu.roll(tile, r, 1), first)
    last = jnp.where(here, pltpu.roll(tile, lax.rem(r + 1, width), 1), last)
    return first, last


def get_edges(meta, recv):
    west = recv[meta[WEST], 0 : 4 * SUBLANES, :].astype(f32)[0:SUBLANES]
    east = recv[meta[EAST], 0 : 4 * SUBLANES, :].astype(f32)[SUBLANES : 2 * SUBLANES]
    south = recv[meta[SOUTH], 0 : 4 * SUBLANES, :].astype(f32)[0:SUBLANES]
    above = recv[meta[NORTH], 0 : 4 * SUBLANES, :].astype(f32)
    north = jnp.where(
        meta[ON_FOLD] == 1,
        above[2 * SUBLANES : 3 * SUBLANES],
        above[SUBLANES : 2 * SUBLANES],
    )
    south = jnp.where(meta[HAS_SOUTH] == 1, south, 0.0)
    north = jnp.where(meta[HAS_NORTH] == 1, north, 0.0)
    return west, east, south, north


def laplace_row(here, below, above, west, east, r, lane):
    width = here.shape[1]
    left = jnp.where(
        lane == 0, pltpu.roll(west, lax.rem(width - r, width), 1), pltpu.roll(here, 1, 1)
    )
    right = jnp.where(
        lane == width - 1, pltpu.roll(east, width - 1 - r, 1), pltpu.roll(here, width - 1, 1)
    )
    return left + right + below + above - 4.0 * here


def column_of(row, comp):
    eye = (
        lax.broadcasted_iota(jnp.int32, (SUBLANES, SUBLANES), 0)
        == lax.broadcasted_iota(jnp.int32, (SUBLANES, SUBLANES), 1)
    ).astype(f32)
    return jnp.sum(
        jnp.broadcast_to(row[pl.ds(comp, 1), :], (SUBLANES, SUBLANES)) * eye,
        axis=1,
        keepdims=True,
    )


def send_kernel(
    rows, peers, slots, source_in, count_in, state_in, kernels, out, by_row, stage, blocks, sems,
    source, count, state, small_sems,
):
    meta = place()
    small = fetch_all([(state_in, state), (source_in, source), (count_in, count)], small_sems)
    width = state.shape[1]
    shape = (SUBLANES, width)
    sub = lax.broadcasted_iota(jnp.int32, shape, 0)
    parts = sems.shape[0]
    part = peers // parts
    copies = [
        pltpu.make_async_copy(
            kernels.at[pl.ds(i * part * slots, part * slots)],
            blocks.at[pl.ds(i * part * slots, part * slots)],
            sems.at[i],
        )
        for i in range(parts)
    ]
    for copy in copies:
        copy.start()
    stage[pl.ds(meta[OWN], peers)] = jnp.zeros((peers,) + stage.shape[1:], f32)

    for copy in small:
        copy.wait()

    def row_step(r, unused):
        by_row[r] = state[pl.ds(r, SUBLANES, stride=rows), :]
        return unused

    lax.fori_loop(0, rows, row_step, 0, unroll=32)
    wide = (16, width)
    which = lax.broadcasted_iota(jnp.int32, wide, 0)
    place_of = lax.broadcasted_iota(jnp.int32, wide, 1)
    unit = jnp.logical_or(
        jnp.logical_and(which == 0, place_of == 0),
        jnp.logical_and(which == 1, place_of == width - 1),
    )
    unit = unit.astype(f32).astype(bf16)
    first = jnp.zeros(shape, f32)
    last = jnp.zeros(shape, f32)
    for ch in range(SUBLANES):
        both = dot_nt(unit, state[ch * rows : (ch + 1) * rows, :].astype(bf16))
        first = jnp.where(sub == ch, jnp.broadcast_to(both[0:1], shape), first)
        last = jnp.where(sub == ch, jnp.broadcast_to(both[1:2], shape), last)
    put_edges(meta, first, last, by_row[0], by_row[rows - 1], stage)

    def peer_step(q, unused):
        for s in range(slots):
            k = q * slots + s
            picked = by_row[source[s, q]].astype(bf16)
            live = (s < count[q]).astype(f32)
            stage[meta[OTHER] + q, s * SUBLANES : (s + 1) * SUBLANES, :] = (
                dot(picked, blocks[k]) * live
            )
        return unused

    for i in range(parts):
        copies[i].wait()
        lax.fori_loop(i * part, (i + 1) * part, peer_step, 0, unroll=math.gcd(part, 4))
    out[...] = stage[...].astype(bf16)


def spread(low, high, step, count):
    return [
        (low + (high - low) * (i + 0.5) / count, functools.partial(step, i)) for i in range(count)
    ]


def weave(*lists):
    for entry in sorted((e for steps in lists for e in steps), key=lambda e: e[0]):
        entry[1]()


def main_kernel(
    rows,
    peers,
    slots,
    share,
    small_share,
    state,
    goal,
    recv,
    *refs,
):
    fetched, refs = refs[:FETCHED], refs[FETCHED:]
    (new_hbm, base_hbm, diffuse_hbm, send_out), refs = refs[:4], refs[4:]
    kept, refs = refs[:FETCHED], refs[FETCHED:]
    fetch_sems, store_sems, new_out, base_out, diffuse_out = refs[:5]
    copies = fetch_all(list(zip(fetched, kept, strict=True)), fetch_sems)
    main_steps(
        rows,
        peers,
        slots,
        share,
        small_share,
        copies,
        state,
        goal,
        recv,
        *kept,
        new_hbm,
        base_hbm,
        diffuse_hbm,
        send_out,
        store_sems,
        new_out,
        base_out,
        diffuse_out,
        *refs[5:],
    )


def main_steps(
    rows,
    peers,
    slots,
    share,
    small_share,
    copies,
    state,
    goal,
    recv,
    landing,
    b_out,
    mask,
    rate_ref,
    couple_ref,
    w_first,
    w_second,
    b_second,
    w_third,
    w_third_back,
    w_second_back,
    w_first_back,
    new_hbm,
    base_hbm,
    diffuse_hbm,
    send_out,
    store_sems,
    new_out,
    base_out,
    diffuse_out,
    stage,
    other,
    misfits,
    feats,
    hid_firsts,
    hid_seconds,
    slope_firsts,
    slope_seconds,
    flux_cots,
    cot_second,
    cot_first,
    flux,
    feat_cot,
    g_first,
    g_second,
    g_third,
    g_bias,
    edges,
    small,
):
    width = state.shape[2]
    hidden = w_second.shape[0]
    shape = (SUBLANES, width)
    cells = BLOCK_ROWS * width
    chunks = cells // CHUNK
    lane = lax.broadcasted_iota(jnp.int32, shape, 1)
    sub = lax.broadcasted_iota(jnp.int32, shape, 0)
    fluxes = couple_ref.shape[2]
    meta = place()
    slot_rows = recv.shape[1]
    assert 2 * small_share <= SUBLANES
    other[...] = jnp.zeros(other.shape, f32)
    misfits[...] = jnp.zeros(misfits.shape, f32)
    for copy in copies:
        copy.wait()

    def land(p, unused):
        block = recv[meta[OTHER] + p].astype(f32)
        for s in range(slots):
            row = landing[s, p]
            sums = (other, misfits)[s % 2]
            sums[row] = sums[row] + block[s * SUBLANES : (s + 1) * SUBLANES]
        return unused

    lax.fori_loop(0, peers, land, 0, unroll=4)
    west, east, south, north = get_edges(meta, recv)
    comp = meta[COMP]
    rate = jnp.broadcast_to(column_of(rate_ref, comp), shape)
    pairs = couple_ref[comp]
    couple = [jnp.broadcast_to(pairs[:, f : f + 1], shape) for f in range(fluxes)]
    ones = (lax.broadcasted_iota(jnp.int32, (16, width), 0) < 3).astype(f32).astype(bf16)
    lanes = CHUNK // width
    for ref in flux_cots:
        ref[...] = jnp.zeros(ref.shape, bf16)
    for ref in feats:
        for i in range(BLOCK_ROWS):
            ref[i, 16:32, :] = ones
    for ref in hid_firsts:
        for i in range(BLOCK_ROWS):
            ref[i, hidden : hidden + 16, :] = ones
    for ref in (g_first, g_second, g_third, g_bias, edges):
        ref[...] = jnp.zeros(ref.shape, f32)
    bias = jnp.broadcast_to(b_second[...], (hidden, CHUNK))
    b_third = jnp.zeros(shape, f32)
    for f in range(fluxes):
        b_third = jnp.where(sub == f, b_out[f], b_third)

    def forward(block, feat, hid_first, hid_second, slope_first, slope_second, flux_cot):
        start = block * BLOCK_ROWS

        def take(i):
            r = start + i
            landed = other[r] + misfits[r]
            feat[i, 0:16, :] = jnp.concatenate([state[r], landed], axis=0).astype(bf16)

        def layer(net, hid_ref, slope_ref, j):
            turn = jnp.tanh(net)
            up = 1.0 + turn
            hid = net * up
            slope = (up + hid) - hid * turn
            hid = hid.astype(bf16)
            for i in range(lanes):
                cols = slice(i * width, (i + 1) * width)
                hid_ref[j * lanes + i, 0:hidden, :] = hid[:, cols]
                slope_ref[j * lanes + i] = slope[:, cols]

        def first(j):
            net = dot(w_first[...], side_by_side(feat, j * lanes, lanes, 0, 32))
            layer(net, hid_first, slope_first, j)

        def second(j):
            net = dot(w_second[...], side_by_side(hid_first, j * lanes, lanes, 0, hidden)) + bias
            layer(net, hid_second, slope_second, j)

        def third(j):
            at = pl.ds(j * CHUNK, CHUNK)
            hid = side_by_side(hid_second, j * lanes, lanes, 0, hidden)
            flux[:, at] = dot(w_third[...], hid)[0:SUBLANES]

        def fields(i):
            at = pl.ds(i * width, width)
            r = start + i
            here = state[r]
            below = jnp.where(r > 0, state[jnp.maximum(r - 1, 0)], south)
            above = jnp.where(r < rows - 1, state[jnp.minimum(r + 1, rows - 1)], north)
            lap = laplace_row(here, below, above, west, east, r, lane)
            wet = jnp.broadcast_to(mask[pl.ds(r, 1), :].astype(f32), shape)
            spread_mask = jnp.where(comp == 1, wet, 1.0)
            wet_flux = (flux[:, at] + b_third) * wet
            updated = here + rate * spread_mask * lap
            for f in range(fluxes):
                updated = updated + couple[f] * jnp.broadcast_to(wet_flux[f : f + 1], shape)
            new_out[pl.ds(r, SUBLANES, stride=rows), :] = updated
            misfit = updated - goal[pl.ds(r, SUBLANES, stride=rows), :]
            diffuse = spread_mask * misfit
            diffuse_out[r] = diffuse
            edges[0], edges[1] = take_edges(diffuse, r, lane, (edges[0], edges[1]))
            misfits[r] = misfit
            pulled = jnp.zeros(shape, f32)
            for f in range(fluxes):
                total = jnp.sum(couple[f] * misfit, axis=0, keepdims=True)
                pulled = jnp.where(sub == f, jnp.broadcast_to(total, shape), pulled)
            pulled = (pulled * wet).astype(bf16)
            flux_cot[i, 0:SUBLANES, :] = pulled
            g_bias[...] = g_bias[...] + pulled.astype(f32)

        return (
            spread(*KEYS["take"], take, BLOCK_ROWS)
            + spread(*KEYS["first"], first, chunks)
            + spread(*KEYS["second"], second, chunks)
            + spread(*KEYS["third"], third, chunks)
            + spread(*KEYS["fields"], fields, BLOCK_ROWS)
        )

    def backward(block, feat, hid_first, hid_second, slope_first, slope_second, flux_cot):
        start = block * BLOCK_ROWS

        def pull(net, slope_ref, cot_ref, j):
            for i in range(lanes):
                cols = slice(i * width, (i + 1) * width)
                cot_ref[j * lanes + i] = (net[:, cols] * slope_ref[j * lanes + i]).astype(bf16)

        def second(j):
            net = dot(w_third_back[...], side_by_side(flux_cot, j * lanes, lanes, 0, 16))
            pull(net, slope_second, cot_second, j)

        def first(j):
            net = dot(w_second_back[...], side_by_side(cot_second, j * lanes, lanes, 0, hidden))
            pull(net, slope_first, cot_first, j)

        def inputs(j):
            at = pl.ds(j * CHUNK, CHUNK)
            cot = side_by_side(cot_first, j * lanes, lanes, 0, hidden)
            feat_cot[:, at] = dot(w_first_back[...], cot)

        def whole(ref):
            return side_by_side(ref, 0, BLOCK_ROWS, 0, ref.shape[1])

        def leave(i):
            at = pl.ds(i * width, width)
            r = start + i
            base_out[r] = misfits[r] + feat_cot[0:SUBLANES, at]
            other[r] = feat_cot[SUBLANES : 2 * SUBLANES, at]

        def grad_second():
            g_second[...] += dot_nt(whole(hid_first), whole(cot_second))

        def grad_third():
            g_third[...] += dot_nt(whole(flux_cot), whole(hid_second))

        def grad_first():
            g_first[...] += dot_nt(whole(feat), whole(cot_first))

        return (
            spread(*KEYS["cot_second"], second, chunks)
            + spread(*KEYS["cot_first"], first, chunks)
            + spread(*KEYS["cot_inputs"], inputs, chunks)
            + spread(*KEYS["leave"], leave, BLOCK_ROWS)
            + [
                (KEYS["grad_second"], grad_second),
                (KEYS["grad_third"], grad_third),
                (KEYS["grad_first"], grad_first),
            ]
        )

    sets = list(
        zip(feats, hid_firsts, hid_seconds, slope_firsts, slope_seconds, flux_cots, strict=True)
    )
    blocks = rows // BLOCK_ROWS

    def beside(block, this, that):
        weave(backward(block, *this), forward(block + 1, *that))

    def pair_step(pair, unused):
        beside(2 * pair, *sets)
        beside(2 * pair + 1, *sets[::-1])
        return unused

    weave(forward(0, *sets[0]))
    lax.fori_loop(0, blocks // 2 - 1, pair_step, 0)
    beside(blocks - 2, *sets)
    ready = rows - BLOCK_ROWS
    stores = fetch_all(
        [
            (new_out, new_hbm),
            (diffuse_out, diffuse_hbm),
            (base_out.at[pl.ds(0, ready)], base_hbm.at[pl.ds(0, ready)]),
        ],
        store_sems,
    )
    weave(backward(blocks - 1, *sets[1]))
    rest = pltpu.make_async_copy(
        base_out.at[pl.ds(ready, BLOCK_ROWS)],
        base_hbm.at[pl.ds(ready, BLOCK_ROWS)],
        store_sems.at[3],
    )
    rest.start()
    stage[pl.ds(meta[OWN], peers), 0:slot_rows, :] = jnp.zeros((peers, slot_rows, width), f32)

    def leave(p, unused):
        for s in range(slots):
            row = landing[s, p]
            stage[meta[OTHER] + p, s * SUBLANES : (s + 1) * SUBLANES, :] = other[row]
        return unused

    lax.fori_loop(0, peers, leave, 0, unroll=2)
    put_edges(meta, edges[0], edges[1], diffuse_out[0], diffuse_out[rows - 1], stage)
    devices = stage.shape[0]
    halves = hidden // width
    inputs = 2 * SUBLANES
    small[...] = jnp.zeros(small.shape, f32)
    low, high = g_first[0:SUBLANES, :], g_first[SUBLANES:inputs, :]
    low, high = jnp.where(comp == 1, high, low), jnp.where(comp == 1, low, high)
    bias_sum = jnp.sum(g_bias[...], axis=1, keepdims=True)
    bias_row = jnp.sum(jnp.where(sub == lane, jnp.broadcast_to(bias_sum, shape), 0.0), axis=0,
                       keepdims=True)
    for h in range(halves):
        cols = slice(h * width, (h + 1) * width)
        top = h * 24
        small[top : top + 8, :] = low[:, cols]
        small[top + 8 : top + 16, :] = high[:, cols]
        small[top + 16 : top + 17, :] = g_first[inputs : inputs + 1, cols]
        small[top + 17 : top + 18, :] = g_second[hidden : hidden + 1, cols]
        if h == 0:
            small[top + 18 : top + 19, :] = bias_row
        small[top + 19 : top + 19 + fluxes, :] = g_third[0:fluxes, cols]
    for d in range(devices):
        done = 0
        while done < share:
            at = d * share + done
            h, row = divmod(at, hidden)
            step = min(share - done, hidden - row)
            if h < halves:
                stage[d, slot_rows + done : slot_rows + done + step, :] = g_second[
                    row : row + step, h * width : (h + 1) * width
                ]
            done += step
    top = SMALL_PLANE * SUBLANES
    for p in range(peers):
        piece = small[p * small_share : (p + 1) * small_share, :]
        head = piece.astype(bf16).astype(f32)
        stage[meta[OWN] + p, top : top + small_share, :] = head
        stage[meta[OWN] + p, top + small_share : top + 2 * small_share, :] = piece - head
    send_out[...] = stage[...].astype(bf16)
    for copy in (*stores, rest):
        copy.wait()


def sum_kernel(scale, peers, share, small_share, recv, out, stage):
    devices = recv.shape[0]
    own = lax.axis_index("comp") * peers
    slot_rows = 4 * SUBLANES
    planes = slice(SMALL_PLANE * SUBLANES, (SMALL_PLANE + 1) * SUBLANES)
    at = slice(slot_rows, slot_rows + -(-share // SUBLANES) * SUBLANES)
    total = recv[0, at, :].astype(f32)
    for d in range(1, devices):
        total = total + recv[d, at, :].astype(f32)
    part = recv[own, planes, :].astype(f32)
    for p in range(1, peers):
        part = part + recv[own + p, planes, :].astype(f32)
    part = part * scale
    piece = part[0:small_share] + part[small_share : 2 * small_share]
    head = piece.astype(bf16).astype(f32)
    stage[0:share, :] = total[0:share] * scale
    stage[share : share + small_share, :] = head
    stage[share + small_share : share + 2 * small_share, :] = piece - head
    total = stage[...].astype(bf16)
    for d in range(devices):
        out[d] = total


def back_kernel(
    rows, peers, slots, recv, kernels, source_in, count_in, rate_in, base_in, diffuse_in, out,
    source, count, rate_ref, base, diffuse, total, blocks, sems, block_sems,
):
    meta = place()
    copies = fetch_all(
        [
            (diffuse_in, diffuse),
            (base_in, base),
            (source_in, source),
            (count_in, count),
            (rate_in, rate_ref),
        ],
        sems,
    )
    parts = block_sems.shape[0]
    part = peers // parts
    steps = [pl.ds(i * part * slots, part * slots) for i in range(parts)]
    block_copies = fetch_all([(kernels.at[at], blocks.at[at]) for at in steps], block_sems)
    for copy in copies:
        copy.wait()
    width = diffuse.shape[2]
    shape = (SUBLANES, width)
    lane = lax.broadcasted_iota(jnp.int32, shape, 1)
    west, east, south, north = get_edges(meta, recv)
    comp = meta[COMP]
    rate = jnp.broadcast_to(column_of(rate_ref, comp), shape)

    def lap_step(r, unused):
        here = diffuse[r]
        below = jnp.where(r > 0, diffuse[jnp.maximum(r - 1, 0)], south)
        above = jnp.where(r < rows - 1, diffuse[jnp.minimum(r + 1, rows - 1)], north)
        total[r] = base[r] + rate * laplace_row(here, below, above, west, east, r, lane)
        return unused

    lax.fori_loop(0, rows, lap_step, 0, unroll=32)

    def peer_step(q, unused):
        block = recv[meta[OTHER] + q, 0 : slots * SUBLANES, :].astype(f32)
        for s in range(slots):
            k = q * slots + s
            sent = block[s * SUBLANES : (s + 1) * SUBLANES].astype(bf16)
            live = (s < count[q]).astype(f32)
            row = source[s, q]
            total[row] = total[row] + dot_nt(sent, blocks[k]) * live
        return unused

    for i in range(parts):
        block_copies[i].wait()
        lax.fori_loop(i * part, (i + 1) * part, peer_step, 0, unroll=math.gcd(part, 4))

    def out_step(r, unused):
        out[pl.ds(r, SUBLANES, stride=rows), :] = total[r]
        return unused

    lax.fori_loop(0, rows, out_step, 0, unroll=32)


def unpack_kernel(share, small_share, fluxes, recv, first, bias_one, second, bias_two, third,
                  bias_three, small):
    devices = recv.shape[0]
    peers = devices // 2
    width = recv.shape[2]
    hidden = second.shape[0]
    halves = hidden // width
    for d in range(devices):
        block = recv[d].astype(f32)
        done = 0
        while done < share:
            at = d * share + done
            h, row = divmod(at, hidden)
            step = min(share - done, hidden - row)
            if h < halves:
                second[row : row + step, h * width : (h + 1) * width] = block[done : done + step]
            done += step
        piece = (
            block[share : share + small_share]
            + block[share + small_share : share + 2 * small_share]
        )
        at = d % peers * small_share
        if d >= peers:
            piece = piece + small[at : at + small_share, :]
        small[at : at + small_share, :] = piece
    for h in range(halves):
        cols = slice(h * width, (h + 1) * width)
        top = h * 24
        first[:, cols] = small[top : top + 16, :]
        bias_one[:, cols] = small[top + 16 : top + 17, :]
        bias_two[:, cols] = small[top + 17 : top + 18, :]
        third[:, cols] = small[top + 19 : top + 19 + fluxes, :]
    bias_three[...] = small[18:19, 0:fluxes]


def shards(
    state,
    target,
    land_mask,
    diffusivity,
    coupling,
    w_in,
    b_in,
    w_mid,
    b_mid,
    w_out,
    b_out,
    remap_weight,
    remap_source,
    remap_target,
    remap_count,
):
    n_gy, n_gx = lax.axis_size("gy"), lax.axis_size("gx")
    tiles = n_gy * n_gx
    devices = 2 * tiles
    comp = lax.axis_index("comp")
    channels, rows, width = state.shape[1:]
    hidden = w_mid.shape[0]
    inputs = w_in.shape[0]
    fluxes = w_out.shape[1]
    peers, slots = remap_source.shape[3:]
    surface = state.reshape(channels * rows, width)
    goal = target.reshape(channels * rows, width)
    mask = land_mask[0]
    source = remap_source.reshape(peers, slots).T
    landing = remap_target.reshape(peers, slots).T
    count = remap_count.reshape(peers)
    kernels = remap_weight.reshape(peers * slots, width, width)
    slot_rows = slots * channels

    vmem = pl.BlockSpec(memory_space=pltpu.VMEM)

    far = pl.BlockSpec(memory_space=pltpu.HBM)
    parts = math.gcd(peers, 4)
    outgoing, by_row = pl.pallas_call(
        functools.partial(send_kernel, rows, peers, slots),
        name="send",
        out_shape=(
            jax.ShapeDtypeStruct((devices, slot_rows, width), bf16),
            jax.ShapeDtypeStruct((rows, channels, width), f32),
        ),
        in_specs=[far] * 4,
        out_specs=(vmem, vmem),
        scratch_shapes=[
            pltpu.VMEM((devices, slot_rows, width), f32),
            pltpu.VMEM(kernels.shape, bf16),
            pltpu.SemaphoreType.DMA((parts,)),
            pltpu.SMEM(source.shape, jnp.int32),
            pltpu.SMEM(count.shape, jnp.int32),
            pltpu.VMEM(surface.shape, f32),
            pltpu.SemaphoreType.DMA((3,)),
        ],
    )(source, count, surface, kernels)
    arrived = lax.all_to_all(outgoing, EVERYWHERE, 0, 0, tiled=True)

    def pieces(bias):
        high = bias.astype(bf16)
        rest = bias - high.astype(f32)
        middle = rest.astype(bf16)
        low = (rest - middle.astype(f32)).astype(bf16)
        return jnp.stack([high, middle, low], axis=0)

    local_in = jnp.where(comp == 1, jnp.roll(w_in, channels, axis=0), w_in)
    half = jnp.asarray(0.5, bf16)
    w_first = jnp.concatenate(
        [local_in, pieces(b_in), jnp.zeros((13, hidden), bf16)], axis=0
    ).T * half
    w_second = w_mid.T * half
    b_second = (b_mid * 0.5)[:, None]
    w_third = jnp.pad(w_out.T, ((0, 16 - fluxes), (0, 0)))
    w_third_back = jnp.pad(w_out * half, ((0, 0), (0, 16 - fluxes)))
    w_second_back = w_mid * half
    w_first_back = local_in

    share = -(-hidden * hidden // (width * devices))
    small_share = -(-24 * hidden // (width * tiles))
    sent = -(-share // 8) * 8
    packed = -(-(share + 2 * small_share) // 8) * 8
    cells = BLOCK_ROWS * width

    def twice(*args):
        return (pltpu.VMEM(*args), pltpu.VMEM(*args))

    tall = (rows, channels, width)
    tables = (
        mask,
        diffusivity,
        coupling,
        w_first,
        w_second,
        b_second,
        w_third,
        w_third_back,
        w_second_back,
        w_first_back,
    )
    new_state, base, diffuse, leaving = pl.pallas_call(
        functools.partial(main_kernel, rows, peers, slots, share, small_share),
        name="main",
        out_shape=(
            jax.ShapeDtypeStruct((channels * rows, width), f32),
            jax.ShapeDtypeStruct(tall, f32),
            jax.ShapeDtypeStruct((rows, channels, width), f32),
            jax.ShapeDtypeStruct((devices, slot_rows + sent, width), bf16),
        ),
        in_specs=[vmem] * 3 + [far] * FETCHED,
        out_specs=(far,) * 3 + (vmem,),
        scratch_shapes=[
            pltpu.SMEM(landing.shape, jnp.int32),
            pltpu.SMEM(b_out.shape, f32),
            *(pltpu.VMEM(array.shape, array.dtype) for array in tables),
            pltpu.SemaphoreType.DMA((FETCHED,)),
            pltpu.SemaphoreType.DMA((4,)),
            pltpu.VMEM((channels * rows, width), f32),
            pltpu.VMEM(tall, f32),
            pltpu.VMEM((rows, channels, width), f32),
            pltpu.VMEM((devices, slot_rows + sent, width), f32),
            pltpu.VMEM(tall, f32),
            pltpu.VMEM(tall, f32),
            twice((BLOCK_ROWS, 32, width), bf16),
            twice((BLOCK_ROWS, hidden + 16, width), bf16),
            twice((BLOCK_ROWS, hidden, width), bf16),
            twice((BLOCK_ROWS, hidden, width), f32),
            twice((BLOCK_ROWS, hidden, width), f32),
            twice((BLOCK_ROWS, 16, width), bf16),
            pltpu.VMEM((BLOCK_ROWS, hidden, width), bf16),
            pltpu.VMEM((BLOCK_ROWS, hidden, width), bf16),
            pltpu.VMEM((8, cells), f32),
            pltpu.VMEM((16, cells), f32),
            pltpu.VMEM((32, hidden), f32),
            pltpu.VMEM((hidden + 16, hidden), f32),
            pltpu.VMEM((16, hidden), f32),
            pltpu.VMEM((8, width), f32),
            pltpu.VMEM((2, 8, width), f32),
            pltpu.VMEM((max(48, small_share * tiles), width), f32),
        ],
    )(
        near(by_row),
        near(goal),
        near(arrived),
        landing,
        b_out,
        *tables,
    )
    returned = lax.all_to_all(leaving, EVERYWHERE, 0, 0, tiled=True)
    scale = 1.0 / (rows * width * tiles)
    summed = pl.pallas_call(
        functools.partial(sum_kernel, scale, peers, share, small_share),
        name="sum",
        out_shape=jax.ShapeDtypeStruct((devices, packed, width), bf16),
        in_specs=[vmem],
        out_specs=vmem,
        scratch_shapes=[pltpu.VMEM((packed, width), f32)],
    )(near(returned))
    gathered = lax.all_to_all(summed, EVERYWHERE, 0, 0, tiled=True)
    adjoint = pl.pallas_call(
        functools.partial(back_kernel, rows, peers, slots),
        name="back",
        out_shape=jax.ShapeDtypeStruct((channels * rows, width), f32),
        in_specs=[vmem] + [far] * 6,
        out_specs=vmem,
        scratch_shapes=[
            pltpu.SMEM(source.shape, jnp.int32),
            pltpu.SMEM(count.shape, jnp.int32),
            pltpu.VMEM(diffusivity.shape, f32),
            pltpu.VMEM(tall, f32),
            pltpu.VMEM(tall, f32),
            pltpu.VMEM(tall, f32),
            pltpu.VMEM(kernels.shape, bf16),
            pltpu.SemaphoreType.DMA((5,)),
            pltpu.SemaphoreType.DMA((parts,)),
        ],
    )(near(returned), kernels, source, count, diffusivity, base, diffuse)
    first, bias_one, second, bias_two, third, bias_three = pl.pallas_call(
        functools.partial(unpack_kernel, share, small_share, fluxes),
        name="unpack",
        out_shape=(
            jax.ShapeDtypeStruct((inputs, hidden), f32),
            jax.ShapeDtypeStruct((1, hidden), f32),
            jax.ShapeDtypeStruct((hidden, hidden), f32),
            jax.ShapeDtypeStruct((1, hidden), f32),
            jax.ShapeDtypeStruct((fluxes, hidden), f32),
            jax.ShapeDtypeStruct((1, fluxes), f32),
        ),
        in_specs=[vmem],
        out_specs=(vmem,) * 6,
        scratch_shapes=[pltpu.VMEM((max(48, small_share * tiles), width), f32)],
    )(near(gathered))
    return (
        new_state.reshape(state.shape),
        adjoint.reshape(state.shape),
        first,
        bias_one[0],
        second,
        bias_two[0],
        third.T,
        bias_three[0],
    )


def near(array):
    return pltpu.with_memory_space_constraint(array, pltpu.VMEM)


def solution(mesh):
    tiles = P("comp", None, "gy", "gx")
    placed = (
        tiles,
        tiles,
        P("comp", "gy", "gx"),
        *(P() for _ in range(8)),
        P("comp", "gy", "gx", None, None, None, None),
        P("comp", "gy", "gx", None, None),
        P("comp", "gy", "gx", None, None),
        P("comp", "gy", "gx", None),
    )
    return jax.shard_map(
        shards,
        mesh=mesh,
        in_specs=placed,
        out_specs=(tiles, tiles, *(P() for _ in range(6))),
        check_vma=False,
    )
```

```python
import functools
import math

import jax
import jax.numpy as jnp
from jax import lax
from jax.experimental import pallas as pl
from jax.experimental.pallas import tpu as pltpu
from jax.sharding import PartitionSpec as P

EVERYWHERE = ("comp", "gy", "gx")
BLOCK_ROWS = 16
CHUNK = 256
FETCHED = 12
SMALL_PLANE = 3
SUBLANES = 8

KEYS = {
    "take": (0.0, 0.05),
    "first": (0, 0.267),
    "second": (0.3, 0.6),
    "third": (0.6, 0.65),
    "fields": (0.65, 1.0),
    "cot_second": (0.05, 0.3),
    "cot_first": (0.3, 0.6),
    "cot_inputs": (0.62, 0.7),
    "leave": (0.837, 1.099),
    "grad_second": 0.61,
    "grad_third": 0.749,
    "grad_first": 0.71,
}

OWN, OTHER, WEST, EAST, SOUTH, NORTH, COMP, HAS_SOUTH, HAS_NORTH, ON_FOLD = range(10)

f32 = jnp.float32
bf16 = jnp.bfloat16


def fetch_all(pairs, sems):
    copies = [
        pltpu.make_async_copy(src, dst, sems.at[i])
        for i, (src, dst) in enumerate(pairs)
    ]
    for copy in copies:
        copy.start()
    return copies


def side_by_side(ref, first, count, low, high):
    return jnp.concatenate([ref[first + i, low:high, :] for i in range(count)], axis=1)


def place():
    n_gy, n_gx = lax.axis_size("gy"), lax.axis_size("gx")
    comp, row, col = (lax.axis_index(axis) for axis in EVERYWHERE)
    tiles = n_gy * n_gx
    own = comp * tiles
    line = own + row * n_gx
    here = line + col
    is_top = row == n_gy - 1
    on_fold = jnp.logical_and(comp == 1, is_top)
    up = jnp.where(is_top, here, here + n_gx)
    return (
        own,
        (1 - comp) * tiles,
        line + lax.rem(col + (n_gx - 1), n_gx),
        line + lax.rem(col + 1, n_gx),
        jnp.where(row > 0, here - n_gx, here),
        jnp.where(on_fold, line + (n_gx - 1) - col, up),
        comp,
        (row > 0).astype(jnp.int32),
        jnp.logical_or(on_fold, jnp.logical_not(is_top)).astype(jnp.int32),
        on_fold.astype(jnp.int32),
    )


def dot(a, b):
    return jnp.dot(a, b, preferred_element_type=f32)


def dot_nt(a, b):
    return lax.dot_general(a, b, (((1,), (1,)), ((), ())), preferred_element_type=f32)


def mirror(tile):
    width = tile.shape[1]
    row = lax.broadcasted_iota(jnp.int32, (width, width), 0)
    col = lax.broadcasted_iota(jnp.int32, (width, width), 1)
    flip = (row + col == width - 1).astype(f32).astype(bf16)
    return dot(tile.astype(bf16), flip)


def put_edges(meta, first, last, bottom, top, stage):
    stage[meta[EAST], 0:SUBLANES, :] = last
    stage[meta[WEST], SUBLANES : 2 * SUBLANES, :] = first
    top = jnp.where(meta[ON_FOLD] == 1, mirror(top), top)
    straight = jnp.logical_and(meta[HAS_NORTH] == 1, meta[ON_FOLD] == 0)
    up = pl.multiple_of(jnp.where(straight, 0, 2 * SUBLANES), SUBLANES)
    down = pl.multiple_of(jnp.where(meta[HAS_SOUTH] == 1, SUBLANES, 2 * SUBLANES), SUBLANES)
    stage[meta[SOUTH], pl.ds(down, SUBLANES), :] = bottom
    stage[meta[NORTH], pl.ds(up, SUBLANES), :] = top


def take_edges(tile, r, lane, sides):
    width = tile.shape[1]
    here = lane == r
    first, last = sides
    first = jnp.where(here, pltpu.roll(tile, r, 1), first)
    last = jnp.where(here, pltpu.roll(tile, lax.rem(r + 1, width), 1), last)
    return first, last


def get_edges(meta, recv):
    west = recv[meta[WEST], 0 : 4 * SUBLANES, :].astype(f32)[0:SUBLANES]
    east = recv[meta[EAST], 0 : 4 * SUBLANES, :].astype(f32)[SUBLANES : 2 * SUBLANES]
    south = recv[meta[SOUTH], 0 : 4 * SUBLANES, :].astype(f32)[0:SUBLANES]
    above = recv[meta[NORTH], 0 : 4 * SUBLANES, :].astype(f32)
    north = jnp.where(
        meta[ON_FOLD] == 1,
        above[2 * SUBLANES : 3 * SUBLANES],
        above[SUBLANES : 2 * SUBLANES],
    )
    south = jnp.where(meta[HAS_SOUTH] == 1, south, 0.0)
    north = jnp.where(meta[HAS_NORTH] == 1, north, 0.0)
    return west, east, south, north


def laplace_row(here, below, above, west, east, r, lane):
    width = here.shape[1]
    left = jnp.where(
        lane == 0, pltpu.roll(west, lax.rem(width - r, width), 1), pltpu.roll(here, 1, 1)
    )
    right = jnp.where(
        lane == width - 1, pltpu.roll(east, width - 1 - r, 1), pltpu.roll(here, width - 1, 1)
    )
    return left + right + below + above - 4.0 * here


def column_of(row, comp):
    eye = (
        lax.broadcasted_iota(jnp.int32, (SUBLANES, SUBLANES), 0)
        == lax.broadcasted_iota(jnp.int32, (SUBLANES, SUBLANES), 1)
    ).astype(f32)
    return jnp.sum(
        jnp.broadcast_to(row[pl.ds(comp, 1), :], (SUBLANES, SUBLANES)) * eye,
        axis=1,
        keepdims=True,
    )


def send_kernel(
    rows, peers, slots, source_in, count_in, state_in, kernels, out, by_row, stage, blocks, sems,
    source, count, state, small_sems,
):
    meta = place()
    small = fetch_all([(state_in, state), (source_in, source), (count_in, count)], small_sems)
    width = state.shape[1]
    shape = (SUBLANES, width)
    sub = lax.broadcasted_iota(jnp.int32, shape, 0)
    parts = sems.shape[0]
    part = peers // parts
    copies = [
        pltpu.make_async_copy(
            kernels.at[pl.ds(i * part * slots, part * slots)],
            blocks.at[pl.ds(i * part * slots, part * slots)],
            sems.at[i],
        )
        for i in range(parts)
    ]
    for copy in copies:
        copy.start()
    stage[pl.ds(meta[OWN], peers)] = jnp.zeros((peers,) + stage.shape[1:], f32)

    for copy in small:
        copy.wait()

    def row_step(r, unused):
        by_row[r] = state[pl.ds(r, SUBLANES, stride=rows), :]
        return unused

    lax.fori_loop(0, rows, row_step, 0, unroll=32)
    wide = (16, width)
    which = lax.broadcasted_iota(jnp.int32, wide, 0)
    place_of = lax.broadcasted_iota(jnp.int32, wide, 1)
    unit = jnp.logical_or(
        jnp.logical_and(which == 0, place_of == 0),
        jnp.logical_and(which == 1, place_of == width - 1),
    )
    unit = unit.astype(f32).astype(bf16)
    first = jnp.zeros(shape, f32)
    last = jnp.zeros(shape, f32)
    for ch in range(SUBLANES):
        both = dot_nt(unit, state[ch * rows : (ch + 1) * rows, :].astype(bf16))
        first = jnp.where(sub == ch, jnp.broadcast_to(both[0:1], shape), first)
        last = jnp.where(sub == ch, jnp.broadcast_to(both[1:2], shape), last)
    put_edges(meta, first, last, by_row[0], by_row[rows - 1], stage)

    def peer_step(q, unused):
        for s in range(slots):
            k = q * slots + s
            picked = by_row[source[s, q]].astype(bf16)
            live = (s < count[q]).astype(f32)
            stage[meta[OTHER] + q, s * SUBLANES : (s + 1) * SUBLANES, :] = (
                dot(picked, blocks[k]) * live
            )
        return unused

    for i in range(parts):
        copies[i].wait()
        lax.fori_loop(i * part, (i + 1) * part, peer_step, 0, unroll=math.gcd(part, 4))
    out[...] = stage[...].astype(bf16)


def spread(low, high, step, count):
    return [
        (low + (high - low) * (i + 0.5) / count, functools.partial(step, i)) for i in range(count)
    ]


def weave(*lists):
    for entry in sorted((e for steps in lists for e in steps), key=lambda e: e[0]):
        entry[1]()


def main_kernel(
    rows,
    peers,
    slots,
    share,
    small_share,
    state,
    goal,
    recv,
    *refs,
):
    fetched, refs = refs[:FETCHED], refs[FETCHED:]
    (new_hbm, base_hbm, diffuse_hbm, send_out), refs = refs[:4], refs[4:]
    kept, refs = refs[:FETCHED], refs[FETCHED:]
    fetch_sems, store_sems, new_out, base_out, diffuse_out = refs[:5]
    copies = fetch_all(list(zip(fetched, kept, strict=True)), fetch_sems)
    main_steps(
        rows,
        peers,
        slots,
        share,
        small_share,
        copies,
        state,
        goal,
        recv,
        *kept,
        new_hbm,
        base_hbm,
        diffuse_hbm,
        send_out,
        store_sems,
        new_out,
        base_out,
        diffuse_out,
        *refs[5:],
    )


def main_steps(
    rows,
    peers,
    slots,
    share,
    small_share,
    copies,
    state,
    goal,
    recv,
    landing,
    b_out,
    mask,
    rate_ref,
    couple_ref,
    w_first,
    w_second,
    b_second,
    w_third,
    w_third_back,
    w_second_back,
    w_first_back,
    new_hbm,
    base_hbm,
    diffuse_hbm,
    send_out,
    store_sems,
    new_out,
    base_out,
    diffuse_out,
    stage,
    other,
    misfits,
    feats,
    hid_firsts,
    hid_seconds,
    slope_firsts,
    slope_seconds,
    flux_cots,
    cot_second,
    cot_first,
    flux,
    feat_cot,
    g_first,
    g_second,
    g_third,
    g_bias,
    edges,
    small,
):
    width = state.shape[2]
    hidden = w_second.shape[0]
    shape = (SUBLANES, width)
    cells = BLOCK_ROWS * width
    chunks = cells // CHUNK
    lane = lax.broadcasted_iota(jnp.int32, shape, 1)
    sub = lax.broadcasted_iota(jnp.int32, shape, 0)
    fluxes = couple_ref.shape[2]
    meta = place()
    slot_rows = recv.shape[1]
    assert 2 * small_share <= SUBLANES
    other[...] = jnp.zeros(other.shape, f32)
    misfits[...] = jnp.zeros(misfits.shape, f32)
    for copy in copies:
        copy.wait()

    def land(p, unused):
        block = recv[meta[OTHER] + p].astype(f32)
        for s in range(slots):
            row = landing[s, p]
            sums = (other, misfits)[s % 2]
            sums[row] = sums[row] + block[s * SUBLANES : (s + 1) * SUBLANES]
        return unused

    lax.fori_loop(0, peers, land, 0, unroll=4)
    west, east, south, north = get_edges(meta, recv)
    comp = meta[COMP]
    rate = jnp.broadcast_to(column_of(rate_ref, comp), shape)
    pairs = couple_ref[comp]
    couple = [jnp.broadcast_to(pairs[:, f : f + 1], shape) for f in range(fluxes)]
    ones = (lax.broadcasted_iota(jnp.int32, (16, width), 0) < 3).astype(f32).astype(bf16)
    lanes = CHUNK // width
    for ref in flux_cots:
        ref[...] = jnp.zeros(ref.shape, bf16)
    for ref in feats:
        for i in range(BLOCK_ROWS):
            ref[i, 16:32, :] = ones
    for ref in hid_firsts:
        for i in range(BLOCK_ROWS):
            ref[i, hidden : hidden + 16, :] = ones
    for ref in (g_first, g_second, g_third, g_bias, edges):
        ref[...] = jnp.zeros(ref.shape, f32)
    bias = jnp.broadcast_to(b_second[...], (hidden, CHUNK))
    b_third = jnp.zeros(shape, f32)
    for f in range(fluxes):
        b_third = jnp.where(sub == f, b_out[f], b_third)

    def forward(block, feat, hid_first, hid_second, slope_first, slope_second, flux_cot):
        start = block * BLOCK_ROWS

        def take(i):
            r = start + i
            landed = other[r] + misfits[r]
            feat[i, 0:16, :] = jnp.concatenate([state[r], landed], axis=0).astype(bf16)

        def layer(net, hid_ref, slope_ref, j):
            turn = jnp.tanh(net)
            up = 1.0 + turn
            hid = net * up
            slope = (up + hid) - hid * turn
            hid = hid.astype(bf16)
            for i in range(lanes):
                cols = slice(i * width, (i + 1) * width)
                hid_ref[j * lanes + i, 0:hidden, :] = hid[:, cols]
                slope_ref[j * lanes + i] = slope[:, cols]

        def first(j):
            net = dot(w_first[...], side_by_side(feat, j * lanes, lanes, 0, 32))
            layer(net, hid_first, slope_first, j)

        def second(j):
            net = dot(w_second[...], side_by_side(hid_first, j * lanes, lanes, 0, hidden)) + bias
            layer(net, hid_second, slope_second, j)

        def third(j):
            at = pl.ds(j * CHUNK, CHUNK)
            hid = side_by_side(hid_second, j * lanes, lanes, 0, hidden)
            flux[:, at] = dot(w_third[...], hid)[0:SUBLANES]

        def fields(i):
            at = pl.ds(i * width, width)
            r = start + i
            here = state[r]
            below = jnp.where(r > 0, state[jnp.maximum(r - 1, 0)], south)
            above = jnp.where(r < rows - 1, state[jnp.minimum(r + 1, rows - 1)], north)
            lap = laplace_row(here, below, above, west, east, r, lane)
            wet = jnp.broadcast_to(mask[pl.ds(r, 1), :].astype(f32), shape)
            spread_mask = jnp.where(comp == 1, wet, 1.0)
            wet_flux = (flux[:, at] + b_third) * wet
            updated = here + rate * spread_mask * lap
            for f in range(fluxes):
                updated = updated + couple[f] * jnp.broadcast_to(wet_flux[f : f + 1], shape)
            new_out[pl.ds(r, SUBLANES, stride=rows), :] = updated
            misfit = updated - goal[pl.ds(r, SUBLANES, stride=rows), :]
            diffuse = spread_mask * misfit
            diffuse_out[r] = diffuse
            edges[0], edges[1] = take_edges(diffuse, r, lane, (edges[0], edges[1]))
            misfits[r] = misfit
            pulled = jnp.zeros(shape, f32)
            for f in range(fluxes):
                total = jnp.sum(couple[f] * misfit, axis=0, keepdims=True)
                pulled = jnp.where(sub == f, jnp.broadcast_to(total, shape), pulled)
            pulled = (pulled * wet).astype(bf16)
            flux_cot[i, 0:SUBLANES, :] = pulled
            g_bias[...] = g_bias[...] + pulled.astype(f32)

        return (
            spread(*KEYS["take"], take, BLOCK_ROWS)
            + spread(*KEYS["first"], first, chunks)
            + spread(*KEYS["second"], second, chunks)
            + spread(*KEYS["third"], third, chunks)
            + spread(*KEYS["fields"], fields, BLOCK_ROWS)
        )

    def backward(block, feat, hid_first, hid_second, slope_first, slope_second, flux_cot):
        start = block * BLOCK_ROWS

        def pull(net, slope_ref, cot_ref, j):
            for i in range(lanes):
                cols = slice(i * width, (i + 1) * width)
                cot_ref[j * lanes + i] = (net[:, cols] * slope_ref[j * lanes + i]).astype(bf16)

        def second(j):
            net = dot(w_third_back[...], side_by_side(flux_cot, j * lanes, lanes, 0, 16))
            pull(net, slope_second, cot_second, j)

        def first(j):
            net = dot(w_second_back[...], side_by_side(cot_second, j * lanes, lanes, 0, hidden))
            pull(net, slope_first, cot_first, j)

        def inputs(j):
            at = pl.ds(j * CHUNK, CHUNK)
            cot = side_by_side(cot_first, j * lanes, lanes, 0, hidden)
            feat_cot[:, at] = dot(w_first_back[...], cot)

        def whole(ref):
            return side_by_side(ref, 0, BLOCK_ROWS, 0, ref.shape[1])

        def leave(i):
            at = pl.ds(i * width, width)
            r = start + i
            base_out[r] = misfits[r] + feat_cot[0:SUBLANES, at]
            other[r] = feat_cot[SUBLANES : 2 * SUBLANES, at]

        def grad_second():
            g_second[...] += dot_nt(whole(hid_first), whole(cot_second))

        def grad_third():
            g_third[...] += dot_nt(whole(flux_cot), whole(hid_second))

        def grad_first():
            g_first[...] += dot_nt(whole(feat), whole(cot_first))

        return (
            spread(*KEYS["cot_second"], second, chunks)
            + spread(*KEYS["cot_first"], first, chunks)
            + spread(*KEYS["cot_inputs"], inputs, chunks)
            + spread(*KEYS["leave"], leave, BLOCK_ROWS)
            + [
                (KEYS["grad_second"], grad_second),
                (KEYS["grad_third"], grad_third),
                (KEYS["grad_first"], grad_first),
            ]
        )

    sets = list(
        zip(feats, hid_firsts, hid_seconds, slope_firsts, slope_seconds, flux_cots, strict=True)
    )
    blocks = rows // BLOCK_ROWS

    def beside(block, this, that):
        weave(backward(block, *this), forward(block + 1, *that))

    def pair_step(pair, unused):
        beside(2 * pair, *sets)
        beside(2 * pair + 1, *sets[::-1])
        return unused

    weave(forward(0, *sets[0]))
    lax.fori_loop(0, blocks // 2 - 1, pair_step, 0)
    beside(blocks - 2, *sets)
    ready = rows - BLOCK_ROWS
    stores = fetch_all(
        [
            (new_out, new_hbm),
            (diffuse_out, diffuse_hbm),
            (base_out.at[pl.ds(0, ready)], base_hbm.at[pl.ds(0, ready)]),
        ],
        store_sems,
    )
    weave(backward(blocks - 1, *sets[1]))
    rest = pltpu.make_async_copy(
        base_out.at[pl.ds(ready, BLOCK_ROWS)],
        base_hbm.at[pl.ds(ready, BLOCK_ROWS)],
        store_sems.at[3],
    )
    rest.start()
    stage[pl.ds(meta[OWN], peers), 0:slot_rows, :] = jnp.zeros((peers, slot_rows, width), f32)

    def leave(p, unused):
        for s in range(slots):
            row = landing[s, p]
            stage[meta[OTHER] + p, s * SUBLANES : (s + 1) * SUBLANES, :] = other[row]
        return unused

    lax.fori_loop(0, peers, leave, 0, unroll=8)
    put_edges(meta, edges[0], edges[1], diffuse_out[0], diffuse_out[rows - 1], stage)
    devices = stage.shape[0]
    halves = hidden // width
    inputs = 2 * SUBLANES
    small[...] = jnp.zeros(small.shape, f32)
    low, high = g_first[0:SUBLANES, :], g_first[SUBLANES:inputs, :]
    low, high = jnp.where(comp == 1, high, low), jnp.where(comp == 1, low, high)
    bias_sum = jnp.sum(g_bias[...], axis=1, keepdims=True)
    bias_row = jnp.sum(jnp.where(sub == lane, jnp.broadcast_to(bias_sum, shape), 0.0), axis=0,
                       keepdims=True)
    for h in range(halves):
        cols = slice(h * width, (h + 1) * width)
        top = h * 24
        small[top : top + 8, :] = low[:, cols]
        small[top + 8 : top + 16, :] = high[:, cols]
        small[top + 16 : top + 17, :] = g_first[inputs : inputs + 1, cols]
        small[top + 17 : top + 18, :] = g_second[hidden : hidden + 1, cols]
        if h == 0:
            small[top + 18 : top + 19, :] = bias_row
        small[top + 19 : top + 19 + fluxes, :] = g_third[0:fluxes, cols]
    for d in range(devices):
        done = 0
        while done < share:
            at = d * share + done
            h, row = divmod(at, hidden)
            step = min(share - done, hidden - row)
            if h < halves:
                stage[d, slot_rows + done : slot_rows + done + step, :] = g_second[
                    row : row + step, h * width : (h + 1) * width
                ]
            done += step
    top = SMALL_PLANE * SUBLANES
    for p in range(peers):
        piece = small[p * small_share : (p + 1) * small_share, :]
        head = piece.astype(bf16).astype(f32)
        stage[meta[OWN] + p, top : top + small_share, :] = head
        stage[meta[OWN] + p, top + small_share : top + 2 * small_share, :] = piece - head
    send_out[...] = stage[...].astype(bf16)
    for copy in (*stores, rest):
        copy.wait()


def sum_kernel(scale, peers, share, small_share, recv, out, stage):
    devices = recv.shape[0]
    own = lax.axis_index("comp") * peers
    slot_rows = 4 * SUBLANES
    planes = slice(SMALL_PLANE * SUBLANES, (SMALL_PLANE + 1) * SUBLANES)
    at = slice(slot_rows, slot_rows + -(-share // SUBLANES) * SUBLANES)
    total = recv[0, at, :].astype(f32)
    for d in range(1, devices):
        total = total + recv[d, at, :].astype(f32)
    part = recv[own, planes, :].astype(f32)
    for p in range(1, peers):
        part = part + recv[own + p, planes, :].astype(f32)
    part = part * scale
    piece = part[0:small_share] + part[small_share : 2 * small_share]
    head = piece.astype(bf16).astype(f32)
    stage[0:share, :] = total[0:share] * scale
    stage[share : share + small_share, :] = head
    stage[share + small_share : share + 2 * small_share, :] = piece - head
    total = stage[...].astype(bf16)
    for d in range(devices):
        out[d] = total


def back_kernel(
    rows, peers, slots, recv, kernels, source_in, count_in, rate_in, base_in, diffuse_in, out,
    source, count, rate_ref, base, diffuse, total, blocks, sems, block_sems,
):
    meta = place()
    copies = fetch_all(
        [
            (diffuse_in, diffuse),
            (base_in, base),
            (source_in, source),
            (count_in, count),
            (rate_in, rate_ref),
        ],
        sems,
    )
    parts = block_sems.shape[0]
    part = peers // parts
    steps = [pl.ds(i * part * slots, part * slots) for i in range(parts)]
    block_copies = fetch_all([(kernels.at[at], blocks.at[at]) for at in steps], block_sems)
    for copy in copies:
        copy.wait()
    width = diffuse.shape[2]
    shape = (SUBLANES, width)
    lane = lax.broadcasted_iota(jnp.int32, shape, 1)
    west, east, south, north = get_edges(meta, recv)
    comp = meta[COMP]
    rate = jnp.broadcast_to(column_of(rate_ref, comp), shape)

    def lap_step(r, unused):
        here = diffuse[r]
        below = jnp.where(r > 0, diffuse[jnp.maximum(r - 1, 0)], south)
        above = jnp.where(r < rows - 1, diffuse[jnp.minimum(r + 1, rows - 1)], north)
        total[r] = base[r] + rate * laplace_row(here, below, above, west, east, r, lane)
        return unused

    lax.fori_loop(0, rows, lap_step, 0, unroll=32)

    def peer_step(q, unused):
        block = recv[meta[OTHER] + q, 0 : slots * SUBLANES, :].astype(f32)
        for s in range(slots):
            k = q * slots + s
            sent = block[s * SUBLANES : (s + 1) * SUBLANES].astype(bf16)
            live = (s < count[q]).astype(f32)
            row = source[s, q]
            total[row] = total[row] + dot_nt(sent, blocks[k]) * live
        return unused

    for i in range(parts):
        block_copies[i].wait()
        lax.fori_loop(i * part, (i + 1) * part, peer_step, 0, unroll=math.gcd(part, 4))

    def out_step(r, unused):
        out[pl.ds(r, SUBLANES, stride=rows), :] = total[r]
        return unused

    lax.fori_loop(0, rows, out_step, 0, unroll=32)


def unpack_kernel(share, small_share, fluxes, recv, first, bias_one, second, bias_two, third,
                  bias_three, small):
    devices = recv.shape[0]
    peers = devices // 2
    width = recv.shape[2]
    hidden = second.shape[0]
    halves = hidden // width
    for d in range(devices):
        block = recv[d].astype(f32)
        done = 0
        while done < share:
            at = d * share + done
            h, row = divmod(at, hidden)
            step = min(share - done, hidden - row)
            if h < halves:
                second[row : row + step, h * width : (h + 1) * width] = block[done : done + step]
            done += step
        piece = (
            block[share : share + small_share]
            + block[share + small_share : share + 2 * small_share]
        )
        at = d % peers * small_share
        if d >= peers:
            piece = piece + small[at : at + small_share, :]
        small[at : at + small_share, :] = piece
    for h in range(halves):
        cols = slice(h * width, (h + 1) * width)
        top = h * 24
        first[:, cols] = small[top : top + 16, :]
        bias_one[:, cols] = small[top + 16 : top + 17, :]
        bias_two[:, cols] = small[top + 17 : top + 18, :]
        third[:, cols] = small[top + 19 : top + 19 + fluxes, :]
    bias_three[...] = small[18:19, 0:fluxes]


def shards(
    state,
    target,
    land_mask,
    diffusivity,
    coupling,
    w_in,
    b_in,
    w_mid,
    b_mid,
    w_out,
    b_out,
    remap_weight,
    remap_source,
    remap_target,
    remap_count,
):
    n_gy, n_gx = lax.axis_size("gy"), lax.axis_size("gx")
    tiles = n_gy * n_gx
    devices = 2 * tiles
    comp = lax.axis_index("comp")
    channels, rows, width = state.shape[1:]
    hidden = w_mid.shape[0]
    inputs = w_in.shape[0]
    fluxes = w_out.shape[1]
    peers, slots = remap_source.shape[3:]
    surface = state.reshape(channels * rows, width)
    goal = target.reshape(channels * rows, width)
    mask = land_mask[0]
    source = remap_source.reshape(peers, slots).T
    landing = remap_target.reshape(peers, slots).T
    count = remap_count.reshape(peers)
    kernels = remap_weight.reshape(peers * slots, width, width)
    slot_rows = slots * channels

    vmem = pl.BlockSpec(memory_space=pltpu.VMEM)

    far = pl.BlockSpec(memory_space=pltpu.HBM)
    parts = math.gcd(peers, 4)
    outgoing, by_row = pl.pallas_call(
        functools.partial(send_kernel, rows, peers, slots),
        name="send",
        out_shape=(
            jax.ShapeDtypeStruct((devices, slot_rows, width), bf16),
            jax.ShapeDtypeStruct((rows, channels, width), f32),
        ),
        in_specs=[far] * 4,
        out_specs=(vmem, vmem),
        scratch_shapes=[
            pltpu.VMEM((devices, slot_rows, width), f32),
            pltpu.VMEM(kernels.shape, bf16),
            pltpu.SemaphoreType.DMA((parts,)),
            pltpu.SMEM(source.shape, jnp.int32),
            pltpu.SMEM(count.shape, jnp.int32),
            pltpu.VMEM(surface.shape, f32),
            pltpu.SemaphoreType.DMA((3,)),
        ],
    )(source, count, surface, kernels)
    arrived = lax.all_to_all(outgoing, EVERYWHERE, 0, 0, tiled=True)

    def pieces(bias):
        high = bias.astype(bf16)
        rest = bias - high.astype(f32)
        middle = rest.astype(bf16)
        low = (rest - middle.astype(f32)).astype(bf16)
        return jnp.stack([high, middle, low], axis=0)

    local_in = jnp.where(comp == 1, jnp.roll(w_in, channels, axis=0), w_in)
    half = jnp.asarray(0.5, bf16)
    w_first = jnp.concatenate(
        [local_in, pieces(b_in), jnp.zeros((13, hidden), bf16)], axis=0
    ).T * half
    w_second = w_mid.T * half
    b_second = (b_mid * 0.5)[:, None]
    w_third = jnp.pad(w_out.T, ((0, 16 - fluxes), (0, 0)))
    w_third_back = jnp.pad(w_out * half, ((0, 0), (0, 16 - fluxes)))
    w_second_back = w_mid * half
    w_first_back = local_in

    share = -(-hidden * hidden // (width * devices))
    small_share = -(-24 * hidden // (width * tiles))
    sent = -(-share // 8) * 8
    packed = -(-(share + 2 * small_share) // 8) * 8
    cells = BLOCK_ROWS * width

    def twice(*args):
        return (pltpu.VMEM(*args), pltpu.VMEM(*args))

    tall = (rows, channels, width)
    tables = (
        mask,
        diffusivity,
        coupling,
        w_first,
        w_second,
        b_second,
        w_third,
        w_third_back,
        w_second_back,
        w_first_back,
    )
    new_state, base, diffuse, leaving = pl.pallas_call(
        functools.partial(main_kernel, rows, peers, slots, share, small_share),
        name="main",
        out_shape=(
            jax.ShapeDtypeStruct((channels * rows, width), f32),
            jax.ShapeDtypeStruct(tall, f32),
            jax.ShapeDtypeStruct((rows, channels, width), f32),
            jax.ShapeDtypeStruct((devices, slot_rows + sent, width), bf16),
        ),
        in_specs=[vmem] * 3 + [far] * FETCHED,
        out_specs=(far,) * 3 + (vmem,),
        scratch_shapes=[
            pltpu.SMEM(landing.shape, jnp.int32),
            pltpu.SMEM(b_out.shape, f32),
            *(pltpu.VMEM(array.shape, array.dtype) for array in tables),
            pltpu.SemaphoreType.DMA((FETCHED,)),
            pltpu.SemaphoreType.DMA((4,)),
            pltpu.VMEM((channels * rows, width), f32),
            pltpu.VMEM(tall, f32),
            pltpu.VMEM((rows, channels, width), f32),
            pltpu.VMEM((devices, slot_rows + sent, width), f32),
            pltpu.VMEM(tall, f32),
            pltpu.VMEM(tall, f32),
            twice((BLOCK_ROWS, 32, width), bf16),
            twice((BLOCK_ROWS, hidden + 16, width), bf16),
            twice((BLOCK_ROWS, hidden, width), bf16),
            twice((BLOCK_ROWS, hidden, width), f32),
            twice((BLOCK_ROWS, hidden, width), f32),
            twice((BLOCK_ROWS, 16, width), bf16),
            pltpu.VMEM((BLOCK_ROWS, hidden, width), bf16),
            pltpu.VMEM((BLOCK_ROWS, hidden, width), bf16),
            pltpu.VMEM((8, cells), f32),
            pltpu.VMEM((16, cells), f32),
            pltpu.VMEM((32, hidden), f32),
            pltpu.VMEM((hidden + 16, hidden), f32),
            pltpu.VMEM((16, hidden), f32),
            pltpu.VMEM((8, width), f32),
            pltpu.VMEM((2, 8, width), f32),
            pltpu.VMEM((max(48, small_share * tiles), width), f32),
        ],
    )(
        near(by_row),
        near(goal),
        near(arrived),
        landing,
        b_out,
        *tables,
    )
    returned = lax.all_to_all(leaving, EVERYWHERE, 0, 0, tiled=True)
    scale = 1.0 / (rows * width * tiles)
    summed = pl.pallas_call(
        functools.partial(sum_kernel, scale, peers, share, small_share),
        name="sum",
        out_shape=jax.ShapeDtypeStruct((devices, packed, width), bf16),
        in_specs=[vmem],
        out_specs=vmem,
        scratch_shapes=[pltpu.VMEM((packed, width), f32)],
    )(near(returned))
    gathered = lax.all_to_all(summed, EVERYWHERE, 0, 0, tiled=True)
    adjoint = pl.pallas_call(
        functools.partial(back_kernel, rows, peers, slots),
        name="back",
        out_shape=jax.ShapeDtypeStruct((channels * rows, width), f32),
        in_specs=[vmem] + [far] * 6,
        out_specs=vmem,
        scratch_shapes=[
            pltpu.SMEM(source.shape, jnp.int32),
            pltpu.SMEM(count.shape, jnp.int32),
            pltpu.VMEM(diffusivity.shape, f32),
            pltpu.VMEM(tall, f32),
            pltpu.VMEM(tall, f32),
            pltpu.VMEM(tall, f32),
            pltpu.VMEM(kernels.shape, bf16),
            pltpu.SemaphoreType.DMA((5,)),
            pltpu.SemaphoreType.DMA((parts,)),
        ],
    )(near(returned), kernels, source, count, diffusivity, base, diffuse)
    first, bias_one, second, bias_two, third, bias_three = pl.pallas_call(
        functools.partial(unpack_kernel, share, small_share, fluxes),
        name="unpack",
        out_shape=(
            jax.ShapeDtypeStruct((inputs, hidden), f32),
            jax.ShapeDtypeStruct((1, hidden), f32),
            jax.ShapeDtypeStruct((hidden, hidden), f32),
            jax.ShapeDtypeStruct((1, hidden), f32),
            jax.ShapeDtypeStruct((fluxes, hidden), f32),
            jax.ShapeDtypeStruct((1, fluxes), f32),
        ),
        in_specs=[vmem],
        out_specs=(vmem,) * 6,
        scratch_shapes=[pltpu.VMEM((max(48, small_share * tiles), width), f32)],
    )(near(gathered))
    return (
        new_state.reshape(state.shape),
        adjoint.reshape(state.shape),
        first,
        bias_one[0],
        second,
        bias_two[0],
        third.T,
        bias_three[0],
    )


def near(array):
    return pltpu.with_memory_space_constraint(array, pltpu.VMEM)


def solution(mesh):
    tiles = P("comp", None, "gy", "gx")
    placed = (
        tiles,
        tiles,
        P("comp", "gy", "gx"),
        *(P() for _ in range(8)),
        P("comp", "gy", "gx", None, None, None, None),
        P("comp", "gy", "gx", None, None),
        P("comp", "gy", "gx", None, None),
        P("comp", "gy", "gx", None),
    )
    return jax.shard_map(
        shards,
        mesh=mesh,
        in_specs=placed,
        out_specs=(tiles, tiles, *(P() for _ in range(6))),
        check_vma=False,
    )
```
